32 devices in a mesh: row: 4 (over y, x), col: 8 (over z, core).
Axes of the slice: x: 2, y: 2, z: 4, core: 2. Of those that a mesh axis runs over, the one named last changes fastest.
Arguments:
- homolog_stack: bfloat16 [128, 128, 256], P(('row', 'col')), may hold values from -6 to 6
- per_amino_features: bfloat16 [128, 256], P(('row', 'col')), may hold values from -6 to 6
- asking_matrix: bfloat16 [256, 256], replicated, may hold values from -24 to 24
- lookup_matrix: bfloat16 [256, 256], replicated, may hold values from -0.375 to 0.375
- content_matrix: bfloat16 [256, 256], replicated, may hold values from -0.375 to 0.375
- sigmoid_scaling_matrix: bfloat16 [256, 256], replicated, may hold values from -0.375 to 0.375
- attention_result_matrix: bfloat16 [256, 256], replicated, may hold values from -0.375 to 0.375
- stack_transition_expand_matrix: bfloat16 [256, 1024], replicated, may hold values from -0.375 to 0.375
- stack_transition_shrink_matrix: bfloat16 [1024, 256], replicated, may hold values from -0.1875 to 0.1875
- former_factor_matrix: bfloat16 [256, 32], replicated, may hold values from -0.375 to 0.375
- latter_factor_matrix: bfloat16 [256, 32], replicated, may hold values from -0.375 to 0.375
- factor_mean_projection: bfloat16 [1024, 128], replicated, may hold values from -1.1953125 to 1.1953125
- row_amino_embedding: bfloat16 [256, 128], replicated, may hold values from -0.375 to 0.375
- column_amino_embedding: bfloat16 [256, 128], replicated, may hold values from -0.375 to 0.375
- offset_embedding_matrix: bfloat16 [65, 128], replicated, may hold values from -3 to 3
- grid_transition_expand: bfloat16 [128, 512], replicated, may hold values from -0.5 to 0.5
- grid_transition_shrink: bfloat16 [512, 128], replicated, may hold values from -0.25 to 0.25
- distance_bins_matrix: bfloat16 [128, 64], replicated, may hold values from -0.5 to 0.5
Outputs:
- alignment_output: bfloat16 [128, 128, 256], P(None, ('row', 'col'))
- pair_output: bfloat16 [128, 128, 128], P('row', 'col')
- distogram: bfloat16 [128, 128, 64], P('row', 'col')
The draws below stay inside these ranges and needn't reach their ends.
All inputs are finite; a program needn't handle non-finite values.
Results may differ from the reference program's by a relative error of at most 0.011.
The reference program's roundings to bfloat16 on the way count: a program that leaves them out, or rounds other values in their place, can miss the bound.
Values may be sent and summed in bfloat16 or wider, within the bound.
No kernel may reach another device: no remote copies, remote signals or barrier semaphores. Data moves between devices by JAX's collectives and lax.ppermute only.
A program may use at most 256 MiB of HBM per device.

```python
import math
import jax
import jax.numpy as jnp
from jax import lax

STACK_FEATURES = 256
HEADS = 8
HEAD = 32
STACK_INNER = 1024
FACTOR_WIDTH = 32
GRID_FEATURES = 128
PAIR_HIDDEN = 512
BINS = 64
CLIP = 32
HOMOLOG_TOTAL = 128
AMINO_TOTAL = 128


def draw_asking_matrix(key, part):
    starting_tensor = jnp.clip(jax.random.normal(key, (STACK_FEATURES, STACK_FEATURES), jnp.float32), -4.0, 4.0)
    result = starting_tensor * 0.0625
    return result.astype(jnp.bfloat16)


def steps_of(rng, shape, cuts, least, high):
    def one(position, parts):
        steps = jax.random.uniform(jax.random.fold_in(jax.random.fold_in(rng, 6), position), (parts,), jnp.float32, least / len(cuts), high / len(cuts))
        return jnp.repeat(jnp.exp(steps), shape[position] // parts).reshape((-1,) + (1,) * (len(shape) - position - 1))

    loudness = one(*cuts[0])
    for cut in cuts[1:]:
        loudness = loudness * one(*cut)
    return loudness


def gaussian(stream_key, shape, scale, reach, shards=(), held_as=jnp.bfloat16):
    array = jax.random.normal(stream_key, shape, jnp.float32) * scale
    if len(shards) > 0:
        array = steps_of(stream_key, shape, shards, -0.22, 0.18) * array
    return jnp.clip(array, min=-reach, max=reach).astype(held_as)


def setup_inputs(seed: int = 0) -> dict:
    streams_of = jax.random.split(jax.random.key(seed), 19)
    homolog_stack = gaussian(streams_of[0], (HOMOLOG_TOTAL, AMINO_TOTAL, STACK_FEATURES), 1.0, 6.0, ((0, 32),))
    per_amino_features = gaussian(streams_of[1], (AMINO_TOTAL, STACK_FEATURES), 1.0, 6.0, ((0, 32),))
    asking_matrix = draw_asking_matrix(jax.random.fold_in(streams_of[18], 71), 0)
    lookup_matrix = gaussian(streams_of[3], (STACK_FEATURES, STACK_FEATURES), STACK_FEATURES ** -0.5, 0.375)
    content_matrix = gaussian(streams_of[4], (STACK_FEATURES, STACK_FEATURES), STACK_FEATURES ** -0.5, 0.375)
    sigmoid_scaling_matrix = gaussian(streams_of[5], (STACK_FEATURES, STACK_FEATURES), STACK_FEATURES ** -0.5, 0.375)
    attention_result_matrix = gaussian(streams_of[6], (STACK_FEATURES, STACK_FEATURES), STACK_FEATURES ** -0.5, 0.375)
    stack_transition_expand_matrix = gaussian(streams_of[7], (STACK_FEATURES, STACK_INNER), STACK_FEATURES ** -0.5, 0.375)
    stack_transition_shrink_matrix = gaussian(streams_of[8], (STACK_INNER, STACK_FEATURES), STACK_INNER ** -0.5, 0.1875)
    former_factor_matrix = gaussian(streams_of[9], (STACK_FEATURES, FACTOR_WIDTH), STACK_FEATURES ** -0.5, 0.375)
    latter_factor_matrix = gaussian(streams_of[10], (STACK_FEATURES, FACTOR_WIDTH), STACK_FEATURES ** -0.5, 0.375)
    factor_mean_projection = gaussian(streams_of[11], (FACTOR_WIDTH * FACTOR_WIDTH, GRID_FEATURES), 0.2, 1.1953125)
    row_amino_embedding = gaussian(streams_of[12], (STACK_FEATURES, GRID_FEATURES), STACK_FEATURES ** -0.5, 0.375)
    column_amino_embedding = gaussian(streams_of[13], (STACK_FEATURES, GRID_FEATURES), STACK_FEATURES ** -0.5, 0.375)
    offset_embedding_matrix = gaussian(streams_of[14], (2 * CLIP + 1, GRID_FEATURES), 0.5, 3.0)
    grid_transition_expand = gaussian(streams_of[15], (GRID_FEATURES, PAIR_HIDDEN), GRID_FEATURES ** -0.5, 0.5)
    grid_transition_shrink = gaussian(streams_of[16], (PAIR_HIDDEN, GRID_FEATURES), PAIR_HIDDEN ** -0.5, 0.25)
    distance_bins_matrix = gaussian(streams_of[17], (GRID_FEATURES, BINS), GRID_FEATURES ** -0.5, 0.5)
    return {"homolog_stack": homolog_stack, "per_amino_features": per_amino_features, "asking_matrix": asking_matrix, "lookup_matrix": lookup_matrix, "content_matrix": content_matrix, "sigmoid_scaling_matrix": sigmoid_scaling_matrix, "attention_result_matrix": attention_result_matrix, "stack_transition_expand_matrix": stack_transition_expand_matrix, "stack_transition_shrink_matrix": stack_transition_shrink_matrix, "former_factor_matrix": former_factor_matrix, "latter_factor_matrix": latter_factor_matrix, "factor_mean_projection": factor_mean_projection, "row_amino_embedding": row_amino_embedding, "column_amino_embedding": column_amino_embedding, "offset_embedding_matrix": offset_embedding_matrix, "grid_transition_expand": grid_transition_expand, "grid_transition_shrink": grid_transition_shrink, "distance_bins_matrix": distance_bins_matrix}


def standardize_features(values):
    middle = lax.optimization_barrier(jnp.mean(values, -1, keepdims=True))
    centred = values - middle
    spread = lax.optimization_barrier(jnp.mean(centred * centred, -1, keepdims=True))
    return centred * lax.rsqrt(spread + 1e-05)

def alignment_layer(block_piece, asking_matrix, lookup_matrix, content_matrix, sigmoid_scaling_matrix, attention_result_matrix, stack_transition_expand_matrix, stack_transition_shrink_matrix):
    count_seq, count_res, feature_width = block_piece.shape
    start = block_piece.astype(jnp.float32).reshape(-1, feature_width)
    standardized = standardize_features(start).astype(jnp.bfloat16)
    query = jnp.dot(standardized, asking_matrix, preferred_element_type=jnp.float32).astype(jnp.bfloat16)
    key_rows = jnp.dot(standardized, lookup_matrix, preferred_element_type=jnp.float32).astype(jnp.bfloat16)
    value_rows = jnp.dot(standardized, content_matrix, preferred_element_type=jnp.float32).astype(jnp.bfloat16)
    gate = jax.nn.sigmoid(jnp.dot(standardized, sigmoid_scaling_matrix, preferred_element_type=jnp.float32))
    query = query.reshape(count_seq, count_res, HEADS, HEAD).astype(jnp.float32)
    key_rows = key_rows.reshape(count_seq, count_res, HEADS, HEAD).astype(jnp.float32)
    value_rows = value_rows.reshape(count_seq, count_res, HEADS, HEAD).astype(jnp.float32)
    scores = jnp.einsum('sihd,tihd->ihst', query, key_rows) / math.sqrt(HEAD)
    weights = jax.nn.softmax(scores, -1).astype(jnp.bfloat16).astype(jnp.float32)
    attended = jnp.einsum('ihst,tihd->sihd', weights, value_rows).reshape(-1, feature_width)
    mixed = (attended * gate).astype(jnp.bfloat16)
    first_part = start + jnp.dot(mixed, attention_result_matrix, preferred_element_type=jnp.float32)
    hidden_units = jax.nn.relu(jnp.dot(standardize_features(first_part).astype(jnp.bfloat16), stack_transition_expand_matrix, preferred_element_type=jnp.float32)).astype(jnp.bfloat16)
    second_part = first_part + jnp.dot(hidden_units, stack_transition_shrink_matrix, preferred_element_type=jnp.float32)
    return second_part.reshape(count_seq, count_res, feature_width)

def pair_block(a_u, b_v, left_u, right_v, start_u, start_v, offset_embedding_matrix, factor_mean_projection, grid_transition_expand, grid_transition_shrink, distance_bins_matrix):
    count_seq, count_u, factor = a_u.shape
    count_v = b_v.shape[1]
    feature_width = left_u.shape[1]
    step_rows = max(1, min(count_u, 1024 // count_v))
    tile_collection = count_u // step_rows
    a_blocks = a_u.reshape(count_seq, tile_collection, step_rows, factor).transpose(1, 0, 2, 3)
    left_blocks = left_u.reshape(tile_collection, step_rows, feature_width)
    flat_v = b_v.reshape(count_seq, count_v * factor)
    columns = start_v + jnp.arange(count_v, dtype=jnp.int32)
    bins = jnp.arange(2 * CLIP + 1, dtype=jnp.int32)

    def one_block(inputs):
        a_blk, left_blk, index = inputs
        outer = lax.dot_general(a_blk.reshape(count_seq, step_rows * factor), flat_v, (((0,), (0,)), ((), ())), preferred_element_type=jnp.float32)
        outer = outer.reshape(step_rows, factor, count_v, factor).transpose(0, 2, 1, 3).reshape(step_rows * count_v, factor * factor)
        outer = (outer / count_seq).astype(jnp.bfloat16)
        projected = jnp.dot(outer, factor_mean_projection, preferred_element_type=jnp.float32)
        rows_here = start_u + index * step_rows + jnp.arange(step_rows, dtype=jnp.int32)
        offset = jnp.clip(columns[None, :] - rows_here[:, None], -CLIP, CLIP) + CLIP
        onehot = (offset[:, :, None] == bins).astype(jnp.bfloat16).reshape(-1, 2 * CLIP + 1)
        relative = jnp.dot(onehot, offset_embedding_matrix, preferred_element_type=jnp.float32)
        embedded = (left_blk.astype(jnp.float32)[:, None, :] + right_v.astype(jnp.float32)[None, :, :]).reshape(-1, feature_width)
        start_pair = embedded + relative + projected
        hidden_units = jax.nn.relu(jnp.dot(standardize_features(start_pair).astype(jnp.bfloat16), grid_transition_expand, preferred_element_type=jnp.float32)).astype(jnp.bfloat16)
        final = start_pair + jnp.dot(hidden_units, grid_transition_shrink, preferred_element_type=jnp.float32)
        rounded = final.astype(jnp.bfloat16)
        logits = jnp.dot(rounded, distance_bins_matrix, preferred_element_type=jnp.float32)
        return (rounded.reshape(step_rows, count_v, feature_width), logits.reshape(step_rows, count_v, -1))
    pairs, logits = lax.map(one_block, (a_blocks, left_blocks, jnp.arange(tile_collection, dtype=jnp.int32)))
    return (pairs.reshape(count_u, count_v, feature_width), logits.reshape(count_u, count_v, -1))

def reference(homolog_stack, per_amino_features, asking_matrix, lookup_matrix, content_matrix, sigmoid_scaling_matrix, attention_result_matrix, stack_transition_expand_matrix, stack_transition_shrink_matrix, former_factor_matrix, latter_factor_matrix, factor_mean_projection, row_amino_embedding, column_amino_embedding, offset_embedding_matrix, grid_transition_expand, grid_transition_shrink, distance_bins_matrix):
    tile_collection = 16
    divide_into_fragments = homolog_stack.reshape(HOMOLOG_TOTAL, tile_collection, AMINO_TOTAL // tile_collection, STACK_FEATURES).transpose(1, 0, 2, 3)
    refreshed_stack = lax.map(lambda partial_block: alignment_layer(partial_block, asking_matrix, lookup_matrix, content_matrix, sigmoid_scaling_matrix, attention_result_matrix, stack_transition_expand_matrix, stack_transition_shrink_matrix), divide_into_fragments)
    refreshed_stack = refreshed_stack.transpose(1, 0, 2, 3).reshape(HOMOLOG_TOTAL, AMINO_TOTAL, STACK_FEATURES)
    alignment_output = refreshed_stack.astype(jnp.bfloat16)
    standardized = standardize_features(refreshed_stack).astype(jnp.bfloat16).reshape(-1, STACK_FEATURES)
    left_opm = jnp.dot(standardized, former_factor_matrix, preferred_element_type=jnp.float32).astype(jnp.bfloat16).reshape(HOMOLOG_TOTAL, AMINO_TOTAL, FACTOR_WIDTH)
    right_opm = jnp.dot(standardized, latter_factor_matrix, preferred_element_type=jnp.float32).astype(jnp.bfloat16).reshape(HOMOLOG_TOTAL, AMINO_TOTAL, FACTOR_WIDTH)
    left_pair = jnp.dot(per_amino_features, row_amino_embedding, preferred_element_type=jnp.float32).astype(jnp.bfloat16)
    right_pair = jnp.dot(per_amino_features, column_amino_embedding, preferred_element_type=jnp.float32).astype(jnp.bfloat16)
    pair_output, logits = pair_block(left_opm, right_opm, left_pair, right_pair, 0, 0, offset_embedding_matrix, factor_mean_projection, grid_transition_expand, grid_transition_shrink, distance_bins_matrix)
    distogram = (logits + logits.transpose(1, 0, 2)).astype(jnp.bfloat16)
    return (alignment_output, pair_output, distogram)
```

```python
import functools
import math

import jax
import jax.numpy as jnp
import numpy as np
from jax import lax
from jax.experimental import pallas as pl
from jax.experimental.pallas import tpu as pltpu
from jax.sharding import PartitionSpec as P

HEADS = 8
HEAD = 32
CLIP = 32
LANES = 128
F32 = jnp.float32
BF16 = jnp.bfloat16


VMEM = pl.BlockSpec(memory_space=pltpu.VMEM)
SMEM = pl.BlockSpec(memory_space=pltpu.SMEM)


def dot(a, b):
    return jnp.dot(a, b, preferred_element_type=F32)


def standardize(values):
    middle = jnp.mean(values, -1, keepdims=True)
    centred = values - middle
    spread = jnp.mean(centred * centred, -1, keepdims=True)
    return centred * lax.rsqrt(spread + 1e-05)


def for_chunks(count, body):
    if count == 1:
        body(0)
    else:
        lax.fori_loop(0, count, lambda i, carry: (body(i), carry)[1], 0)


def rows_at(start, size):
    if not isinstance(start, int):
        start = pl.multiple_of(start, math.gcd(size, 128))
    return pl.ds(start, size)


def chunk_kernel(n_res, x_ref, o_ref, x_scr, o_scr):
    n_seq, amino, feature = x_ref.shape
    devices = amino // n_res
    for t in range(feature // LANES):
        lanes = slice(t * LANES, (t + 1) * LANES)
        x_scr[t] = x_ref[:, :, lanes].reshape(n_seq * amino, LANES).astype(F32)
        for seq in range(n_seq):
            for res in range(n_res):
                o_scr[t, pl.ds(seq * n_res + res, devices, stride=n_seq * n_res), :] = x_scr[
                    t, pl.ds(seq * amino + res, devices, stride=n_res), :
                ]
        o_ref[:, lanes] = o_scr[t].astype(BF16)


def chunks(x, n_res):
    n_seq, amino, feature = x.shape
    return pl.pallas_call(
        functools.partial(chunk_kernel, n_res),
        out_shape=jax.ShapeDtypeStruct((n_seq * amino, feature), BF16),
        in_specs=[VMEM],
        out_specs=VMEM,
        scratch_shapes=[
            pltpu.VMEM((feature // LANES, n_seq * amino, LANES), F32),
            pltpu.VMEM((feature // LANES, n_seq * amino, LANES), F32),
        ],
        name="chunks",
    )(x)


def spread_kernel(group, w_ref, o_ref, w_scr):
    factor = math.isqrt(w_ref.shape[0])
    w_scr[...] = w_ref[...].astype(F32)
    o_ref[...] = jnp.zeros_like(o_ref)
    for e in range(factor):
        block = w_scr[pl.ds(e, factor, stride=factor), :].astype(BF16)
        for i in range(group):
            row = (e * group + i) * factor
            o_ref[row : row + factor, i * LANES : (i + 1) * LANES] = block


def spread_projection(w, group):
    return pl.pallas_call(
        functools.partial(spread_kernel, group),
        out_shape=jax.ShapeDtypeStruct((w.shape[0] * group, w.shape[1] * group), BF16),
        in_specs=[VMEM],
        out_specs=VMEM,
        scratch_shapes=[pltpu.VMEM(w.shape, F32)],
        name="spread",
    )(w)


def attention_kernel(
    n_res,
    x_ref,
    amino_ref,
    wq_ref,
    wk_ref,
    wv_ref,
    wg_ref,
    wo_ref,
    w1_ref,
    w2_ref,
    fg_ref,
    re_ref,
    ce_ref,
    align_ref,
    send_ref,
    nat_scr,
    res_scr,
    q_scr,
    k_scr,
    v_scr,
    g_scr,
    mix_scr,
    ln_scr,
):
    rows, feature = x_ref.shape
    seqs = rows // n_res
    chunk = min(rows, 512)
    tiles = feature // LANES
    tile_lanes = [slice(t * LANES, (t + 1) * LANES) for t in range(tiles)]
    for t, lanes in enumerate(tile_lanes):
        nat_scr[t] = x_ref[:, lanes].astype(F32)
        for i in range(n_res):
            res_scr[i * seqs : (i + 1) * seqs, lanes] = nat_scr[t, pl.ds(i, seqs, stride=n_res), :]

    def project(step):
        at = rows_at(step * chunk, chunk)
        normed = standardize(res_scr[at, :]).astype(BF16)
        q_scr[at, :] = dot(normed, wq_ref[...]).astype(BF16)
        k_scr[at, :] = dot(normed, wk_ref[...]).astype(BF16)
        v_scr[at, :] = dot(normed, wv_ref[...]).astype(BF16)
        g_scr[at, :] = jax.nn.sigmoid(dot(normed, wg_ref[...]))

    for_chunks(rows // chunk, project)

    group = LANES // HEAD
    head_of_row = lax.broadcasted_iota(jnp.int32, (LANES, seqs), 0) // HEAD
    scale = 1.0 / math.sqrt(HEAD)

    def attend(index, tile):
        at = rows_at(index * seqs, seqs)
        lanes = tile_lanes[tile]
        q_t = q_scr[at, lanes].astype(F32).T
        stacked = jnp.concatenate(
            [jnp.where(head_of_row == h, q_t, 0.0).astype(BF16) for h in range(group)], axis=1
        )
        scores = dot(k_scr[at, lanes], stacked)
        top = jnp.max(scores, axis=0, keepdims=True)
        powers = jnp.exp((scores - top) * scale)
        total = jnp.sum(powers, axis=0, keepdims=True)
        weights = (powers * (1.0 / total)).astype(BF16)
        v_t = v_scr[at, lanes].astype(F32).T.astype(BF16)
        summed = dot(v_t, weights)
        picked = jnp.concatenate(
            [
                summed[h * HEAD : (h + 1) * HEAD, h * seqs : (h + 1) * seqs]
                for h in range(group)
            ],
            axis=0,
        )
        mix_scr[at, lanes] = (picked.T * g_scr[at, lanes]).astype(BF16)

    if seqs <= LANES:
        for i in range(n_res):
            for tile in range(tiles):
                attend(i, tile)
    else:

        def attend_all(i):
            for tile in range(tiles):
                attend(i, tile)

        for_chunks(n_res, attend_all)

    def transition(step):
        at = rows_at(step * chunk, chunk)
        first = res_scr[at, :] + dot(mix_scr[at, :], wo_ref[...])
        hidden = jnp.maximum(dot(standardize(first).astype(BF16), w1_ref[...]), 0.0).astype(BF16)
        second = first + dot(hidden, w2_ref[...])
        res_scr[at, :] = second
        ln_scr[at, :] = standardize(second).astype(BF16)

    for_chunks(rows // chunk, transition)

    for t, lanes in enumerate(tile_lanes):
        for i in range(n_res):
            nat_scr[t, pl.ds(i, seqs, stride=n_res), :] = res_scr[i * seqs : (i + 1) * seqs, lanes]
        align_ref[:, lanes] = nat_scr[t].astype(BF16)
    side = jnp.concatenate([ln_scr[i * seqs : (i + 1) * seqs, :] for i in range(n_res)], axis=1)
    factors = dot(side, fg_ref[...])
    send_ref[0:seqs, :] = factors[:, :LANES].astype(BF16)
    for t in range(seqs // LANES):
        turned = factors[t * LANES : (t + 1) * LANES, LANES:].T
        send_ref[seqs + t * LANES : seqs + (t + 1) * LANES, :] = turned.astype(BF16)
    by_row = lax.broadcasted_iota(jnp.int32, (16, LANES), 0)
    pairs = jnp.where(
        by_row < n_res, dot(amino_ref[...], re_ref[...]), dot(amino_ref[...], ce_ref[...])
    )
    send_ref[2 * seqs :, :] = pairs.astype(BF16)


def attention(x, amino, weights, n_res):
    rows, feature = x.shape
    seqs = rows // n_res
    return pl.pallas_call(
        functools.partial(attention_kernel, n_res),
        out_shape=(
            jax.ShapeDtypeStruct((rows, feature), BF16),
            jax.ShapeDtypeStruct((2 * seqs + 16, LANES), BF16),
        ),
        in_specs=[VMEM] * (2 + len(weights)),
        out_specs=(VMEM, VMEM),
        scratch_shapes=[
            pltpu.VMEM((feature // LANES, rows, LANES), F32),
            pltpu.VMEM((rows, feature), F32),
            pltpu.VMEM((rows, feature), BF16),
            pltpu.VMEM((rows, feature), BF16),
            pltpu.VMEM((rows, feature), BF16),
            pltpu.VMEM((rows, feature), F32),
            pltpu.VMEM((rows, feature), BF16),
            pltpu.VMEM((rows, feature), BF16),
        ],
        name="attention",
    )(x, amino, *weights)


def pair_kernel(n_row, n_col, n_res, seqs, *refs):
    place_ref = refs[0]
    row_refs = refs[1 : 1 + n_row]
    col_refs = refs[1 + n_row : 1 + n_row + n_col]
    (bd_ref, off_ref, w1_ref, w2_ref, bins_ref) = refs[1 + n_row + n_col : 6 + n_row + n_col]
    pair_ref, dist_ref = refs[6 + n_row + n_col : 8 + n_row + n_col]
    (turn_r, turn_c, a_r, a_c, lhs, grid, logit_scr) = refs[8 + n_row + n_col :]
    factor = LANES // n_res
    count_i = n_row * n_res
    count_j = n_col * n_res
    my_row = place_ref[0]
    my_col = place_ref[1]
    half = n_row // 2

    row_place = []
    for slot in range(n_row):
        m, q = slot % half, slot // half
        row_place.append(my_col ^ (2 * m + q))
    source_row = my_col // (n_row // n_col)
    col_place = []
    for slot in range(n_col):
        col_place.append(place_ref[2 + my_col * n_col + (my_row ^ slot ^ source_row)])

    for slot in range(n_row):
        for t in range(seqs // LANES):
            turn_r[t, slot * LANES : (slot + 1) * LANES, :] = row_refs[slot][
                seqs + t * LANES : seqs + (t + 1) * LANES, :
            ].astype(F32)
    for slot in range(n_col):
        at = rows_at(col_place[slot] * LANES, LANES)
        for t in range(seqs // LANES):
            turn_c[t, at, :] = col_refs[slot][
                seqs + t * LANES : seqs + (t + 1) * LANES, :
            ].astype(F32)
    for e in range(factor):
        for t in range(seqs // LANES):
            lanes = slice(t * LANES, (t + 1) * LANES)
            a_r[e * count_i : (e + 1) * count_i, lanes] = turn_r[
                t, pl.ds(e, count_i, stride=factor), :
            ].astype(BF16)
            a_c[e * count_j : (e + 1) * count_j, lanes] = turn_c[
                t, pl.ds(e, count_j, stride=factor), :
            ].astype(BF16)

    inverse = 1.0 / seqs

    def outer(a_ref, count, pieces, base):
        rows = factor * count
        chunk = min(rows, 1024)
        per = chunk // count
        step_pieces = 2
        for s in range(0, len(pieces), step_pieces):
            left = jnp.concatenate([p[0:seqs, :] for p in pieces[s : s + step_pieces]], axis=1)

            def one(step):
                made = dot(a_ref[rows_at(step * chunk, chunk), :], left) * inverse
                made = made.astype(BF16)
                for k in range(step_pieces):
                    for e in range(per):
                        lane = (step * per + e) * LANES
                        if not isinstance(lane, int):
                            lane = pl.multiple_of(lane, LANES)
                        lhs[
                            base + (s + k) * count : base + (s + k + 1) * count, pl.ds(lane, LANES)
                        ] = made[e * count : (e + 1) * count, k * LANES : (k + 1) * LANES]

            for_chunks(rows // chunk, one)

    direct = n_row * count_j
    mirrored = n_col * count_i
    outer(a_c, count_j, row_refs, 0)
    outer(a_r, count_i, col_refs, direct)

    row_side = jnp.concatenate([r[2 * seqs : 2 * seqs + 16, :] for r in row_refs], axis=0)
    col_side = jnp.concatenate([r[2 * seqs : 2 * seqs + 16, :] for r in col_refs], axis=0)

    def pick(side, places, count):
        width = side.shape[0]
        line = lax.broadcasted_iota(jnp.int32, (count, width), 0)
        column = lax.broadcasted_iota(jnp.int32, (count, width), 1)
        goal = column % 16 - n_res
        place = jnp.zeros_like(column)
        for slot, where in enumerate(places):
            place = jnp.where(column // 16 == slot, where, place)
        hit = (goal >= 0) & (goal < n_res) & (line == place * n_res + goal)
        return dot(jnp.where(hit, 1.0, 0.0).astype(BF16), side)

    right_r = pick(row_side, list(range(n_row)), count_i)
    right_c = pick(col_side, col_place, count_j)
    row_start = my_row * count_i
    col_start = my_col * count_j
    bins = lax.broadcasted_iota(jnp.int32, (count_j, LANES), 1)
    j_here = col_start + lax.broadcasted_iota(jnp.int32, (count_j, LANES), 0)
    bins_m = lax.broadcasted_iota(jnp.int32, (count_i, LANES), 1)
    i_slot = lax.broadcasted_iota(jnp.int32, (count_i, LANES), 0)
    i_here = i_slot % n_res + row_start
    for slot in range(n_row):
        i_here = jnp.where(i_slot // n_res == slot, i_here + row_place[slot] * n_res, i_here)

    def relative(offset, lanes):
        index = jnp.clip(offset, -CLIP, CLIP) + CLIP
        return jnp.where(index == lanes, 1.0, 0.0).astype(BF16)

    marks = []
    for slot in range(n_row):
        for r in range(n_res):
            i = row_start + row_place[slot] * n_res + r
            marks.append(relative(j_here - i, bins))
    for slot in range(n_col):
        for r in range(n_res):
            j = col_start + col_place[slot] * n_res + r
            marks.append(relative(i_here - j, bins_m))
    embedded = dot(jnp.concatenate(marks, axis=0), off_ref[...])

    total = direct + mirrored
    chunk = min(total, 256)

    def project(step):
        at = rows_at(step * chunk, chunk)
        made = dot(lhs[at, :], bd_ref[...])
        lhs_out[at, :] = made

    lhs_out = grid[1]
    start = grid[0]
    for_chunks(total // chunk, project)
    side_r = row_side.astype(F32)
    side_c = col_side.astype(F32)
    place = 0
    for slot in range(n_row):
        for r in range(n_res):
            made = lhs_out[slot * count_j : (slot + 1) * count_j, r * LANES : (r + 1) * LANES]
            left = side_r[slot * 16 + r : slot * 16 + r + 1, :]
            start[place : place + count_j, :] = (
                (left + right_c) + embedded[place : place + count_j, :] + made
            )
            place += count_j
    for slot in range(n_col):
        for r in range(n_res):
            made = lhs_out[
                direct + slot * count_i : direct + (slot + 1) * count_i,
                r * LANES : (r + 1) * LANES,
            ]
            left = side_c[slot * 16 + r : slot * 16 + r + 1, :]
            start[place : place + count_i, :] = (
                (left + right_r) + embedded[place : place + count_i, :] + made
            )
            place += count_i

    cells = count_i * count_j
    chunk2 = min(2 * cells, 1024)
    rounded_scr, all_logits = grid[2], grid[3]

    def transition(step):
        at = rows_at(step * chunk2, chunk2)
        begin = start[at, :]
        hidden = jnp.maximum(dot(standardize(begin).astype(BF16), w1_ref[...]), 0.0).astype(BF16)
        final = (begin + dot(hidden, w2_ref[...])).astype(BF16)
        rounded_scr[at, :] = final
        all_logits[at, :] = dot(final, bins_ref[...])

    for_chunks(2 * cells // chunk2, transition)
    for slot in range(n_col):
        for r in range(n_res):
            source = cells + (slot * n_res + r) * count_i
            goal = (col_place[slot] * n_res + r) * count_i
            logit_scr[rows_at(goal, count_i), :] = all_logits[source : source + count_i, :]
    for slot in range(n_row):
        for r in range(n_res):
            at = (slot * n_res + r) * count_j
            goal = row_place[slot] * n_res + r
            pair_ref[goal] = rounded_scr[at : at + count_j, :]
            mirror = logit_scr[pl.ds(slot * n_res + r, count_j, stride=count_i), :]
            summed = all_logits[at : at + count_j, :] + mirror
            dist_ref[goal] = summed[:, : dist_ref.shape[2]].astype(BF16)


def pair_grid(place, row_pieces, col_pieces, weights, n_res, seqs, n_bins):
    n_row, n_col = len(row_pieces), len(col_pieces)
    count_i, count_j = n_row * n_res, n_col * n_res
    factor = LANES // n_res
    total = n_row * count_j + n_col * count_i
    cells = count_i * count_j
    return pl.pallas_call(
        functools.partial(pair_kernel, n_row, n_col, n_res, seqs),
        out_shape=(
            jax.ShapeDtypeStruct((count_i, count_j, LANES), BF16),
            jax.ShapeDtypeStruct((count_i, count_j, n_bins), BF16),
        ),
        in_specs=[SMEM] + [VMEM] * (n_row + n_col + len(weights)),
        out_specs=(VMEM, VMEM),
        scratch_shapes=[
            pltpu.VMEM((seqs // LANES, n_row * LANES, LANES), F32),
            pltpu.VMEM((seqs // LANES, n_col * LANES, LANES), F32),
            pltpu.VMEM((factor * count_i, seqs), BF16),
            pltpu.VMEM((factor * count_j, seqs), BF16),
            pltpu.VMEM((total, factor * LANES), BF16),
            (
                pltpu.VMEM((2 * cells, LANES), F32),
                pltpu.VMEM((total, n_res * LANES), F32),
                pltpu.VMEM((2 * cells, LANES), BF16),
                pltpu.VMEM((2 * cells, LANES), F32),
            ),
            pltpu.VMEM((cells, LANES), F32),
        ],
        name="pairs",
    )(place, *row_pieces, *col_pieces, *weights)


def plane_offsets(n_row, n_col):
    offsets = []
    by_hops = sorted(range(n_row), key=lambda v: (bin(v).count("1"), v))
    for column in range(n_col):
        home = column // 2
        far = sorted(
            range(n_row),
            key=lambda m: (-abs((column * n_row + m) % n_col // 2 - home), m),
        )
        line = [0] * n_row
        for position, m in enumerate(far):
            line[m] = by_hops[position]
        offsets.append(line)
    return offsets


def shards(
    n_rows,
    n_cols,
    homolog_stack,
    per_amino_features,
    asking_matrix,
    lookup_matrix,
    content_matrix,
    sigmoid_scaling_matrix,
    attention_result_matrix,
    stack_transition_expand_matrix,
    stack_transition_shrink_matrix,
    former_factor_matrix,
    latter_factor_matrix,
    factor_mean_projection,
    row_amino_embedding,
    column_amino_embedding,
    offset_embedding_matrix,
    grid_transition_expand,
    grid_transition_shrink,
    distance_bins_matrix,
):
    devices = n_rows * n_cols
    n_seq, amino, feature = homolog_stack.shape
    n_res = amino // devices
    seqs = n_seq * devices
    axes = ("row", "col")

    sent = chunks(homolog_stack, n_res).reshape(devices, n_seq * n_res, feature)
    moved = lax.all_to_all(sent, axes, split_axis=0, concat_axis=0, tiled=True)
    moved = moved.reshape(seqs * n_res, feature)

    unit = jnp.eye(n_res, dtype=BF16)
    factors = jnp.concatenate(
        [jnp.kron(unit, former_factor_matrix), jnp.kron(unit, latter_factor_matrix)], axis=1
    )
    amino_rows = jnp.concatenate(
        [per_amino_features, per_amino_features, jnp.zeros((16 - 2 * n_res, feature), BF16)], axis=0
    )
    spread = spread_projection(factor_mean_projection, n_res)
    offsets = jnp.pad(
        offset_embedding_matrix, ((0, LANES - offset_embedding_matrix.shape[0]), (0, 0))
    )
    bins = jnp.pad(distance_bins_matrix, ((0, 0), (0, LANES - distance_bins_matrix.shape[1])))

    aligned, piece = attention(
        moved,
        amino_rows,
        (
            asking_matrix,
            lookup_matrix,
            content_matrix,
            sigmoid_scaling_matrix,
            attention_result_matrix,
            stack_transition_expand_matrix,
            stack_transition_shrink_matrix,
            factors,
            row_amino_embedding,
            column_amino_embedding,
        ),
        n_res,
    )
    alignment_output = aligned.reshape(seqs, n_res, feature)

    table = plane_offsets(n_rows, n_cols)
    turn = []
    for p in range(devices):
        column, m = p // n_rows, p % n_rows
        turn.append((p, ((p // n_cols) ^ table[column][m]) * n_cols + column))
    turned = lax.ppermute(piece, axes, turn)

    def along_col(value, m):
        return lax.ppermute(value, "col", [(c, c ^ m) for c in range(n_cols)])

    def along_row(value, m):
        return lax.ppermute(value, "row", [(r, r ^ m) for r in range(n_rows)])

    own = [piece] + [along_col(piece, 2 * m) for m in range(1, n_cols // 2)]
    other = [along_col(value, 1) for value in own]
    col_pieces = [turned] + [along_row(turned, m) for m in range(1, n_rows)]

    inverse = []
    for line in table:
        back = [0] * n_rows
        for m, offset in enumerate(line):
            back[offset] = m
        inverse.extend(back)
    here = jnp.stack([lax.axis_index("row"), lax.axis_index("col")]).astype(jnp.int32)
    place = jnp.concatenate([here, jnp.asarray(np.array(inverse, np.int32))])
    pair_output, distogram = pair_grid(
        place,
        own + other,
        col_pieces,
        (spread, offsets, grid_transition_expand, grid_transition_shrink, bins),
        n_res,
        seqs,
        distance_bins_matrix.shape[1],
    )
    return (alignment_output, pair_output, distogram)


def solution(mesh):
    n_rows, n_cols = mesh.shape["row"], mesh.shape["col"]
    assert n_cols == 2 * n_rows and n_rows & (n_rows - 1) == 0
    placed = (P(("row", "col"), None, None), P(("row", "col"), None)) + (P(),) * 16
    return jax.shard_map(
        functools.partial(shards, n_rows, n_cols),
        mesh=mesh,
        in_specs=placed,
        out_specs=(P(None, ("row", "col"), None), P("row", "col", None), P("row", "col", None)),
        check_vma=False,
    )
```

```python
import functools
import math

import jax
import jax.numpy as jnp
from jax import lax
from jax.experimental import pallas as pl
from jax.experimental.pallas import tpu as pltpu
from jax.sharding import PartitionSpec as P

HEADS = 8
HEAD = 32
CLIP = 32
LANES = 128
F32 = jnp.float32
BF16 = jnp.bfloat16


VMEM = pl.BlockSpec(memory_space=pltpu.VMEM)
HBM = pl.BlockSpec(memory_space=pltpu.MemorySpace.HBM)


def near(value):
    return pltpu.with_memory_space_constraint(value, pltpu.MemorySpace.VMEM)


def far(value):
    return pltpu.with_memory_space_constraint(value, pltpu.MemorySpace.HBM)


def local_call(kernel, *, scratch_shapes, **options):
    held = 0
    for ref in jax.tree.leaves(scratch_shapes):
        if ref.memory_space != pltpu.MemorySpace.VMEM:
            continue
        held += math.prod(ref.shape) * jnp.dtype(ref.dtype).itemsize
    limit = min(2 * held + (8 << 20), 48 << 20)
    return pl.pallas_call(
        kernel,
        scratch_shapes=scratch_shapes,
        compiler_params=pltpu.CompilerParams(vmem_limit_bytes=limit),
        **options,
    )


def dot(a, b):
    return jnp.dot(a, b, preferred_element_type=F32)


def standardize(values):
    middle = jnp.mean(values, -1, keepdims=True)
    centred = values - middle
    spread = jnp.mean(centred * centred, -1, keepdims=True)
    return centred * lax.rsqrt(spread + 1e-05)


def for_chunks(count, body):
    if count == 1:
        body(0)
    else:
        lax.fori_loop(0, count, lambda i, carry: (body(i), carry)[1], 0)


def rows_at(start, size):
    if not isinstance(start, int):
        start = pl.multiple_of(start, math.gcd(size, 128))
    return pl.ds(start, size)


def chunk_kernel(n_res, x_ref, o_ref, x_scr, o_scr):
    n_seq, amino, feature = x_ref.shape
    devices = amino // n_res
    for t in range(feature // LANES):
        lanes = slice(t * LANES, (t + 1) * LANES)
        x_scr[t] = x_ref[:, :, lanes].reshape(n_seq * amino, LANES).astype(F32)
        for seq in range(n_seq):
            for res in range(n_res):
                o_scr[t, pl.ds(seq * n_res + res, devices, stride=n_seq * n_res), :] = x_scr[
                    t, pl.ds(seq * amino + res, devices, stride=n_res), :
                ]
        o_ref[:, lanes] = o_scr[t].astype(BF16)


def chunks(x, n_res):
    n_seq, amino, feature = x.shape
    return local_call(
        functools.partial(chunk_kernel, n_res),
        out_shape=jax.ShapeDtypeStruct((n_seq * amino, feature), BF16),
        in_specs=[VMEM],
        out_specs=VMEM,
        scratch_shapes=[
            pltpu.VMEM((feature // LANES, n_seq * amino, LANES), F32),
            pltpu.VMEM((feature // LANES, n_seq * amino, LANES), F32),
        ],
        name="chunks",
    )(x)


def spread_kernel(group, w_ref, o_ref, w_scr):
    factor = math.isqrt(w_ref.shape[0])
    w_scr[...] = w_ref[...].astype(F32)
    o_ref[...] = jnp.zeros_like(o_ref)
    for e in range(factor):
        block = w_scr[pl.ds(e, factor, stride=factor), :].astype(BF16)
        for i in range(group):
            row = (e * group + i) * factor
            o_ref[row : row + factor, i * LANES : (i + 1) * LANES] = block


def spread_projection(w, group):
    return local_call(
        functools.partial(spread_kernel, group),
        out_shape=pltpu.HBM((w.shape[0] * group, w.shape[1] * group), BF16),
        in_specs=[VMEM],
        out_specs=VMEM,
        scratch_shapes=[pltpu.VMEM(w.shape, F32)],
        name="spread",
    )(w)


def attention_kernel(
    n_res,
    x_ref,
    amino_ref,
    wq_ref,
    wk_ref,
    wv_ref,
    wg_ref,
    wo_ref,
    fg_ref,
    re_ref,
    ce_ref,
    w1_far,
    w2_far,
    _,
    align_ref,
    send_ref,
    nat_scr,
    res_scr,
    q_scr,
    k_scr,
    v_scr,
    g_scr,
    mix_scr,
    ln_scr,
    w1_ref,
    w2_ref,
    arrived,
):
    fetch_1 = pltpu.make_async_copy(w1_far, w1_ref, arrived.at[0])
    fetch_2 = pltpu.make_async_copy(w2_far, w2_ref, arrived.at[1])
    fetch_1.start()
    fetch_2.start()
    rows, feature = x_ref.shape
    seqs = rows // n_res
    chunk = min(rows, 512)
    tiles = feature // LANES
    tile_lanes = [slice(t * LANES, (t + 1) * LANES) for t in range(tiles)]
    for t, lanes in enumerate(tile_lanes):
        nat_scr[t] = x_ref[:, lanes].astype(F32)
        for i in range(n_res):
            res_scr[i * seqs : (i + 1) * seqs, lanes] = nat_scr[t, pl.ds(i, seqs, stride=n_res), :]

    def project(step):
        at = rows_at(step * chunk, chunk)
        normed = standardize(res_scr[at, :]).astype(BF16)
        q_scr[at, :] = dot(normed, wq_ref[...]).astype(BF16)
        k_scr[at, :] = dot(normed, wk_ref[...]).astype(BF16)
        v_scr[at, :] = dot(normed, wv_ref[...]).astype(BF16)
        g_scr[at, :] = jax.nn.sigmoid(dot(normed, wg_ref[...]))

    for_chunks(rows // chunk, project)

    group = LANES // HEAD
    head_of_row = lax.broadcasted_iota(jnp.int32, (LANES, seqs), 0) // HEAD
    scale = 1.0 / math.sqrt(HEAD)

    def attend(index, tile):
        at = rows_at(index * seqs, seqs)
        lanes = tile_lanes[tile]
        q_t = q_scr[at, lanes].astype(F32).T
        stacked = jnp.concatenate(
            [jnp.where(head_of_row == h, q_t, 0.0).astype(BF16) for h in range(group)], axis=1
        )
        scores = dot(k_scr[at, lanes], stacked)
        top = jnp.max(scores, axis=0, keepdims=True)
        powers = jnp.exp((scores - top) * scale)
        total = jnp.sum(powers, axis=0, keepdims=True)
        weights = (powers * (1.0 / total)).astype(BF16)
        v_t = v_scr[at, lanes].astype(F32).T.astype(BF16)
        summed = dot(v_t, weights)
        picked = jnp.concatenate(
            [
                summed[h * HEAD : (h + 1) * HEAD, h * seqs : (h + 1) * seqs]
                for h in range(group)
            ],
            axis=0,
        )
        mix_scr[at, lanes] = (picked.T * g_scr[at, lanes]).astype(BF16)

    if seqs <= LANES:
        for i in range(n_res):
            for tile in range(tiles):
                attend(i, tile)
    else:

        def attend_all(i):
            for tile in range(tiles):
                attend(i, tile)

        for_chunks(n_res, attend_all)

    fetch_1.wait()
    fetch_2.wait()

    def transition(step):
        at = rows_at(step * chunk, chunk)
        first = res_scr[at, :] + dot(mix_scr[at, :], wo_ref[...])
        hidden = jnp.maximum(dot(standardize(first).astype(BF16), w1_ref[...]), 0.0).astype(BF16)
        second = first + dot(hidden, w2_ref[...])
        res_scr[at, :] = second
        ln_scr[at, :] = standardize(second).astype(BF16)

    for_chunks(rows // chunk, transition)

    for t, lanes in enumerate(tile_lanes):
        for i in range(n_res):
            nat_scr[t, pl.ds(i, seqs, stride=n_res), :] = res_scr[i * seqs : (i + 1) * seqs, lanes]
        align_ref[:, lanes] = nat_scr[t].astype(BF16)
    side = jnp.concatenate([ln_scr[i * seqs : (i + 1) * seqs, :] for i in range(n_res)], axis=1)
    factors = dot(side, fg_ref[...])
    send_ref[0:seqs, :] = factors[:, :LANES].astype(BF16)
    for t in range(seqs // LANES):
        turned = factors[t * LANES : (t + 1) * LANES, LANES:].T
        send_ref[seqs + t * LANES : seqs + (t + 1) * LANES, :] = turned.astype(BF16)
    by_row = lax.broadcasted_iota(jnp.int32, (16, LANES), 0)
    pairs = jnp.where(
        by_row < n_res, dot(amino_ref[...], re_ref[...]), dot(amino_ref[...], ce_ref[...])
    )
    send_ref[2 * seqs :, :] = pairs.astype(BF16)


def attention(x, amino, weights, large, after, n_res):
    rows, feature = x.shape
    seqs = rows // n_res
    return local_call(
        functools.partial(attention_kernel, n_res),
        out_shape=(
            pltpu.VMEM((rows, feature), BF16),
            pltpu.VMEM((2 * seqs + 16, LANES), BF16),
        ),
        in_specs=[VMEM] * (2 + len(weights)) + [HBM] * (len(large) + 1),
        out_specs=(VMEM, VMEM),
        scratch_shapes=[
            pltpu.VMEM((feature // LANES, rows, LANES), F32),
            pltpu.VMEM((rows, feature), F32),
            pltpu.VMEM((rows, feature), BF16),
            pltpu.VMEM((rows, feature), BF16),
            pltpu.VMEM((rows, feature), BF16),
            pltpu.VMEM((rows, feature), F32),
            pltpu.VMEM((rows, feature), BF16),
            pltpu.VMEM((rows, feature), BF16),
            *[pltpu.VMEM(w.shape, BF16) for w in large],
            pltpu.SemaphoreType.DMA((len(large),)),
        ],
        name="attention",
    )(near(x), near(amino), *[near(w) for w in weights], *[far(w) for w in large], far(after))


def pair_kernel(n_row, n_col, n_res, seqs, places, *refs):
    row_refs = refs[0:n_row]
    col_refs = refs[n_row : n_row + n_col]
    refs = refs[n_row + n_col :]
    off_ref, bins_ref, bd_far, w1_far, w2_far, pair_ref, dist_ref = refs[:7]
    (turn_r, turn_c, a_r, a_c, lhs, grid, logit_scr, off_scr, bd_ref, w1_ref, w2_ref, arrived) = (
        refs[7:]
    )
    fetches = [
        pltpu.make_async_copy(far, local, arrived.at[k])
        for k, (far, local) in enumerate(((bd_far, bd_ref), (w1_far, w1_ref), (w2_far, w2_ref)))
    ]
    for fetch in fetches:
        fetch.start()
    factor = LANES // n_res
    count_i = n_row * n_res
    count_j = n_col * n_res
    my_row = lax.axis_index("row")
    my_col = lax.axis_index("col")
    half = n_row // 2

    row_place = []
    for slot in range(n_row):
        m, q = slot % half, slot // half
        row_place.append(my_col ^ (2 * m + q))
    source_row = my_col // (n_row // n_col)
    col_place = []
    for slot in range(n_col):
        key = my_col * n_col + (my_row ^ slot ^ source_row)
        where = jnp.int32(0)
        for entry, value in enumerate(places):
            where = jnp.where(key == entry, value, where)
        col_place.append(where)

    for slot in range(n_row):
        for t in range(seqs // LANES):
            turn_r[t, slot * LANES : (slot + 1) * LANES, :] = row_refs[slot][
                seqs + t * LANES : seqs + (t + 1) * LANES, :
            ].astype(F32)
    for slot in range(n_col):
        at = rows_at(col_place[slot] * LANES, LANES)
        for t in range(seqs // LANES):
            turn_c[t, at, :] = col_refs[slot][
                seqs + t * LANES : seqs + (t + 1) * LANES, :
            ].astype(F32)
    for e in range(factor):
        for t in range(seqs // LANES):
            lanes = slice(t * LANES, (t + 1) * LANES)
            a_r[e * count_i : (e + 1) * count_i, lanes] = turn_r[
                t, pl.ds(e, count_i, stride=factor), :
            ].astype(BF16)
            a_c[e * count_j : (e + 1) * count_j, lanes] = turn_c[
                t, pl.ds(e, count_j, stride=factor), :
            ].astype(BF16)

    inverse = 1.0 / seqs

    def outer(a_ref, count, pieces, base):
        rows = factor * count
        chunk = min(rows, 1024)
        per = chunk // count
        step_pieces = 2
        for s in range(0, len(pieces), step_pieces):
            left = jnp.concatenate([p[0:seqs, :] for p in pieces[s : s + step_pieces]], axis=1)

            def one(step):
                made = dot(a_ref[rows_at(step * chunk, chunk), :], left) * inverse
                made = made.astype(BF16)
                for k in range(step_pieces):
                    for e in range(per):
                        lane = (step * per + e) * LANES
                        if not isinstance(lane, int):
                            lane = pl.multiple_of(lane, LANES)
                        lhs[
                            base + (s + k) * count : base + (s + k + 1) * count, pl.ds(lane, LANES)
                        ] = made[e * count : (e + 1) * count, k * LANES : (k + 1) * LANES]

            for_chunks(rows // chunk, one)

    direct = n_row * count_j
    mirrored = n_col * count_i
    outer(a_c, count_j, row_refs, 0)
    outer(a_r, count_i, col_refs, direct)

    row_side = jnp.concatenate([r[2 * seqs : 2 * seqs + 16, :] for r in row_refs], axis=0)
    col_side = jnp.concatenate([r[2 * seqs : 2 * seqs + 16, :] for r in col_refs], axis=0)

    def pick(side, places, count):
        width = side.shape[0]
        line = lax.broadcasted_iota(jnp.int32, (count, width), 0)
        column = lax.broadcasted_iota(jnp.int32, (count, width), 1)
        goal = column % 16 - n_res
        place = jnp.zeros_like(column)
        for slot, where in enumerate(places):
            place = jnp.where(column // 16 == slot, where, place)
        hit = (goal >= 0) & (goal < n_res) & (line == place * n_res + goal)
        return dot(jnp.where(hit, 1.0, 0.0).astype(BF16), side)

    right_r = pick(row_side, list(range(n_row)), count_i)
    right_c = pick(col_side, col_place, count_j)
    row_start = my_row * count_i
    col_start = my_col * count_j
    bins = lax.broadcasted_iota(jnp.int32, (count_j, LANES), 1)
    j_here = col_start + lax.broadcasted_iota(jnp.int32, (count_j, LANES), 0)
    bins_m = lax.broadcasted_iota(jnp.int32, (count_i, LANES), 1)
    i_slot = lax.broadcasted_iota(jnp.int32, (count_i, LANES), 0)
    i_here = i_slot % n_res + row_start
    for slot in range(n_row):
        i_here = jnp.where(i_slot // n_res == slot, i_here + row_place[slot] * n_res, i_here)

    def relative(offset, lanes):
        index = jnp.clip(offset, -CLIP, CLIP) + CLIP
        return jnp.where(index == lanes, 1.0, 0.0).astype(BF16)

    marks = []
    for slot in range(n_row):
        for r in range(n_res):
            i = row_start + row_place[slot] * n_res + r
            marks.append(relative(j_here - i, bins))
    for slot in range(n_col):
        for r in range(n_res):
            j = col_start + col_place[slot] * n_res + r
            marks.append(relative(i_here - j, bins_m))
    off_scr[...] = jnp.zeros_like(off_scr)
    off_scr[0 : off_ref.shape[0], :] = off_ref[...].astype(F32)
    embedded = dot(jnp.concatenate(marks, axis=0), off_scr[...].astype(BF16))

    total = direct + mirrored
    chunk = min(total, 256)

    def project(step):
        at = rows_at(step * chunk, chunk)
        made = dot(lhs[at, :], bd_ref[...])
        lhs_out[at, :] = made

    lhs_out = grid[1]
    start = grid[0]
    for fetch in fetches:
        fetch.wait()
    for_chunks(total // chunk, project)
    side_r = row_side.astype(F32)
    side_c = col_side.astype(F32)
    place = 0
    for slot in range(n_row):
        for r in range(n_res):
            made = lhs_out[slot * count_j : (slot + 1) * count_j, r * LANES : (r + 1) * LANES]
            left = side_r[slot * 16 + r : slot * 16 + r + 1, :]
            start[place : place + count_j, :] = (
                (left + right_c) + embedded[place : place + count_j, :] + made
            )
            place += count_j
    for slot in range(n_col):
        for r in range(n_res):
            made = lhs_out[
                direct + slot * count_i : direct + (slot + 1) * count_i,
                r * LANES : (r + 1) * LANES,
            ]
            left = side_c[slot * 16 + r : slot * 16 + r + 1, :]
            start[place : place + count_i, :] = (
                (left + right_r) + embedded[place : place + count_i, :] + made
            )
            place += count_i

    cells = count_i * count_j
    n_bins = dist_ref.shape[2]
    chunk2 = min(2 * cells, 1024)
    rounded_scr, all_logits = grid[2], grid[3]

    def transition(step):
        at = rows_at(step * chunk2, chunk2)
        begin = start[at, :]
        hidden = jnp.maximum(dot(standardize(begin).astype(BF16), w1_ref[...]), 0.0).astype(BF16)
        final = (begin + dot(hidden, w2_ref[...])).astype(BF16)
        rounded_scr[at, :] = final
        all_logits[at, :] = lax.dot_general(
            final, bins_ref[...], (((1,), (1,)), ((), ())), preferred_element_type=F32
        )

    for_chunks(2 * cells // chunk2, transition)
    for slot in range(n_col):
        for r in range(n_res):
            source = cells + (slot * n_res + r) * count_i
            goal = (col_place[slot] * n_res + r) * count_i
            logit_scr[rows_at(goal, count_i), :n_bins] = all_logits[source : source + count_i, :]
    for slot in range(n_row):
        for r in range(n_res):
            at = (slot * n_res + r) * count_j
            goal = row_place[slot] * n_res + r
            pair_ref[goal] = rounded_scr[at : at + count_j, :]
            mirror = logit_scr[pl.ds(slot * n_res + r, count_j, stride=count_i), :]
            summed = all_logits[at : at + count_j, :] + mirror[:, :n_bins]
            dist_ref[goal] = summed.astype(BF16)


def pair_grid(places, row_pieces, col_pieces, weights, large, n_res, seqs):
    n_row, n_col = len(row_pieces), len(col_pieces)
    count_i, count_j = n_row * n_res, n_col * n_res
    factor = LANES // n_res
    total = n_row * count_j + n_col * count_i
    cells = count_i * count_j
    n_bins = weights[1].shape[0]
    return local_call(
        functools.partial(pair_kernel, n_row, n_col, n_res, seqs, places),
        out_shape=(
            jax.ShapeDtypeStruct((count_i, count_j, LANES), BF16),
            jax.ShapeDtypeStruct((count_i, count_j, n_bins), BF16),
        ),
        in_specs=[VMEM] * (n_row + n_col + len(weights)) + [HBM] * len(large),
        out_specs=(VMEM, VMEM),
        scratch_shapes=[
            pltpu.VMEM((seqs // LANES, n_row * LANES, LANES), F32),
            pltpu.VMEM((seqs // LANES, n_col * LANES, LANES), F32),
            pltpu.VMEM((factor * count_i, seqs), BF16),
            pltpu.VMEM((factor * count_j, seqs), BF16),
            pltpu.VMEM((total, factor * LANES), BF16),
            (
                pltpu.VMEM((2 * cells, LANES), F32),
                pltpu.VMEM((total, n_res * LANES), F32),
                pltpu.VMEM((2 * cells, LANES), BF16),
                pltpu.VMEM((2 * cells, n_bins), F32),
            ),
            pltpu.VMEM((cells, LANES), F32),
            pltpu.VMEM((LANES, LANES), F32),
            *[pltpu.VMEM(w.shape, BF16) for w in large],
            pltpu.SemaphoreType.DMA((len(large),)),
        ],
        name="pairs",
    )(*[near(v) for v in (*row_pieces, *col_pieces, *weights)], *[far(w) for w in large])


def plane_offsets(n_row, n_col):
    offsets = []
    by_hops = sorted(range(n_row), key=lambda v: (bin(v).count("1"), v))
    for column in range(n_col):
        home = column // 2
        far = sorted(
            range(n_row),
            key=lambda m: (-abs((column * n_row + m) % n_col // 2 - home), m),
        )
        line = [0] * n_row
        for position, m in enumerate(far):
            line[m] = by_hops[position]
        offsets.append(line)
    return offsets


def shards(
    n_rows,
    n_cols,
    homolog_stack,
    per_amino_features,
    asking_matrix,
    lookup_matrix,
    content_matrix,
    sigmoid_scaling_matrix,
    attention_result_matrix,
    stack_transition_expand_matrix,
    stack_transition_shrink_matrix,
    former_factor_matrix,
    latter_factor_matrix,
    factor_mean_projection,
    row_amino_embedding,
    column_amino_embedding,
    offset_embedding_matrix,
    grid_transition_expand,
    grid_transition_shrink,
    distance_bins_matrix,
):
    devices = n_rows * n_cols
    n_seq, amino, feature = homolog_stack.shape
    n_res = amino // devices
    seqs = n_seq * devices
    axes = ("row", "col")

    sent = chunks(homolog_stack, n_res).reshape(devices, n_seq * n_res, feature)
    moved = lax.all_to_all(sent, axes, split_axis=0, concat_axis=0, tiled=True)
    moved = moved.reshape(seqs * n_res, feature)

    unit = jnp.eye(n_res, dtype=BF16)
    factors = jnp.concatenate(
        [jnp.kron(unit, former_factor_matrix), jnp.kron(unit, latter_factor_matrix)], axis=1
    )
    amino_rows = jnp.concatenate(
        [per_amino_features, per_amino_features, jnp.zeros((16 - 2 * n_res, feature), BF16)], axis=0
    )
    spread = spread_projection(factor_mean_projection, n_res)
    aligned, piece = attention(
        moved,
        amino_rows,
        (
            asking_matrix,
            lookup_matrix,
            content_matrix,
            sigmoid_scaling_matrix,
            attention_result_matrix,
            factors,
            row_amino_embedding,
            column_amino_embedding,
        ),
        (stack_transition_expand_matrix, stack_transition_shrink_matrix),
        spread,
        n_res,
    )
    alignment_output = aligned.reshape(seqs, n_res, feature)

    table = plane_offsets(n_rows, n_cols)
    turn = []
    for p in range(devices):
        column, m = p // n_rows, p % n_rows
        turn.append((p, ((p // n_cols) ^ table[column][m]) * n_cols + column))
    turned = lax.ppermute(piece, axes, turn)

    def along_col(value, m):
        return lax.ppermute(value, "col", [(c, c ^ m) for c in range(n_cols)])

    def along_row(value, m):
        return lax.ppermute(value, "row", [(r, r ^ m) for r in range(n_rows)])

    own = [piece] + [along_col(piece, 2 * m) for m in range(1, n_cols // 2)]
    other = [along_col(value, 1) for value in own]
    col_pieces = [turned] + [along_row(turned, m) for m in range(1, n_rows)]

    inverse = []
    for line in table:
        back = [0] * n_rows
        for m, offset in enumerate(line):
            back[offset] = m
        inverse.extend(back)
    pair_output, distogram = pair_grid(
        inverse,
        own + other,
        col_pieces,
        (offset_embedding_matrix, distance_bins_matrix.T),
        (spread, grid_transition_expand, grid_transition_shrink),
        n_res,
        seqs,
    )
    return (alignment_output, pair_output, distogram)


def solution(mesh):
    n_rows, n_cols = mesh.shape["row"], mesh.shape["col"]
    assert n_cols == 2 * n_rows and n_rows & (n_rows - 1) == 0
    placed = (P(("row", "col"), None, None), P(("row", "col"), None)) + (P(),) * 16
    return jax.shard_map(
        functools.partial(shards, n_rows, n_cols),
        mesh=mesh,
        in_specs=placed,
        out_specs=(P(None, ("row", "col"), None), P("row", "col", None), P("row", "col", None)),
        check_vma=False,
    )
```

```python
import functools
import math

import jax
import jax.numpy as jnp
from jax import lax
from jax.experimental import pallas as pl
from jax.experimental.pallas import tpu as pltpu
from jax.sharding import PartitionSpec as P

HEADS = 8
HEAD = 32
CLIP = 32
LANES = 128
F32 = jnp.float32
BF16 = jnp.bfloat16


VMEM = pl.BlockSpec(memory_space=pltpu.VMEM)
HBM = pl.BlockSpec(memory_space=pltpu.MemorySpace.HBM)


def near(value):
    return pltpu.with_memory_space_constraint(value, pltpu.MemorySpace.VMEM)


def far(value):
    return pltpu.with_memory_space_constraint(value, pltpu.MemorySpace.HBM)


def local_call(kernel, *, scratch_shapes, **options):
    held = 0
    for ref in jax.tree.leaves(scratch_shapes):
        if ref.memory_space != pltpu.MemorySpace.VMEM:
            continue
        held += math.prod(ref.shape) * jnp.dtype(ref.dtype).itemsize
    limit = min(2 * held + (8 << 20), 48 << 20)
    return pl.pallas_call(
        kernel,
        scratch_shapes=scratch_shapes,
        compiler_params=pltpu.CompilerParams(vmem_limit_bytes=limit),
        **options,
    )


def dot(a, b):
    return jnp.dot(a, b, preferred_element_type=F32)


def standardize(values):
    middle = jnp.mean(values, -1, keepdims=True)
    centred = values - middle
    spread = jnp.mean(centred * centred, -1, keepdims=True)
    return centred * lax.rsqrt(spread + 1e-05)


def for_chunks(count, body):
    if count == 1:
        body(0)
    else:
        lax.fori_loop(0, count, lambda i, carry: (body(i), carry)[1], 0)


def rows_at(start, size):
    if not isinstance(start, int):
        start = pl.multiple_of(start, math.gcd(size, 128))
    return pl.ds(start, size)


def chunk_kernel(n_res, x_ref, o_ref, x_scr, o_scr):
    n_seq, amino, feature = x_ref.shape
    devices = amino // n_res
    for t in range(feature // LANES):
        lanes = slice(t * LANES, (t + 1) * LANES)
        x_scr[t] = x_ref[:, :, lanes].reshape(n_seq * amino, LANES).astype(F32)
        for seq in range(n_seq):
            for res in range(n_res):
                o_scr[t, pl.ds(seq * n_res + res, devices, stride=n_seq * n_res), :] = x_scr[
                    t, pl.ds(seq * amino + res, devices, stride=n_res), :
                ]
        o_ref[:, lanes] = o_scr[t].astype(BF16)


def chunks(x, n_res):
    n_seq, amino, feature = x.shape
    return local_call(
        functools.partial(chunk_kernel, n_res),
        out_shape=jax.ShapeDtypeStruct((n_seq * amino, feature), BF16),
        in_specs=[VMEM],
        out_specs=VMEM,
        scratch_shapes=[
            pltpu.VMEM((feature // LANES, n_seq * amino, LANES), F32),
            pltpu.VMEM((feature // LANES, n_seq * amino, LANES), F32),
        ],
        name="chunks",
    )(x)


def turn_kernel(w_ref, o_ref, w_scr):
    factor = math.isqrt(w_ref.shape[0])
    w_scr[...] = w_ref[...].astype(F32)
    for e in range(factor):
        o_ref[e * factor : (e + 1) * factor, :] = w_scr[pl.ds(e, factor, stride=factor), :].astype(
            BF16
        )


def turn_projection(w):
    return local_call(
        turn_kernel,
        out_shape=pltpu.HBM(w.shape, BF16),
        in_specs=[VMEM],
        out_specs=VMEM,
        scratch_shapes=[pltpu.VMEM(w.shape, F32)],
        name="turn",
    )(w)


def attention_kernel(
    n_res,
    x_ref,
    amino_ref,
    wq_ref,
    wk_ref,
    wv_ref,
    wg_ref,
    wo_ref,
    fg_ref,
    re_ref,
    ce_ref,
    w1_far,
    w2_far,
    _,
    align_ref,
    send_ref,
    nat_scr,
    res_scr,
    q_scr,
    k_scr,
    v_scr,
    g_scr,
    mix_scr,
    ln_scr,
    w1_ref,
    w2_ref,
    arrived,
):
    fetch_1 = pltpu.make_async_copy(w1_far, w1_ref, arrived.at[0])
    fetch_2 = pltpu.make_async_copy(w2_far, w2_ref, arrived.at[1])
    fetch_1.start()
    fetch_2.start()
    rows, feature = x_ref.shape
    seqs = rows // n_res
    chunk = min(rows, 512)
    tiles = feature // LANES
    tile_lanes = [slice(t * LANES, (t + 1) * LANES) for t in range(tiles)]
    for t, lanes in enumerate(tile_lanes):
        nat_scr[t] = x_ref[:, lanes].astype(F32)
        for i in range(n_res):
            res_scr[i * seqs : (i + 1) * seqs, lanes] = nat_scr[t, pl.ds(i, seqs, stride=n_res), :]

    def project(step):
        at = rows_at(step * chunk, chunk)
        normed = standardize(res_scr[at, :]).astype(BF16)
        q_scr[at, :] = dot(normed, wq_ref[...]).astype(BF16)
        k_scr[at, :] = dot(normed, wk_ref[...]).astype(BF16)
        v_scr[at, :] = dot(normed, wv_ref[...]).astype(BF16)
        g_scr[at, :] = jax.nn.sigmoid(dot(normed, wg_ref[...]))

    for_chunks(rows // chunk, project)

    group = LANES // HEAD
    head_of_row = lax.broadcasted_iota(jnp.int32, (LANES, seqs), 0) // HEAD
    head_of_lane = lax.broadcasted_iota(jnp.int32, (seqs, LANES), 1) // HEAD
    scale = math.log2(math.e) / math.sqrt(HEAD)

    def attend(index, tile):
        at = rows_at(index * seqs, seqs)
        lanes = tile_lanes[tile]
        q_t = q_scr[at, lanes].astype(F32).T.astype(BF16)
        v_t = v_scr[at, lanes].astype(F32).T
        keys = k_scr[at, lanes].astype(F32)
        stacked = jnp.concatenate(
            [jnp.where(head_of_lane == h, keys, 0.0).astype(BF16) for h in range(group)], axis=0
        )
        scores = dot(stacked, q_t)
        powers, inverse = [], []
        for h in range(group):
            mine = scores[h * seqs : (h + 1) * seqs, :]
            power = jnp.exp2((mine - jnp.max(mine, axis=0, keepdims=True)) * scale)
            total = 1.0 / jnp.sum(power, axis=0, keepdims=True)
            powers.append(power.astype(BF16))
            inverse.append(jnp.broadcast_to(total, (HEAD, seqs)))
        values = jnp.concatenate(
            [jnp.where(head_of_row == h, v_t, 0.0).astype(BF16) for h in range(group)], axis=1
        )
        summed = dot(values, jnp.concatenate(powers, axis=0)) * jnp.concatenate(inverse, axis=0)
        mix_scr[at, lanes] = (summed.T * g_scr[at, lanes]).astype(BF16)

    if seqs <= LANES:
        for i in range(n_res):
            for tile in range(tiles):
                attend(i, tile)
    else:

        def attend_all(i):
            for tile in range(tiles):
                attend(i, tile)

        for_chunks(n_res, attend_all)

    fetch_1.wait()
    fetch_2.wait()

    def transition(step):
        at = rows_at(step * chunk, chunk)
        first = res_scr[at, :] + dot(mix_scr[at, :], wo_ref[...])
        hidden = jnp.maximum(dot(standardize(first).astype(BF16), w1_ref[...]), 0.0).astype(BF16)
        second = first + dot(hidden, w2_ref[...])
        res_scr[at, :] = second
        ln_scr[at, :] = standardize(second).astype(BF16)

    for_chunks(rows // chunk, transition)

    for t, lanes in enumerate(tile_lanes):
        for i in range(n_res):
            nat_scr[t, pl.ds(i, seqs, stride=n_res), :] = res_scr[i * seqs : (i + 1) * seqs, lanes]
        align_ref[:, lanes] = nat_scr[t].astype(BF16)
    side = jnp.concatenate([ln_scr[i * seqs : (i + 1) * seqs, :] for i in range(n_res)], axis=1)
    factors = dot(side, fg_ref[...])
    send_ref[0:seqs, :] = factors[:, :LANES].astype(BF16)
    for t in range(seqs // LANES):
        turned = factors[t * LANES : (t + 1) * LANES, LANES:].T
        send_ref[seqs + t * LANES : seqs + (t + 1) * LANES, :] = turned.astype(BF16)
    by_row = lax.broadcasted_iota(jnp.int32, (16, LANES), 0)
    pairs = jnp.where(
        by_row < n_res, dot(amino_ref[...], re_ref[...]), dot(amino_ref[...], ce_ref[...])
    )
    send_ref[2 * seqs :, :] = pairs.astype(BF16)


def attention(x, amino, weights, large, after, n_res):
    rows, feature = x.shape
    seqs = rows // n_res
    return local_call(
        functools.partial(attention_kernel, n_res),
        out_shape=(
            pltpu.VMEM((rows, feature), BF16),
            pltpu.VMEM((2 * seqs + 16, LANES), BF16),
        ),
        in_specs=[VMEM] * (2 + len(weights)) + [HBM] * (len(large) + 1),
        out_specs=(VMEM, VMEM),
        scratch_shapes=[
            pltpu.VMEM((feature // LANES, rows, LANES), F32),
            pltpu.VMEM((rows, feature), F32),
            pltpu.VMEM((rows, feature), BF16),
            pltpu.VMEM((rows, feature), BF16),
            pltpu.VMEM((rows, feature), BF16),
            pltpu.VMEM((rows, feature), F32),
            pltpu.VMEM((rows, feature), BF16),
            pltpu.VMEM((rows, feature), BF16),
            *[pltpu.VMEM(w.shape, BF16) for w in large],
            pltpu.SemaphoreType.DMA((len(large),)),
        ],
        name="attention",
    )(near(x), near(amino), *[near(w) for w in weights], *[far(w) for w in large], far(after))


def placement(n_row, n_col, places):
    my_row = lax.axis_index("row")
    my_col = lax.axis_index("col")
    half = n_row // 2
    row_place = [my_col ^ (2 * (slot % half) + slot // half) for slot in range(n_row)]
    line = []
    for offset in range(n_col):
        entry = jnp.int32(places[offset])
        for column in range(1, n_row):
            entry = jnp.where(my_col == column, places[column * n_col + offset], entry)
        line.append(entry)
    source_row = my_col // (n_row // n_col)
    col_place = []
    for slot in range(n_col):
        key = my_row ^ slot ^ source_row
        where = line[0]
        for offset in range(1, n_col):
            where = jnp.where(key == offset, line[offset], where)
        col_place.append(where)
    return my_row, my_col, row_place, col_place


def relative_kernel(n_row, n_col, n_res, places, off_ref, o_ref, off_scr):
    my_row, my_col, row_place, col_place = placement(n_row, n_col, places)
    count_i, count_j = n_row * n_res, n_col * n_res
    row_start = my_row * count_i
    col_start = my_col * count_j
    bins = lax.broadcasted_iota(jnp.int32, (count_j, LANES), 1)
    j_here = col_start + lax.broadcasted_iota(jnp.int32, (count_j, LANES), 0)
    bins_m = lax.broadcasted_iota(jnp.int32, (count_i, LANES), 1)
    i_slot = lax.broadcasted_iota(jnp.int32, (count_i, LANES), 0)
    i_here = i_slot % n_res + row_start
    for slot in range(n_row):
        i_here = jnp.where(i_slot // n_res == slot, i_here + row_place[slot] * n_res, i_here)

    def relative(offset, lanes):
        index = jnp.clip(offset, -CLIP, CLIP) + CLIP
        return jnp.where(index == lanes, 1.0, 0.0).astype(BF16)

    marks = []
    for slot in range(n_row):
        for r in range(n_res):
            i = row_start + row_place[slot] * n_res + r
            marks.append(relative(j_here - i, bins))
    for slot in range(n_col):
        for r in range(n_res):
            j = col_start + col_place[slot] * n_res + r
            marks.append(relative(i_here - j, bins_m))
    off_scr[...] = jnp.zeros_like(off_scr)
    off_scr[0 : off_ref.shape[0], :] = off_ref[...].astype(F32)
    o_ref[...] = dot(jnp.concatenate(marks, axis=0), off_scr[...].astype(BF16)).astype(BF16)


def relative_rows(places, table, n_row, n_col, n_res):
    return local_call(
        functools.partial(relative_kernel, n_row, n_col, n_res, places),
        out_shape=pltpu.VMEM((2 * n_row * n_col * n_res * n_res, LANES), BF16),
        in_specs=[VMEM],
        out_specs=VMEM,
        scratch_shapes=[pltpu.VMEM((LANES, LANES), F32)],
        name="relative",
    )(near(table))


def pair_kernel(n_row, n_col, n_res, seqs, places, *refs):
    row_refs = refs[0:n_row]
    col_refs = refs[n_row : n_row + n_col]
    refs = refs[n_row + n_col :]
    rel_ref, bins_ref, wp_far, w1_far, w2_far, pair_far, dist_far = refs[:7]
    (turn_r, turn_c, a_r, a_c, lhs, grid, logit_scr) = refs[7:14]
    wp_ref, w1_ref, w2_ref, bd_ref, pair_ref, dist_ref, arrived, left_sem = refs[14:]
    fetches = [
        pltpu.make_async_copy(away, local, arrived.at[k])
        for k, (away, local) in enumerate(((wp_far, wp_ref), (w1_far, w1_ref), (w2_far, w2_ref)))
    ]
    for fetch in fetches:
        fetch.start()
    factor = LANES // n_res
    count_i = n_row * n_res
    count_j = n_col * n_res
    my_row, my_col, row_place, col_place = placement(n_row, n_col, places)

    for slot in range(n_row):
        for t in range(seqs // LANES):
            turn_r[t, slot * LANES : (slot + 1) * LANES, :] = row_refs[slot][
                seqs + t * LANES : seqs + (t + 1) * LANES, :
            ].astype(F32)
    for slot in range(n_col):
        at = rows_at(col_place[slot] * LANES, LANES)
        for t in range(seqs // LANES):
            turn_c[t, at, :] = col_refs[slot][
                seqs + t * LANES : seqs + (t + 1) * LANES, :
            ].astype(F32)
    for e in range(factor):
        for t in range(seqs // LANES):
            lanes = slice(t * LANES, (t + 1) * LANES)
            a_r[e * count_i : (e + 1) * count_i, lanes] = turn_r[
                t, pl.ds(e, count_i, stride=factor), :
            ].astype(BF16)
            a_c[e * count_j : (e + 1) * count_j, lanes] = turn_c[
                t, pl.ds(e, count_j, stride=factor), :
            ].astype(BF16)

    for fetch in fetches:
        fetch.wait()
    for e in range(factor):
        block = wp_ref[e * factor : (e + 1) * factor, :]
        for r in range(n_res):
            row = (e * n_res + r) * factor
            for other in range(n_res):
                bd_ref[row : row + factor, other * LANES : (other + 1) * LANES] = (
                    block if other == r else jnp.zeros_like(block)
                )
    inverse = 1.0 / seqs

    def outer(a_ref, count, pieces, base):
        rows = factor * count
        chunk = min(rows, 1024)
        per = chunk // count
        step_pieces = 2
        for s in range(0, len(pieces), step_pieces):
            left = jnp.concatenate([p[0:seqs, :] for p in pieces[s : s + step_pieces]], axis=1)

            def one(step):
                made = dot(a_ref[rows_at(step * chunk, chunk), :], left) * inverse
                made = made.astype(BF16)
                for k in range(step_pieces):
                    for e in range(per):
                        lane = (step * per + e) * LANES
                        if not isinstance(lane, int):
                            lane = pl.multiple_of(lane, LANES)
                        lhs[
                            base + (s + k) * count : base + (s + k + 1) * count, pl.ds(lane, LANES)
                        ] = made[e * count : (e + 1) * count, k * LANES : (k + 1) * LANES]

            for_chunks(rows // chunk, one)

    direct = n_row * count_j
    mirrored = n_col * count_i
    outer(a_c, count_j, row_refs, 0)
    outer(a_r, count_i, col_refs, direct)

    row_side = jnp.concatenate([r[2 * seqs : 2 * seqs + 16, :] for r in row_refs], axis=0)
    col_side = jnp.concatenate([r[2 * seqs : 2 * seqs + 16, :] for r in col_refs], axis=0)

    def pick(side, places, count):
        width = side.shape[0]
        line = lax.broadcasted_iota(jnp.int32, (count, width), 0)
        column = lax.broadcasted_iota(jnp.int32, (count, width), 1)
        goal = column % 16 - n_res
        place = jnp.zeros_like(column)
        for slot, where in enumerate(places):
            place = jnp.where(column // 16 == slot, where, place)
        hit = (goal >= 0) & (goal < n_res) & (line == place * n_res + goal)
        return dot(jnp.where(hit, 1.0, 0.0).astype(BF16), side)

    right_r = pick(row_side, list(range(n_row)), count_i)
    right_c = pick(col_side, col_place, count_j)
    total = direct + mirrored
    chunk = min(total, 256)

    def project(step):
        at = rows_at(step * chunk, chunk)
        made = dot(lhs[at, :], bd_ref[...])
        lhs_out[at, :] = made

    lhs_out = grid[1]
    start = grid[0]
    for_chunks(total // chunk, project)
    side_r = row_side.astype(F32)
    side_c = col_side.astype(F32)
    place = 0
    for slot in range(n_row):
        for r in range(n_res):
            made = lhs_out[slot * count_j : (slot + 1) * count_j, r * LANES : (r + 1) * LANES]
            left = side_r[slot * 16 + r : slot * 16 + r + 1, :]
            start[place : place + count_j, :] = (
                (left + right_c) + rel_ref[place : place + count_j, :] + made
            )
            place += count_j
    for slot in range(n_col):
        for r in range(n_res):
            made = lhs_out[
                direct + slot * count_i : direct + (slot + 1) * count_i,
                r * LANES : (r + 1) * LANES,
            ]
            left = side_c[slot * 16 + r : slot * 16 + r + 1, :]
            start[place : place + count_i, :] = (
                (left + right_r) + rel_ref[place : place + count_i, :] + made
            )
            place += count_i

    cells = count_i * count_j
    n_bins = dist_ref.shape[2]
    chunk2 = min(cells, 512)
    rounded_scr, all_logits = grid[2], grid[3]

    def transition(step):
        at = rows_at(step * chunk2, chunk2)
        begin = start[at, :]
        hidden = jnp.maximum(dot(standardize(begin).astype(BF16), w1_ref[...]), 0.0).astype(BF16)
        final = (begin + dot(hidden, w2_ref[...])).astype(BF16)
        rounded_scr[at, :] = final
        all_logits[at, :] = lax.dot_general(
            final, bins_ref[...], (((1,), (1,)), ((), ())), preferred_element_type=F32
        )

    steps = cells // chunk2
    for_chunks(steps, transition)
    for slot in range(n_row):
        for r in range(n_res):
            at = (slot * n_res + r) * count_j
            goal = row_place[slot] * n_res + r
            pair_ref[goal] = rounded_scr[at : at + count_j, :]
    leave_pair = pltpu.make_async_copy(pair_ref, pair_far, left_sem.at[0])
    leave_pair.start()
    if steps == 1:
        transition(1)
    else:
        for_chunks(steps, lambda step: transition(step + steps))
    for slot in range(n_col):
        for r in range(n_res):
            source = cells + (slot * n_res + r) * count_i
            goal = (col_place[slot] * n_res + r) * count_i
            logit_scr[rows_at(goal, count_i), :n_bins] = all_logits[source : source + count_i, :]
    leaves = [leave_pair]
    for slot in range(n_row):
        for r in range(n_res):
            at = (slot * n_res + r) * count_j
            goal = row_place[slot] * n_res + r
            mirror = logit_scr[pl.ds(slot * n_res + r, count_j, stride=count_i), :]
            summed = all_logits[at : at + count_j, :] + mirror[:, :n_bins]
            dist_ref[goal] = summed.astype(BF16)
        rows = pl.ds(row_place[slot] * n_res, n_res)
        leave = pltpu.make_async_copy(dist_ref.at[rows], dist_far.at[rows], left_sem.at[1 + slot])
        leave.start()
        leaves.append(leave)
    for leave in leaves:
        leave.wait()


def pair_grid(places, row_pieces, col_pieces, weights, large, n_res, seqs):
    n_row, n_col = len(row_pieces), len(col_pieces)
    count_i, count_j = n_row * n_res, n_col * n_res
    factor = LANES // n_res
    total = n_row * count_j + n_col * count_i
    cells = count_i * count_j
    n_bins = weights[1].shape[0]
    return local_call(
        functools.partial(pair_kernel, n_row, n_col, n_res, seqs, places),
        out_shape=(
            jax.ShapeDtypeStruct((count_i, count_j, LANES), BF16),
            jax.ShapeDtypeStruct((count_i, count_j, n_bins), BF16),
        ),
        in_specs=[VMEM] * (n_row + n_col + len(weights)) + [HBM] * len(large),
        out_specs=(HBM, HBM),
        scratch_shapes=[
            pltpu.VMEM((seqs // LANES, n_row * LANES, LANES), F32),
            pltpu.VMEM((seqs // LANES, n_col * LANES, LANES), F32),
            pltpu.VMEM((factor * count_i, seqs), BF16),
            pltpu.VMEM((factor * count_j, seqs), BF16),
            pltpu.VMEM((total, factor * LANES), BF16),
            (
                pltpu.VMEM((2 * cells, LANES), F32),
                pltpu.VMEM((total, n_res * LANES), F32),
                pltpu.VMEM((2 * cells, LANES), BF16),
                pltpu.VMEM((2 * cells, n_bins), F32),
            ),
            pltpu.VMEM((cells, LANES), F32),
            *[pltpu.VMEM(w.shape, BF16) for w in large],
            pltpu.VMEM((factor * LANES, n_res * LANES), BF16),
            pltpu.VMEM((count_i, count_j, LANES), BF16),
            pltpu.VMEM((count_i, count_j, n_bins), BF16),
            pltpu.SemaphoreType.DMA((len(large),)),
            pltpu.SemaphoreType.DMA((1 + n_row,)),
        ],
        name="pairs",
    )(*[near(v) for v in (*row_pieces, *col_pieces, *weights)], *[far(w) for w in large])


def plane_offsets(n_row, n_col):
    offsets = []
    by_hops = sorted(range(n_row), key=lambda v: (bin(v).count("1"), v))
    for column in range(n_col):
        home = column // 2
        far = sorted(
            range(n_row),
            key=lambda m: (-abs((column * n_row + m) % n_col // 2 - home), m),
        )
        line = [0] * n_row
        for position, m in enumerate(far):
            line[m] = by_hops[position]
        offsets.append(line)
    return offsets


def shards(
    n_rows,
    n_cols,
    homolog_stack,
    per_amino_features,
    asking_matrix,
    lookup_matrix,
    content_matrix,
    sigmoid_scaling_matrix,
    attention_result_matrix,
    stack_transition_expand_matrix,
    stack_transition_shrink_matrix,
    former_factor_matrix,
    latter_factor_matrix,
    factor_mean_projection,
    row_amino_embedding,
    column_amino_embedding,
    offset_embedding_matrix,
    grid_transition_expand,
    grid_transition_shrink,
    distance_bins_matrix,
):
    devices = n_rows * n_cols
    n_seq, amino, feature = homolog_stack.shape
    n_res = amino // devices
    seqs = n_seq * devices
    axes = ("row", "col")

    sent = chunks(homolog_stack, n_res).reshape(devices, n_seq * n_res, feature)
    moved = lax.all_to_all(sent, axes, split_axis=0, concat_axis=0, tiled=True)
    moved = moved.reshape(seqs * n_res, feature)

    unit = jnp.eye(n_res, dtype=BF16)
    factors = jnp.concatenate(
        [jnp.kron(unit, former_factor_matrix), jnp.kron(unit, latter_factor_matrix)], axis=1
    )
    amino_rows = jnp.concatenate(
        [per_amino_features, per_amino_features, jnp.zeros((16 - 2 * n_res, feature), BF16)], axis=0
    )
    projection = turn_projection(factor_mean_projection)
    aligned, piece = attention(
        moved,
        amino_rows,
        (
            asking_matrix,
            lookup_matrix,
            content_matrix,
            sigmoid_scaling_matrix,
            attention_result_matrix,
            factors,
            row_amino_embedding,
            column_amino_embedding,
        ),
        (stack_transition_expand_matrix, stack_transition_shrink_matrix),
        projection,
        n_res,
    )
    alignment_output = aligned.reshape(seqs, n_res, feature)

    table = plane_offsets(n_rows, n_cols)
    turn = []
    for p in range(devices):
        column, m = p // n_rows, p % n_rows
        turn.append((p, ((p // n_cols) ^ table[column][m]) * n_cols + column))
    turned = lax.ppermute(piece, axes, turn)

    def along_col(value, m):
        return lax.ppermute(value, "col", [(c, c ^ m) for c in range(n_cols)])

    def along_row(value, m):
        return lax.ppermute(value, "row", [(r, r ^ m) for r in range(n_rows)])

    own = [piece] + [along_col(piece, 2 * m) for m in range(1, n_cols // 2)]
    other = [along_col(value, 1) for value in own]
    col_pieces = [turned] + [along_row(turned, m) for m in range(1, n_rows)]

    inverse = []
    for line in table:
        back = [0] * n_rows
        for m, offset in enumerate(line):
            back[offset] = m
        inverse.extend(back)
    pair_output, distogram = pair_grid(
        inverse,
        own + other,
        col_pieces,
        (
            relative_rows(inverse, offset_embedding_matrix, n_cols, n_rows, n_res),
            distance_bins_matrix.T,
        ),
        (projection, grid_transition_expand, grid_transition_shrink),
        n_res,
        seqs,
    )
    return (alignment_output, pair_output, distogram)


def solution(mesh):
    n_rows, n_cols = mesh.shape["row"], mesh.shape["col"]
    assert n_cols == 2 * n_rows and n_rows & (n_rows - 1) == 0
    placed = (P(("row", "col"), None, None), P(("row", "col"), None)) + (P(),) * 16
    return jax.shard_map(
        functools.partial(shards, n_rows, n_cols),
        mesh=mesh,
        in_specs=placed,
        out_specs=(P(None, ("row", "col"), None), P("row", "col", None), P("row", "col", None)),
        check_vma=False,
    )
```

```python
import functools
import math

import jax
import jax.numpy as jnp
from jax import lax
from jax.experimental import pallas as pl
from jax.experimental.pallas import tpu as pltpu
from jax.sharding import PartitionSpec as P

HEAD = 32
CLIP = 32
LANES = 128
GROUP = 4
SWAP_LIMIT = 512
F32 = jnp.float32
BF16 = jnp.bfloat16


VMEM = pl.BlockSpec(memory_space=pltpu.VMEM)
HBM = pl.BlockSpec(memory_space=pltpu.MemorySpace.HBM)


def near(value):
    return pltpu.with_memory_space_constraint(value, pltpu.MemorySpace.VMEM)


def far(value):
    return pltpu.with_memory_space_constraint(value, pltpu.MemorySpace.HBM)


def local_call(kernel, *, scratch_shapes, **options):
    held = 0
    for ref in jax.tree.leaves(scratch_shapes):
        if ref.memory_space != pltpu.MemorySpace.VMEM:
            continue
        held += math.prod(ref.shape) * jnp.dtype(ref.dtype).itemsize
    limit = min(2 * held + (8 << 20), 48 << 20)
    return pl.pallas_call(
        kernel,
        scratch_shapes=scratch_shapes,
        compiler_params=pltpu.CompilerParams(vmem_limit_bytes=limit),
        **options,
    )


def dot(a, b):
    return jnp.dot(a, b, preferred_element_type=F32)


def standardize(values):
    middle = jnp.mean(values, -1, keepdims=True)
    centred = values - middle
    spread = jnp.mean(centred * centred, -1, keepdims=True)
    return centred * lax.rsqrt(spread + 1e-05)


def for_chunks(count, body):
    if count == 1:
        body(0)
    else:
        lax.fori_loop(0, count, lambda i, carry: (body(i), carry)[1], 0)


def rows_at(start, size):
    if not isinstance(start, int):
        start = pl.multiple_of(start, math.gcd(size, 128))
    return pl.ds(start, size)


def chunk_kernel(n_res, parts, x_far, o_far, x_in, o_out, came, left):
    n_seq, amino, feature = x_far.shape
    width = amino // parts
    rows = n_seq * width
    pair = 2 * n_res
    ins, outs = [], []
    for p in range(parts):
        ins.append(
            pltpu.make_async_copy(x_far.at[:, pl.ds(p * width, width), :], x_in.at[p], came.at[p])
        )
        ins[p].start()
    for p in range(parts):
        ins[p].wait()
        values = [
            x_in[p, seq].astype(F32).reshape(width // pair, pair, feature) for seq in range(n_seq)
        ]
        upper = lax.broadcasted_iota(jnp.int32, values[0].shape, 1) < n_res
        even, odd = [], []
        for seq in range(0, n_seq, 2):
            one, two = values[seq], values[seq + 1]
            even.append(jnp.where(upper, one, pltpu.roll(two, n_res, 1)))
            odd.append(jnp.where(upper, pltpu.roll(one, n_res, 1), two))
        made = jnp.stack(even + odd, axis=1).reshape(rows, feature)
        o_out[p * rows : (p + 1) * rows, :] = made.astype(BF16)
        part = pl.ds(p * rows, rows)
        outs.append(pltpu.make_async_copy(o_out.at[part], o_far.at[part], left.at[p]))
        outs[p].start()
    for copy in outs:
        copy.wait()


def chunks(x, n_res):
    n_seq, amino, feature = x.shape
    parts = 4
    width = amino // parts
    assert n_seq % 2 == 0 and 2 * n_res == 8
    return local_call(
        functools.partial(chunk_kernel, n_res, parts),
        out_shape=pltpu.HBM((n_seq * amino, feature), BF16),
        in_specs=[HBM],
        out_specs=HBM,
        scratch_shapes=[
            pltpu.VMEM((parts, n_seq, width, feature), BF16),
            pltpu.VMEM((n_seq * amino, feature), BF16),
            pltpu.SemaphoreType.DMA((parts,)),
            pltpu.SemaphoreType.DMA((parts,)),
        ],
        name="chunks",
    )(far(x))


def turn_kernel(w_ref, o_ref, w_scr):
    factor = math.isqrt(w_ref.shape[0])
    w_scr[...] = w_ref[...].astype(F32)
    for e in range(factor):
        o_ref[e * factor : (e + 1) * factor, :] = w_scr[pl.ds(e, factor, stride=factor), :].astype(
            BF16
        )


def turn_projection(w):
    return local_call(
        turn_kernel,
        out_shape=pltpu.HBM(w.shape, BF16),
        in_specs=[VMEM],
        out_specs=VMEM,
        scratch_shapes=[pltpu.VMEM(w.shape, F32)],
        name="turn",
    )(w)


def attention_kernel(
    n_res,
    x_ref,
    amino_ref,
    wq_ref,
    wk_ref,
    wv_ref,
    wg_ref,
    wo_ref,
    fg_ref,
    re_ref,
    ce_ref,
    w1_far,
    w2_far,
    _,
    _2,
    align_ref,
    send_ref,
    nat_scr,
    res_scr,
    q_scr,
    k_scr,
    v_scr,
    g_scr,
    mix_scr,
    ln_scr,
    w1_ref,
    w2_ref,
    arrived,
):
    fetch_1 = pltpu.make_async_copy(w1_far, w1_ref, arrived.at[0])
    fetch_2 = pltpu.make_async_copy(w2_far, w2_ref, arrived.at[1])
    fetch_1.start()
    fetch_2.start()
    rows, feature = x_ref.shape
    seqs = rows // n_res
    chunk = min(rows, 512)
    tiles = feature // LANES
    tile_lanes = [slice(t * LANES, (t + 1) * LANES) for t in range(tiles)]
    for t, lanes in enumerate(tile_lanes):
        nat_scr[t] = x_ref[:, lanes].astype(F32)
        for i in range(n_res):
            res_scr[i * seqs : (i + 1) * seqs, lanes] = nat_scr[t, pl.ds(i, seqs, stride=n_res), :]

    def project(step):
        at = rows_at(step * chunk, chunk)
        normed = standardize(res_scr[at, :]).astype(BF16)
        q_scr[at, :] = dot(normed, wq_ref[...]).astype(BF16)
        k_scr[at, :] = dot(normed, wk_ref[...]).astype(BF16)
        v_scr[at, :] = dot(normed, wv_ref[...]).astype(BF16)
        g_scr[at, :] = jax.nn.sigmoid(dot(normed, wg_ref[...]))

    for_chunks(rows // chunk, project)

    group = LANES // HEAD
    head_of_row = lax.broadcasted_iota(jnp.int32, (LANES, seqs), 0) // HEAD
    head_of_lane = lax.broadcasted_iota(jnp.int32, (seqs, LANES), 1) // HEAD
    scale = math.log2(math.e) / math.sqrt(HEAD)

    def attend(index, tile):
        at = rows_at(index * seqs, seqs)
        lanes = tile_lanes[tile]
        q_t = q_scr[at, lanes].astype(F32).T.astype(BF16)
        v_t = v_scr[at, lanes].astype(F32).T
        keys = k_scr[at, lanes].astype(F32)
        stacked = jnp.concatenate(
            [jnp.where(head_of_lane == h, keys, 0.0).astype(BF16) for h in range(group)], axis=0
        )
        scores = dot(stacked, q_t)
        powers, inverse = [], []
        for h in range(group):
            mine = scores[h * seqs : (h + 1) * seqs, :]
            power = jnp.exp2((mine - jnp.max(mine, axis=0, keepdims=True)) * scale)
            total = 1.0 / jnp.sum(power, axis=0, keepdims=True)
            powers.append(power.astype(BF16))
            inverse.append(jnp.broadcast_to(total, (HEAD, seqs)))
        values = jnp.concatenate(
            [jnp.where(head_of_row == h, v_t, 0.0).astype(BF16) for h in range(group)], axis=1
        )
        summed = dot(values, jnp.concatenate(powers, axis=0)) * jnp.concatenate(inverse, axis=0)
        mix_scr[at, lanes] = (summed.T * g_scr[at, lanes]).astype(BF16)

    if seqs <= LANES:
        for i in range(n_res):
            for tile in range(tiles):
                attend(i, tile)
    else:

        def attend_all(i):
            for tile in range(tiles):
                attend(i, tile)

        for_chunks(n_res, attend_all)

    fetch_1.wait()
    fetch_2.wait()

    def transition(step):
        at = rows_at(step * chunk, chunk)
        first = res_scr[at, :] + dot(mix_scr[at, :], wo_ref[...])
        hidden = jnp.maximum(dot(standardize(first).astype(BF16), w1_ref[...]), 0.0).astype(BF16)
        second = first + dot(hidden, w2_ref[...])
        align_ref[at, :] = second.astype(BF16)
        ln_scr[at, :] = standardize(second).astype(BF16)

    for_chunks(rows // chunk, transition)

    side = jnp.concatenate([ln_scr[i * seqs : (i + 1) * seqs, :] for i in range(n_res)], axis=1)
    factors = dot(side, fg_ref[...])
    send_ref[0:seqs, :] = factors[:, :LANES].astype(BF16)
    for t in range(seqs // LANES):
        turned = factors[t * LANES : (t + 1) * LANES, LANES:].T.astype(BF16)
        if seqs & (seqs - 1) == 0:
            turned = (turned.astype(F32) * (1.0 / seqs)).astype(BF16)
        send_ref[seqs + t * LANES : seqs + (t + 1) * LANES, :] = turned
    by_row = lax.broadcasted_iota(jnp.int32, (16, LANES), 0)
    pairs = jnp.where(
        by_row < n_res, dot(amino_ref[...], re_ref[...]), dot(amino_ref[...], ce_ref[...])
    )
    send_ref[2 * seqs :, :] = pairs.astype(BF16)


def attention(x, amino, weights, large, ready, n_res):
    rows, feature = x.shape
    seqs = rows // n_res
    return local_call(
        functools.partial(attention_kernel, n_res),
        out_shape=(
            pltpu.VMEM((rows, feature), BF16),
            pltpu.VMEM((2 * seqs + 16, LANES), BF16),
        ),
        in_specs=[VMEM] * (2 + len(weights)) + [HBM] * (len(large) + len(ready)),
        out_specs=(VMEM, VMEM),
        scratch_shapes=[
            pltpu.VMEM((feature // LANES, rows, LANES), F32),
            pltpu.VMEM((rows, feature), F32),
            pltpu.VMEM((rows, feature), BF16),
            pltpu.VMEM((rows, feature), BF16),
            pltpu.VMEM((rows, feature), BF16),
            pltpu.VMEM((rows, feature), F32),
            pltpu.VMEM((rows, feature), BF16),
            pltpu.VMEM((rows, feature), BF16),
            *[pltpu.VMEM(w.shape, BF16) for w in large],
            pltpu.SemaphoreType.DMA((len(large),)),
        ],
        name="attention",
    )(near(x), near(amino), *[near(w) for w in weights], *[far(w) for w in (*large, *ready)])


def placement(n_row, n_col, places):
    my_row = lax.axis_index("row")
    my_col = lax.axis_index("col")
    half = n_row // 2
    row_place = [my_col ^ (2 * (slot % half) + slot // half) for slot in range(n_row)]
    line = []
    for offset in range(n_col):
        entry = jnp.int32(places[offset])
        for column in range(1, n_row):
            entry = jnp.where(my_col == column, places[column * n_col + offset], entry)
        line.append(entry)
    source_row = my_col // (n_row // n_col)
    col_place = []
    for slot in range(n_col):
        key = my_row ^ slot ^ source_row
        where = line[0]
        for offset in range(1, n_col):
            where = jnp.where(key == offset, line[offset], where)
        col_place.append(where)
    return my_row, my_col, row_place, col_place


def relative_kernel(n_row, n_col, n_res, places, off_ref, o_ref, swap_ref, off_scr):
    my_row, my_col, row_place, col_place = placement(n_row, n_col, places)
    count_i, count_j = n_row * n_res, n_col * n_res
    row_start = my_row * count_i
    col_start = my_col * count_j
    bins = lax.broadcasted_iota(jnp.int32, (count_j, LANES), 1)
    j_here = col_start + lax.broadcasted_iota(jnp.int32, (count_j, LANES), 0)
    bins_m = lax.broadcasted_iota(jnp.int32, (count_i, LANES), 1)
    i_slot = lax.broadcasted_iota(jnp.int32, (count_i, LANES), 0)
    i_here = i_slot % n_res + row_start
    for slot in range(n_row):
        i_here = jnp.where(i_slot // n_res == slot, i_here + row_place[slot] * n_res, i_here)

    def relative(offset, lanes):
        index = jnp.clip(offset, -CLIP, CLIP) + CLIP
        return jnp.where(index == lanes, 1.0, 0.0).astype(BF16)

    marks = []
    for slot in range(n_row):
        for r in range(n_res):
            i = row_start + row_place[slot] * n_res + r
            marks.append(relative(j_here - i, bins))
    for slot in range(n_col):
        for r in range(n_res):
            j = col_start + col_place[slot] * n_res + r
            marks.append(relative(i_here - j, bins_m))
    off_scr[...] = jnp.zeros_like(off_scr)
    off_scr[0 : off_ref.shape[0], :] = off_ref[...].astype(F32)
    o_ref[...] = dot(jnp.concatenate(marks, axis=0), off_scr[...].astype(BF16)).astype(BF16)

    width = swap_ref.shape[1]
    chunk = min(swap_ref.shape[0], 128)
    source = lax.broadcasted_iota(jnp.int32, (chunk, width), 1)
    slot_of = source // (n_res * count_i)
    place = jnp.zeros_like(source)
    for slot in range(n_col):
        place = jnp.where(slot_of == slot, col_place[slot], place)
    goal = (source % count_i) * count_j + place * n_res + source // count_i % n_res
    line = lax.broadcasted_iota(jnp.int32, (chunk, width), 0)
    for start in range(0, swap_ref.shape[0], chunk):
        swap_ref[start : start + chunk, :] = jnp.where(goal == line + start, 1.0, 0.0).astype(BF16)


def relative_rows(places, table, n_row, n_col, n_res):
    cells = n_row * n_col * n_res * n_res
    swapped = cells if cells <= SWAP_LIMIT else LANES
    return local_call(
        functools.partial(relative_kernel, n_row, n_col, n_res, places),
        out_shape=(pltpu.HBM((2 * cells, LANES), BF16), pltpu.HBM((swapped, swapped), BF16)),
        in_specs=[VMEM],
        out_specs=(VMEM, VMEM),
        scratch_shapes=[pltpu.VMEM((LANES, LANES), F32)],
        name="relative",
    )(near(table))


def pair_kernel(n_row, n_col, n_res, seqs, places, *refs):
    row_refs = refs[0:n_row]
    col_refs = refs[n_row : n_row + n_col]
    refs = refs[n_row + n_col :]
    rel_ref, swap_ref, bins_ref, wp_far, w1_far, w2_far, pair_far, dist_far = refs[:8]
    (a_r, a_c, lhs, grid, logit_scr) = refs[8:13]
    wp_ref, w1_ref, w2_ref, bd_ref, pair_ref, dist_ref, arrived, left_sem = refs[13:]
    fetches = [
        pltpu.make_async_copy(away, local, arrived.at[k])
        for k, (away, local) in enumerate(((wp_far, wp_ref), (w1_far, w1_ref), (w2_far, w2_ref)))
    ]
    for fetch in fetches:
        fetch.start()
    factor = LANES // n_res
    count_i = n_row * n_res
    count_j = n_col * n_res
    _, _, row_place, col_place = placement(n_row, n_col, places)

    def clear(e):
        for r in range(n_res):
            row = (e * n_res + r) * factor
            for other in range(n_res):
                if other != r:
                    bd_ref[row : row + factor, other * LANES : (other + 1) * LANES] = jnp.zeros(
                        (factor, LANES), BF16
                    )

    def fill(e):
        block = wp_ref[e * factor : (e + 1) * factor, :]
        for r in range(n_res):
            row = (e * n_res + r) * factor
            bd_ref[row : row + factor, r * LANES : (r + 1) * LANES] = block

    def gather_rows(count, places):
        width = GROUP * count
        line = lax.broadcasted_iota(jnp.int32, (width, width), 0)
        column = lax.broadcasted_iota(jnp.int32, (width, width), 1)
        piece = column // (GROUP * n_res)
        place = piece
        if places is not None:
            for slot, where in enumerate(places):
                place = jnp.where(piece == slot, where, place)
        goal = column % GROUP * count + place * n_res + column // GROUP % n_res
        return jnp.where(line == goal, 1.0, 0.0).astype(BF16)

    def stack(pieces, g):
        lanes = []
        for t in range(seqs // LANES):
            first = seqs + t * LANES + g * GROUP * n_res
            lanes.append(
                jnp.concatenate([p[first : first + GROUP * n_res, :] for p in pieces], axis=0)
            )
        return jnp.concatenate(lanes, axis=1)

    gather_c = gather_rows(count_j, col_place)
    gather_r = gather_rows(count_i, None)
    groups = factor // GROUP
    for g in range(groups):
        a_c[g * GROUP * count_j : (g + 1) * GROUP * count_j, :] = dot(
            gather_c, stack(col_refs, g)
        ).astype(BF16)
        a_r[g * GROUP * count_i : (g + 1) * GROUP * count_i, :] = dot(
            gather_r, stack(row_refs, g)
        ).astype(BF16)
        for e in range(g * GROUP, (g + 1) * GROUP):
            clear(e)
    for fetch in fetches:
        fetch.wait()
    todo = list(range(factor))

    exact = seqs & (seqs - 1) == 0

    def outer(a_ref, count, pieces, base):
        rows = factor * count
        chunk = min(rows, 1024)
        per = chunk // count
        step_pieces = 2
        for s in range(0, len(pieces), step_pieces):
            left = jnp.concatenate([p[0:seqs, :] for p in pieces[s : s + step_pieces]], axis=1)

            def one(step):
                made = dot(a_ref[rows_at(step * chunk, chunk), :], left)
                if not exact:
                    made = made * (1.0 / seqs)
                made = made.astype(BF16)
                for k in range(step_pieces):
                    for e in range(per):
                        lane = (step * per + e) * LANES
                        if not isinstance(lane, int):
                            lane = pl.multiple_of(lane, LANES)
                        lhs[
                            base + (s + k) * count : base + (s + k + 1) * count, pl.ds(lane, LANES)
                        ] = made[e * count : (e + 1) * count, k * LANES : (k + 1) * LANES]

            for_chunks(rows // chunk, one)
            for _ in range(min(share, len(todo))):
                fill(todo.pop())

    share = -(-factor * 2 // (n_row + n_col))
    direct = n_row * count_j
    mirrored = n_col * count_i
    outer(a_c, count_j, row_refs, 0)
    outer(a_r, count_i, col_refs, direct)

    while todo:
        fill(todo.pop())

    row_side = jnp.concatenate([r[2 * seqs : 2 * seqs + 16, :] for r in row_refs], axis=0)
    col_side = jnp.concatenate([r[2 * seqs : 2 * seqs + 16, :] for r in col_refs], axis=0)

    def pick(side, places, count):
        width = side.shape[0]
        line = lax.broadcasted_iota(jnp.int32, (count, width), 0)
        column = lax.broadcasted_iota(jnp.int32, (count, width), 1)
        goal = column % 16 - n_res
        place = jnp.zeros_like(column)
        for slot, where in enumerate(places):
            place = jnp.where(column // 16 == slot, where, place)
        hit = (goal >= 0) & (goal < n_res) & (line == place * n_res + goal)
        return dot(jnp.where(hit, 1.0, 0.0).astype(BF16), side)

    right_r = pick(row_side, list(range(n_row)), count_i)
    right_c = pick(col_side, col_place, count_j)
    total = direct + mirrored
    chunk = min(total, 256)

    def project(step):
        at = rows_at(step * chunk, chunk)
        made = dot(lhs[at, :], bd_ref[...])
        lhs_out[at, :] = made

    lhs_out = grid[1]
    start = grid[0]
    for_chunks(total // chunk, project)
    side_r = row_side.astype(F32)
    side_c = col_side.astype(F32)
    place = 0
    for slot in range(n_row):
        for r in range(n_res):
            made = lhs_out[slot * count_j : (slot + 1) * count_j, r * LANES : (r + 1) * LANES]
            left = side_r[slot * 16 + r : slot * 16 + r + 1, :]
            start[place : place + count_j, :] = (
                (left + right_c) + rel_ref[place : place + count_j, :] + made
            )
            place += count_j
    for slot in range(n_col):
        for r in range(n_res):
            made = lhs_out[
                direct + slot * count_i : direct + (slot + 1) * count_i,
                r * LANES : (r + 1) * LANES,
            ]
            left = side_c[slot * 16 + r : slot * 16 + r + 1, :]
            start[place : place + count_i, :] = (
                (left + right_r) + rel_ref[place : place + count_i, :] + made
            )
            place += count_i

    cells = count_i * count_j
    n_bins = dist_ref.shape[2]
    chunk2 = min(cells, 512)
    rounded_scr, all_logits = grid[2], grid[3]

    def transition(step):
        at = rows_at(step * chunk2, chunk2)
        begin = start[at, :]
        hidden = jnp.maximum(dot(standardize(begin).astype(BF16), w1_ref[...]), 0.0).astype(BF16)
        final = (begin + dot(hidden, w2_ref[...])).astype(BF16)
        rounded_scr[at, :] = final
        if swap_ref.shape[0] == cells:
            return
        all_logits[at, :] = lax.dot_general(
            final, bins_ref[...], (((1,), (1,)), ((), ())), preferred_element_type=F32
        )

    steps = cells // chunk2
    for_chunks(steps, transition)
    for slot in range(n_row):
        for r in range(n_res):
            at = (slot * n_res + r) * count_j
            goal = row_place[slot] * n_res + r
            pair_ref[goal] = rounded_scr[at : at + count_j, :]
    leave_pair = pltpu.make_async_copy(pair_ref, pair_far, left_sem.at[0])
    leave_pair.start()
    if steps == 1:
        transition(1)
    else:
        for_chunks(steps, lambda step: transition(step + steps))
    if swap_ref.shape[0] == cells:
        swapped = dot(swap_ref[...], rounded_scr[cells:, :]).astype(BF16)
        both = jnp.concatenate([rounded_scr[:cells, :], swapped], axis=1)
        twice = jnp.concatenate([bins_ref[...], bins_ref[...]], axis=1)
        made = lax.dot_general(
            both, twice, (((1,), (1,)), ((), ())), preferred_element_type=F32
        ).astype(BF16)
        leaves = [leave_pair]
        for slot in range(n_row):
            for r in range(n_res):
                at = (slot * n_res + r) * count_j
                dist_ref[row_place[slot] * n_res + r] = made[at : at + count_j, :]
        leave = pltpu.make_async_copy(dist_ref, dist_far, left_sem.at[1])
        leave.start()
        leave_pair.wait()
        leave.wait()
        return
    for slot in range(n_col):
        for r in range(n_res):
            source = cells + (slot * n_res + r) * count_i
            goal = (col_place[slot] * n_res + r) * count_i
            logit_scr[rows_at(goal, count_i), :n_bins] = all_logits[source : source + count_i, :]
    leaves = [leave_pair]
    for slot in range(n_row):
        for r in range(n_res):
            at = (slot * n_res + r) * count_j
            goal = row_place[slot] * n_res + r
            mirror = logit_scr[pl.ds(slot * n_res + r, count_j, stride=count_i), :]
            summed = all_logits[at : at + count_j, :] + mirror[:, :n_bins]
            dist_ref[goal] = summed.astype(BF16)
        rows = pl.ds(row_place[slot] * n_res, n_res)
        leave = pltpu.make_async_copy(dist_ref.at[rows], dist_far.at[rows], left_sem.at[1 + slot])
        leave.start()
        leaves.append(leave)
    for leave in leaves:
        leave.wait()


def pair_grid(places, row_pieces, col_pieces, weights, large, n_res, seqs):
    n_row, n_col = len(row_pieces), len(col_pieces)
    count_i, count_j = n_row * n_res, n_col * n_res
    factor = LANES // n_res
    total = n_row * count_j + n_col * count_i
    cells = count_i * count_j
    n_bins = weights[2].shape[0]
    return local_call(
        functools.partial(pair_kernel, n_row, n_col, n_res, seqs, places),
        out_shape=(
            jax.ShapeDtypeStruct((count_i, count_j, LANES), BF16),
            jax.ShapeDtypeStruct((count_i, count_j, n_bins), BF16),
        ),
        in_specs=[VMEM] * (n_row + n_col + len(weights)) + [HBM] * len(large),
        out_specs=(HBM, HBM),
        scratch_shapes=[
            pltpu.VMEM((factor * count_i, seqs), BF16),
            pltpu.VMEM((factor * count_j, seqs), BF16),
            pltpu.VMEM((total, factor * LANES), BF16),
            (
                pltpu.VMEM((2 * cells, LANES), F32),
                pltpu.VMEM((total, n_res * LANES), F32),
                pltpu.VMEM((2 * cells, LANES), BF16),
                pltpu.VMEM((2 * cells, n_bins), F32),
            ),
            pltpu.VMEM((cells, LANES), F32),
            *[pltpu.VMEM(w.shape, BF16) for w in large],
            pltpu.VMEM((factor * LANES, n_res * LANES), BF16),
            pltpu.VMEM((count_i, count_j, LANES), BF16),
            pltpu.VMEM((count_i, count_j, n_bins), BF16),
            pltpu.SemaphoreType.DMA((len(large),)),
            pltpu.SemaphoreType.DMA((1 + n_row,)),
        ],
        name="pairs",
    )(*[near(v) for v in (*row_pieces, *col_pieces, *weights)], *[far(w) for w in large])


def plane_offsets(n_row, n_col):
    offsets = []
    by_hops = sorted(range(n_row), key=lambda v: (bin(v).count("1"), v))
    for column in range(n_col):
        home = column // 2
        far = sorted(
            range(n_row),
            key=lambda m: (-abs((column * n_row + m) % n_col // 2 - home), m),
        )
        line = [0] * n_row
        for position, m in enumerate(far):
            line[m] = by_hops[position]
        offsets.append(line)
    return offsets


def shards(
    n_rows,
    n_cols,
    homolog_stack,
    per_amino_features,
    asking_matrix,
    lookup_matrix,
    content_matrix,
    sigmoid_scaling_matrix,
    attention_result_matrix,
    stack_transition_expand_matrix,
    stack_transition_shrink_matrix,
    former_factor_matrix,
    latter_factor_matrix,
    factor_mean_projection,
    row_amino_embedding,
    column_amino_embedding,
    offset_embedding_matrix,
    grid_transition_expand,
    grid_transition_shrink,
    distance_bins_matrix,
):
    devices = n_rows * n_cols
    n_seq, amino, feature = homolog_stack.shape
    n_res = amino // devices
    seqs = n_seq * devices
    axes = ("row", "col")

    sent = chunks(homolog_stack, n_res).reshape(devices, n_seq * n_res, feature)
    moved = lax.all_to_all(sent, axes, split_axis=0, concat_axis=0, tiled=True)
    moved = moved.reshape(seqs * n_res, feature)

    unit = jnp.eye(n_res, dtype=BF16)
    grouped = latter_factor_matrix.reshape(feature, -1, GROUP)
    latter = jnp.einsum("pr,fge->pfgre", unit, grouped).reshape(n_res * feature, -1)
    factors = jnp.concatenate([jnp.kron(unit, former_factor_matrix), latter], axis=1)
    amino_rows = jnp.concatenate(
        [per_amino_features, per_amino_features, jnp.zeros((16 - 2 * n_res, feature), BF16)], axis=0
    )
    projection = turn_projection(factor_mean_projection)
    table = plane_offsets(n_rows, n_cols)
    inverse = []
    for line in table:
        back = [0] * n_rows
        for m, offset in enumerate(line):
            back[offset] = m
        inverse.extend(back)
    relative, swap = relative_rows(inverse, offset_embedding_matrix, n_cols, n_rows, n_res)

    aligned, piece = attention(
        moved,
        amino_rows,
        (
            asking_matrix,
            lookup_matrix,
            content_matrix,
            sigmoid_scaling_matrix,
            attention_result_matrix,
            factors,
            row_amino_embedding,
            column_amino_embedding,
        ),
        (stack_transition_expand_matrix, stack_transition_shrink_matrix),
        (projection, relative),
        n_res,
    )
    alignment_output = aligned.reshape(n_res, seqs, feature).transpose(1, 0, 2)

    turn = []
    for p in range(devices):
        column, m = p // n_rows, p % n_rows
        turn.append((p, ((p // n_cols) ^ table[column][m]) * n_cols + column))
    turned = lax.ppermute(piece, axes, turn)

    def along_col(value, m):
        return lax.ppermute(value, "col", [(c, c ^ m) for c in range(n_cols)])

    def along_row(value, m):
        return lax.ppermute(value, "row", [(r, r ^ m) for r in range(n_rows)])

    own = [piece] + [along_col(piece, 2 * m) for m in range(1, n_cols // 2)]
    other = [along_col(value, 1) for value in own]
    col_pieces = [turned] + [along_row(turned, m) for m in range(1, n_rows)]

    pair_output, distogram = pair_grid(
        inverse,
        own + other,
        col_pieces,
        (
            relative,
            swap,
            distance_bins_matrix.T,
        ),
        (projection, grid_transition_expand, grid_transition_shrink),
        n_res,
        seqs,
    )
    return (alignment_output, pair_output, distogram)


def solution(mesh):
    n_rows, n_cols = mesh.shape["row"], mesh.shape["col"]
    assert n_cols == 2 * n_rows and n_rows & (n_rows - 1) == 0
    placed = (P(("row", "col"), None, None), P(("row", "col"), None)) + (P(),) * 16
    return jax.shard_map(
        functools.partial(shards, n_rows, n_cols),
        mesh=mesh,
        in_specs=placed,
        out_specs=(P(None, ("row", "col"), None), P("row", "col", None), P("row", "col", None)),
        check_vma=False,
    )
```

```python
import functools
import math

import jax
import jax.numpy as jnp
from jax import lax
from jax.experimental import pallas as pl
from jax.experimental.pallas import tpu as pltpu
from jax.sharding import PartitionSpec as P

HEAD = 32
CLIP = 32
LANES = 128
GROUP = 4
PAIR = 2
SWAP_LIMIT = 512
F32 = jnp.float32
BF16 = jnp.bfloat16


VMEM = pl.BlockSpec(memory_space=pltpu.VMEM)
HBM = pl.BlockSpec(memory_space=pltpu.MemorySpace.HBM)


def near(value):
    return pltpu.with_memory_space_constraint(value, pltpu.MemorySpace.VMEM)


def far(value):
    return pltpu.with_memory_space_constraint(value, pltpu.MemorySpace.HBM)


def local_call(kernel, *, scratch_shapes, **options):
    held = 0
    for ref in jax.tree.leaves(scratch_shapes):
        if ref.memory_space != pltpu.MemorySpace.VMEM:
            continue
        held += math.prod(ref.shape) * jnp.dtype(ref.dtype).itemsize
    limit = min(2 * held + (8 << 20), 48 << 20)
    return pl.pallas_call(
        kernel,
        scratch_shapes=scratch_shapes,
        compiler_params=pltpu.CompilerParams(vmem_limit_bytes=limit),
        **options,
    )


def dot(a, b):
    return jnp.dot(a, b, preferred_element_type=F32)


def standardize(values):
    middle = jnp.mean(values, -1, keepdims=True)
    centred = values - middle
    spread = jnp.mean(centred * centred, -1, keepdims=True)
    return centred * lax.rsqrt(spread + 1e-05)


def for_chunks(count, body):
    if count == 1:
        body(0)
    else:
        lax.fori_loop(0, count, lambda i, carry: (body(i), carry)[1], 0)


def rows_at(start, size):
    if not isinstance(start, int):
        start = pl.multiple_of(start, math.gcd(size, 128))
    return pl.ds(start, size)


def chunk_kernel(n_res, parts, x_far, o_far, x_in, o_out, came, left):
    n_seq, amino, feature = x_far.shape
    width = amino // parts
    rows = n_seq * width
    pair = 2 * n_res
    ins, outs = [], []
    for p in range(parts):
        ins.append(
            pltpu.make_async_copy(x_far.at[:, pl.ds(p * width, width), :], x_in.at[p], came.at[p])
        )
        ins[p].start()
    for p in range(parts):
        ins[p].wait()
        values = [
            x_in[p, seq].astype(F32).reshape(width // pair, pair, feature) for seq in range(n_seq)
        ]
        upper = lax.broadcasted_iota(jnp.int32, values[0].shape, 1) < n_res
        even, odd = [], []
        for seq in range(0, n_seq, 2):
            one, two = values[seq], values[seq + 1]
            even.append(jnp.where(upper, one, pltpu.roll(two, n_res, 1)))
            odd.append(jnp.where(upper, pltpu.roll(one, n_res, 1), two))
        made = jnp.stack(even + odd, axis=1).reshape(rows, feature)
        o_out[p * rows : (p + 1) * rows, :] = made.astype(BF16)
        part = pl.ds(p * rows, rows)
        outs.append(pltpu.make_async_copy(o_out.at[part], o_far.at[part], left.at[p]))
        outs[p].start()
    for copy in outs:
        copy.wait()


def chunks(x, n_res):
    n_seq, amino, feature = x.shape
    parts = 4
    width = amino // parts
    assert n_seq % 2 == 0 and 2 * n_res == 8
    return local_call(
        functools.partial(chunk_kernel, n_res, parts),
        out_shape=pltpu.HBM((n_seq * amino, feature), BF16),
        in_specs=[HBM],
        out_specs=HBM,
        scratch_shapes=[
            pltpu.VMEM((parts, n_seq, width, feature), BF16),
            pltpu.VMEM((n_seq * amino, feature), BF16),
            pltpu.SemaphoreType.DMA((parts,)),
            pltpu.SemaphoreType.DMA((parts,)),
        ],
        name="chunks",
    )(far(x))


def turn_kernel(w_ref, o_ref, w_scr):
    factor = math.isqrt(w_ref.shape[0])
    w_scr[...] = w_ref[...].astype(F32)
    for e in range(factor):
        o_ref[e * factor : (e + 1) * factor, :] = w_scr[pl.ds(e, factor, stride=factor), :].astype(
            BF16
        )


def turn_projection(w):
    return local_call(
        turn_kernel,
        out_shape=pltpu.HBM(w.shape, BF16),
        in_specs=[VMEM],
        out_specs=VMEM,
        scratch_shapes=[pltpu.VMEM(w.shape, F32)],
        name="turn",
    )(w)


def attention_kernel(
    n_res,
    x_ref,
    amino_ref,
    wq_ref,
    wk_ref,
    wv_ref,
    wg_ref,
    wo_ref,
    fg_ref,
    re_ref,
    ce_ref,
    w1_ref,
    w2_ref,
    _,
    _2,
    align_ref,
    send_ref,
    nat_scr,
    res_scr,
    q_scr,
    k_scr,
    v_scr,
    g_scr,
    mix_scr,
    ln_scr,
):
    rows, feature = x_ref.shape
    seqs = rows // n_res
    chunk = min(rows, 512)
    tiles = feature // LANES
    tile_lanes = [slice(t * LANES, (t + 1) * LANES) for t in range(tiles)]
    for t, lanes in enumerate(tile_lanes):
        nat_scr[t] = x_ref[:, lanes].astype(F32)
        for i in range(n_res):
            res_scr[i * seqs : (i + 1) * seqs, lanes] = nat_scr[t, pl.ds(i, seqs, stride=n_res), :]

    def project(step):
        at = rows_at(step * chunk, chunk)
        normed = standardize(res_scr[at, :]).astype(BF16)
        q_scr[at, :] = dot(normed, wq_ref[...]).astype(BF16)
        k_scr[at, :] = dot(normed, wk_ref[...]).astype(BF16)
        v_scr[at, :] = dot(normed, wv_ref[...]).astype(BF16)
        g_scr[at, :] = jax.nn.sigmoid(dot(normed, wg_ref[...]))

    for_chunks(rows // chunk, project)

    group = LANES // HEAD
    head_of_row = lax.broadcasted_iota(jnp.int32, (LANES, seqs), 0) // HEAD
    head_of_lane = lax.broadcasted_iota(jnp.int32, (seqs, LANES), 1) // HEAD
    scale = math.log2(math.e) / math.sqrt(HEAD)

    def attend(index, tile):
        at = rows_at(index * seqs, seqs)
        lanes = tile_lanes[tile]
        q_t = q_scr[at, lanes].astype(F32).T.astype(BF16)
        v_t = v_scr[at, lanes].astype(F32).T
        keys = k_scr[at, lanes].astype(F32)
        stacked = jnp.concatenate(
            [jnp.where(head_of_lane == h, keys, 0.0).astype(BF16) for h in range(group)], axis=0
        )
        scores = dot(stacked, q_t)
        powers, inverse = [], []
        for h in range(group):
            mine = scores[h * seqs : (h + 1) * seqs, :]
            power = jnp.exp2((mine - jnp.max(mine, axis=0, keepdims=True)) * scale)
            total = 1.0 / jnp.sum(power, axis=0, keepdims=True)
            powers.append(power.astype(BF16))
            inverse.append(jnp.broadcast_to(total, (HEAD, seqs)))
        values = jnp.concatenate(
            [jnp.where(head_of_row == h, v_t, 0.0).astype(BF16) for h in range(group)], axis=1
        )
        summed = dot(values, jnp.concatenate(powers, axis=0)) * jnp.concatenate(inverse, axis=0)
        mix_scr[at, lanes] = (summed.T * g_scr[at, lanes]).astype(BF16)

    if seqs <= LANES:
        for i in range(n_res):
            for tile in range(tiles):
                attend(i, tile)
    else:

        def attend_all(i):
            for tile in range(tiles):
                attend(i, tile)

        for_chunks(n_res, attend_all)

    def transition(step):
        at = rows_at(step * chunk, chunk)
        first = res_scr[at, :] + dot(mix_scr[at, :], wo_ref[...])
        hidden = jnp.maximum(dot(standardize(first).astype(BF16), w1_ref[...]), 0.0).astype(BF16)
        second = first + dot(hidden, w2_ref[...])
        align_ref[at, :] = second.astype(BF16)
        ln_scr[at, :] = standardize(second).astype(BF16)

    for_chunks(rows // chunk, transition)

    side = jnp.concatenate([ln_scr[i * seqs : (i + 1) * seqs, :] for i in range(n_res)], axis=1)
    factors = dot(side, fg_ref[...])
    send_ref[0:seqs, :] = factors[:, :LANES].astype(BF16)
    for t in range(seqs // LANES):
        turned = factors[t * LANES : (t + 1) * LANES, LANES:].T.astype(BF16)
        if seqs & (seqs - 1) == 0:
            turned = (turned.astype(F32) * (1.0 / seqs)).astype(BF16)
        send_ref[seqs + t * LANES : seqs + (t + 1) * LANES, :] = turned
    by_row = lax.broadcasted_iota(jnp.int32, (16, LANES), 0)
    pairs = jnp.where(
        by_row < n_res, dot(amino_ref[...], re_ref[...]), dot(amino_ref[...], ce_ref[...])
    )
    send_ref[2 * seqs :, :] = pairs.astype(BF16)


def attention(x, amino, weights, ready, n_res):
    rows, feature = x.shape
    seqs = rows // n_res
    return local_call(
        functools.partial(attention_kernel, n_res),
        out_shape=(
            pltpu.VMEM((rows, feature), BF16),
            pltpu.VMEM((2 * seqs + 16, LANES), BF16),
        ),
        in_specs=[VMEM] * (2 + len(weights)) + [HBM] * len(ready),
        out_specs=(VMEM, VMEM),
        scratch_shapes=[
            pltpu.VMEM((feature // LANES, rows, LANES), F32),
            pltpu.VMEM((rows, feature), F32),
            pltpu.VMEM((rows, feature), BF16),
            pltpu.VMEM((rows, feature), BF16),
            pltpu.VMEM((rows, feature), BF16),
            pltpu.VMEM((rows, feature), F32),
            pltpu.VMEM((rows, feature), BF16),
            pltpu.VMEM((rows, feature), BF16),
        ],
        name="attention",
    )(near(x), near(amino), *[near(w) for w in weights], *[far(w) for w in ready])


def placement(n_row, n_col, places):
    my_row = lax.axis_index("row")
    my_col = lax.axis_index("col")
    half = n_row // 2
    row_place = [my_col ^ (2 * (slot % half) + slot // half) for slot in range(n_row)]
    line = []
    for offset in range(n_col):
        entry = jnp.int32(places[offset])
        for column in range(1, n_row):
            entry = jnp.where(my_col == column, places[column * n_col + offset], entry)
        line.append(entry)
    source_row = my_col // (n_row // n_col)
    col_place = []
    for slot in range(n_col):
        key = my_row ^ slot ^ source_row
        where = line[0]
        for offset in range(1, n_col):
            where = jnp.where(key == offset, line[offset], where)
        col_place.append(where)
    return my_row, my_col, row_place, col_place


def relative_kernel(n_row, n_col, n_res, places, off_ref, o_ref, swap_ref, off_scr):
    my_row, my_col, row_place, col_place = placement(n_row, n_col, places)
    count_i, count_j = n_row * n_res, n_col * n_res
    row_start = my_row * count_i
    col_start = my_col * count_j
    bins = lax.broadcasted_iota(jnp.int32, (count_j, LANES), 1)
    j_here = col_start + lax.broadcasted_iota(jnp.int32, (count_j, LANES), 0)
    bins_m = lax.broadcasted_iota(jnp.int32, (count_i, LANES), 1)
    i_slot = lax.broadcasted_iota(jnp.int32, (count_i, LANES), 0)
    i_here = i_slot % n_res + row_start
    for slot in range(n_row):
        i_here = jnp.where(i_slot // n_res == slot, i_here + row_place[slot] * n_res, i_here)

    def relative(offset, lanes):
        index = jnp.clip(offset, -CLIP, CLIP) + CLIP
        return jnp.where(index == lanes, 1.0, 0.0).astype(BF16)

    marks = []
    for slot in range(n_row):
        for r in range(n_res):
            i = row_start + row_place[slot] * n_res + r
            marks.append(relative(j_here - i, bins))
    for slot in range(n_col):
        for r in range(n_res):
            j = col_start + col_place[slot] * n_res + r
            marks.append(relative(i_here - j, bins_m))
    off_scr[...] = jnp.zeros_like(off_scr)
    off_scr[0 : off_ref.shape[0], :] = off_ref[...].astype(F32)
    o_ref[...] = dot(jnp.concatenate(marks, axis=0), off_scr[...].astype(BF16)).astype(BF16)

    width = swap_ref.shape[1]
    chunk = min(swap_ref.shape[0], 128)
    source = lax.broadcasted_iota(jnp.int32, (chunk, width), 1)
    slot_of = source // (n_res * count_i)
    place = jnp.zeros_like(source)
    for slot in range(n_col):
        place = jnp.where(slot_of == slot, col_place[slot], place)
    goal = (source % count_i) * count_j + place * n_res + source // count_i % n_res
    line = lax.broadcasted_iota(jnp.int32, (chunk, width), 0)
    for start in range(0, swap_ref.shape[0], chunk):
        swap_ref[start : start + chunk, :] = jnp.where(goal == line + start, 1.0, 0.0).astype(BF16)


def relative_rows(places, table, n_row, n_col, n_res):
    cells = n_row * n_col * n_res * n_res
    swapped = cells if cells <= SWAP_LIMIT else LANES
    return local_call(
        functools.partial(relative_kernel, n_row, n_col, n_res, places),
        out_shape=(pltpu.HBM((2 * cells, LANES), BF16), pltpu.HBM((swapped, swapped), BF16)),
        in_specs=[VMEM],
        out_specs=(VMEM, VMEM),
        scratch_shapes=[pltpu.VMEM((LANES, LANES), F32)],
        name="relative",
    )(near(table))


def pair_kernel(n_row, n_col, n_res, seqs, places, *refs):
    row_refs = refs[0:n_row]
    col_refs = refs[n_row : n_row + n_col]
    refs = refs[n_row + n_col :]
    rel_ref, swap_ref, bins_ref, wp_ref, w1_ref, w2_ref, pair_far, dist_far = refs[:8]
    (a_r, a_c, lhs, grid, logit_scr) = refs[8:13]
    bd_ref, pair_ref, dist_ref, left_sem = refs[13:]
    factor = LANES // n_res
    count_i = n_row * n_res
    count_j = n_col * n_res
    _, _, row_place, col_place = placement(n_row, n_col, places)

    halves = n_res // PAIR

    def fill(e):
        block = wp_ref[e * factor : (e + 1) * factor, :]
        for r in range(PAIR):
            row = (e * PAIR + r) * factor
            for other in range(PAIR):
                bd_ref[row : row + factor, other * LANES : (other + 1) * LANES] = (
                    block if other == r else jnp.zeros_like(block)
                )

    def gather_rows(count, places):
        width = GROUP * count
        line = lax.broadcasted_iota(jnp.int32, (width, width), 0)
        column = lax.broadcasted_iota(jnp.int32, (width, width), 1)
        piece = column // (GROUP * n_res)
        place = piece
        if places is not None:
            for slot, where in enumerate(places):
                place = jnp.where(piece == slot, where, place)
        goal = column % GROUP * count + place * n_res + column // GROUP % n_res
        return jnp.where(line == goal, 1.0, 0.0).astype(BF16)

    def stack(pieces, g):
        lanes = []
        for t in range(seqs // LANES):
            first = seqs + t * LANES + g * GROUP * n_res
            lanes.append(
                jnp.concatenate([p[first : first + GROUP * n_res, :] for p in pieces], axis=0)
            )
        return jnp.concatenate(lanes, axis=1)

    gather_c = gather_rows(count_j, col_place)
    gather_r = gather_rows(count_i, None)
    groups = factor // GROUP
    for g in range(groups):
        for a_ref, gather, pieces, count in (
            (a_c, gather_c, col_refs, count_j),
            (a_r, gather_r, row_refs, count_i),
        ):
            made = dot(gather, stack(pieces, g)).astype(BF16)
            for k in range(GROUP):
                row = (g * GROUP + k) // PAIR * count
                lane = k % PAIR * seqs
                a_ref[row : row + count, lane : lane + seqs] = made[k * count : (k + 1) * count, :]
    todo = list(range(factor))

    exact = seqs & (seqs - 1) == 0
    width = LANES // PAIR
    lane_half = lax.broadcasted_iota(jnp.int32, (seqs, LANES), 1) // width

    def aside(value):
        value = value.astype(F32)
        rows = []
        for e in range(PAIR):
            tiles = []
            for half in range(halves):
                shifted = value if half == e else pltpu.roll(value, width, 1)
                tiles.append(jnp.where(lane_half == e, shifted, 0.0))
            rows.append(jnp.concatenate(tiles, axis=1))
        return jnp.concatenate(rows, axis=0).astype(BF16)

    def outer(a_ref, count, pieces, base):
        rows = factor // PAIR * count
        chunk = min(rows, 1024)
        per = chunk // count
        for s, piece in enumerate(pieces):
            left = aside(piece[0:seqs, :])

            def one(step):
                made = dot(a_ref[rows_at(step * chunk, chunk), :], left)
                if not exact:
                    made = made * (1.0 / seqs)
                made = made.astype(BF16)
                for e in range(per):
                    lane = (step * per + e) * LANES
                    if not isinstance(lane, int):
                        lane = pl.multiple_of(lane, LANES)
                    for half in range(halves):
                        row = base + (half * len(pieces) + s) * count
                        lhs[row : row + count, pl.ds(lane, LANES)] = made[
                            e * count : (e + 1) * count, half * LANES : (half + 1) * LANES
                        ]

            for_chunks(rows // chunk, one)
            for _ in range(min(share, len(todo))):
                fill(todo.pop())

    share = -(-factor // (n_row + n_col))
    direct = halves * n_row * count_j
    mirrored = halves * n_col * count_i
    outer(a_c, count_j, row_refs, 0)
    outer(a_r, count_i, col_refs, direct)
    while todo:
        fill(todo.pop())

    row_side = jnp.concatenate([r[2 * seqs : 2 * seqs + 16, :] for r in row_refs], axis=0)
    col_side = jnp.concatenate([r[2 * seqs : 2 * seqs + 16, :] for r in col_refs], axis=0)

    def pick(side, places, count):
        width = side.shape[0]
        line = lax.broadcasted_iota(jnp.int32, (count, width), 0)
        column = lax.broadcasted_iota(jnp.int32, (count, width), 1)
        goal = column % 16 - n_res
        place = jnp.zeros_like(column)
        for slot, where in enumerate(places):
            place = jnp.where(column // 16 == slot, where, place)
        hit = (goal >= 0) & (goal < n_res) & (line == place * n_res + goal)
        return dot(jnp.where(hit, 1.0, 0.0).astype(BF16), side)

    right_r = pick(row_side, list(range(n_row)), count_i)
    right_c = pick(col_side, col_place, count_j)
    total = direct + mirrored
    chunk = min(total, 256)

    def project(step):
        at = rows_at(step * chunk, chunk)
        made = dot(lhs[at, :], bd_ref[...])
        lhs_out[at, :] = made

    lhs_out = grid[1]
    start = grid[0]
    if total == 2 * chunk:
        project(0)
        project(1)
    else:
        for_chunks(total // chunk, project)
    side_r = row_side.astype(F32)
    side_c = col_side.astype(F32)
    place = 0
    for slot in range(n_row):
        for r in range(n_res):
            row = (r // PAIR * n_row + slot) * count_j
            lane = r % PAIR * LANES
            made = lhs_out[row : row + count_j, lane : lane + LANES]
            left = side_r[slot * 16 + r : slot * 16 + r + 1, :]
            start[place : place + count_j, :] = (
                (left + right_c) + rel_ref[place : place + count_j, :] + made
            )
            place += count_j
    for slot in range(n_col):
        for r in range(n_res):
            row = direct + (r // PAIR * n_col + slot) * count_i
            lane = r % PAIR * LANES
            made = lhs_out[row : row + count_i, lane : lane + LANES]
            left = side_c[slot * 16 + r : slot * 16 + r + 1, :]
            start[place : place + count_i, :] = (
                (left + right_r) + rel_ref[place : place + count_i, :] + made
            )
            place += count_i

    cells = count_i * count_j
    n_bins = dist_ref.shape[2]
    chunk2 = min(cells, 512)
    rounded_scr, all_logits = grid[2], grid[3]

    def transition(step):
        at = rows_at(step * chunk2, chunk2)
        begin = start[at, :]
        hidden = jnp.maximum(dot(standardize(begin).astype(BF16), w1_ref[...]), 0.0).astype(BF16)
        final = (begin + dot(hidden, w2_ref[...])).astype(BF16)
        rounded_scr[at, :] = final
        if swap_ref.shape[0] == cells:
            return
        all_logits[at, :] = lax.dot_general(
            final, bins_ref[...], (((1,), (1,)), ((), ())), preferred_element_type=F32
        )

    steps = cells // chunk2
    for_chunks(steps, transition)
    for slot in range(n_row):
        for r in range(n_res):
            at = (slot * n_res + r) * count_j
            goal = row_place[slot] * n_res + r
            pair_ref[goal] = rounded_scr[at : at + count_j, :]
    leave_pair = pltpu.make_async_copy(pair_ref, pair_far, left_sem.at[0])
    leave_pair.start()
    if steps == 1:
        transition(1)
    else:
        for_chunks(steps, lambda step: transition(step + steps))
    if swap_ref.shape[0] == cells:
        swapped = dot(swap_ref[...], rounded_scr[cells:, :]).astype(BF16)
        both = jnp.concatenate([rounded_scr[:cells, :], swapped], axis=1)
        twice = jnp.concatenate([bins_ref[...], bins_ref[...]], axis=1)
        made = lax.dot_general(
            both, twice, (((1,), (1,)), ((), ())), preferred_element_type=F32
        ).astype(BF16)
        leaves = [leave_pair]
        for slot in range(n_row):
            for r in range(n_res):
                at = (slot * n_res + r) * count_j
                dist_ref[row_place[slot] * n_res + r] = made[at : at + count_j, :]
        leave = pltpu.make_async_copy(dist_ref, dist_far, left_sem.at[1])
        leave.start()
        leave_pair.wait()
        leave.wait()
        return
    for slot in range(n_col):
        for r in range(n_res):
            source = cells + (slot * n_res + r) * count_i
            goal = (col_place[slot] * n_res + r) * count_i
            logit_scr[rows_at(goal, count_i), :n_bins] = all_logits[source : source + count_i, :]
    leaves = [leave_pair]
    for slot in range(n_row):
        for r in range(n_res):
            at = (slot * n_res + r) * count_j
            goal = row_place[slot] * n_res + r
            mirror = logit_scr[pl.ds(slot * n_res + r, count_j, stride=count_i), :]
            summed = all_logits[at : at + count_j, :] + mirror[:, :n_bins]
            dist_ref[goal] = summed.astype(BF16)
        rows = pl.ds(row_place[slot] * n_res, n_res)
        leave = pltpu.make_async_copy(dist_ref.at[rows], dist_far.at[rows], left_sem.at[1 + slot])
        leave.start()
        leaves.append(leave)
    for leave in leaves:
        leave.wait()


def pair_grid(places, row_pieces, col_pieces, weights, n_res, seqs):
    n_row, n_col = len(row_pieces), len(col_pieces)
    count_i, count_j = n_row * n_res, n_col * n_res
    factor = LANES // n_res
    total = (n_row * count_j + n_col * count_i) * n_res // PAIR
    cells = count_i * count_j
    n_bins = weights[2].shape[0]
    return local_call(
        functools.partial(pair_kernel, n_row, n_col, n_res, seqs, places),
        out_shape=(
            jax.ShapeDtypeStruct((count_i, count_j, LANES), BF16),
            jax.ShapeDtypeStruct((count_i, count_j, n_bins), BF16),
        ),
        in_specs=[VMEM] * (n_row + n_col + len(weights)),
        out_specs=(HBM, HBM),
        scratch_shapes=[
            pltpu.VMEM((factor // PAIR * count_i, PAIR * seqs), BF16),
            pltpu.VMEM((factor // PAIR * count_j, PAIR * seqs), BF16),
            pltpu.VMEM((total, factor // PAIR * LANES), BF16),
            (
                pltpu.VMEM((2 * cells, LANES), F32),
                pltpu.VMEM((total, PAIR * LANES), F32),
                pltpu.VMEM((2 * cells, LANES), BF16),
                pltpu.VMEM((2 * cells, n_bins), F32),
            ),
            pltpu.VMEM((cells, LANES), F32),
            pltpu.VMEM((factor // PAIR * LANES, PAIR * LANES), BF16),
            pltpu.VMEM((count_i, count_j, LANES), BF16),
            pltpu.VMEM((count_i, count_j, n_bins), BF16),
            pltpu.SemaphoreType.DMA((1 + n_row,)),
        ],
        name="pairs",
    )(*[near(v) for v in (*row_pieces, *col_pieces, *weights)])


def plane_offsets(n_row, n_col):
    offsets = []
    by_hops = sorted(range(n_row), key=lambda v: (bin(v).count("1"), v))
    for column in range(n_col):
        home = column // 2
        far = sorted(
            range(n_row),
            key=lambda m: (-abs((column * n_row + m) % n_col // 2 - home), m),
        )
        line = [0] * n_row
        for position, m in enumerate(far):
            line[m] = by_hops[position]
        offsets.append(line)
    return offsets


def shards(
    n_rows,
    n_cols,
    homolog_stack,
    per_amino_features,
    asking_matrix,
    lookup_matrix,
    content_matrix,
    sigmoid_scaling_matrix,
    attention_result_matrix,
    stack_transition_expand_matrix,
    stack_transition_shrink_matrix,
    former_factor_matrix,
    latter_factor_matrix,
    factor_mean_projection,
    row_amino_embedding,
    column_amino_embedding,
    offset_embedding_matrix,
    grid_transition_expand,
    grid_transition_shrink,
    distance_bins_matrix,
):
    devices = n_rows * n_cols
    n_seq, amino, feature = homolog_stack.shape
    n_res = amino // devices
    seqs = n_seq * devices
    axes = ("row", "col")

    sent = chunks(homolog_stack, n_res).reshape(devices, n_seq * n_res, feature)
    moved = lax.all_to_all(sent, axes, split_axis=0, concat_axis=0, tiled=True)
    moved = moved.reshape(seqs * n_res, feature)

    unit = jnp.eye(n_res, dtype=BF16)
    grouped = latter_factor_matrix.reshape(feature, -1, GROUP)
    latter = jnp.einsum("pr,fge->pfgre", unit, grouped).reshape(n_res * feature, -1)
    factors = jnp.concatenate([jnp.kron(unit, former_factor_matrix), latter], axis=1)
    amino_rows = jnp.concatenate(
        [per_amino_features, per_amino_features, jnp.zeros((16 - 2 * n_res, feature), BF16)], axis=0
    )
    projection = turn_projection(factor_mean_projection)
    table = plane_offsets(n_rows, n_cols)
    inverse = []
    for line in table:
        back = [0] * n_rows
        for m, offset in enumerate(line):
            back[offset] = m
        inverse.extend(back)
    relative, swap = relative_rows(inverse, offset_embedding_matrix, n_cols, n_rows, n_res)

    aligned, piece = attention(
        moved,
        amino_rows,
        (
            asking_matrix,
            lookup_matrix,
            content_matrix,
            sigmoid_scaling_matrix,
            attention_result_matrix,
            factors,
            row_amino_embedding,
            column_amino_embedding,
            stack_transition_expand_matrix,
            stack_transition_shrink_matrix,
        ),
        (projection, relative),
        n_res,
    )
    alignment_output = aligned.reshape(n_res, seqs, feature).transpose(1, 0, 2)

    turn = []
    for p in range(devices):
        column, m = p // n_rows, p % n_rows
        turn.append((p, ((p // n_cols) ^ table[column][m]) * n_cols + column))
    turned = lax.ppermute(piece, axes, turn)

    def along_col(value, m):
        return lax.ppermute(value, "col", [(c, c ^ m) for c in range(n_cols)])

    def along_row(value, m):
        return lax.ppermute(value, "row", [(r, r ^ m) for r in range(n_rows)])

    own = [piece] + [along_col(piece, 2 * m) for m in range(1, n_cols // 2)]
    other = [along_col(value, 1) for value in own]
    col_pieces = [turned] + [along_row(turned, m) for m in range(1, n_rows)]

    pair_output, distogram = pair_grid(
        inverse,
        own + other,
        col_pieces,
        (
            relative,
            swap,
            distance_bins_matrix.T,
            projection,
            grid_transition_expand,
            grid_transition_shrink,
        ),
        n_res,
        seqs,
    )
    return (alignment_output, pair_output, distogram)


def solution(mesh):
    n_rows, n_cols = mesh.shape["row"], mesh.shape["col"]
    assert n_cols == 2 * n_rows and n_rows & (n_rows - 1) == 0
    placed = (P(("row", "col"), None, None), P(("row", "col"), None)) + (P(),) * 16
    return jax.shard_map(
        functools.partial(shards, n_rows, n_cols),
        mesh=mesh,
        in_specs=placed,
        out_specs=(P(None, ("row", "col"), None), P("row", "col", None), P("row", "col", None)),
        check_vma=False,
    )
```

```python
import functools
import math

import jax
import jax.numpy as jnp
from jax import lax
from jax.experimental import pallas as pl
from jax.experimental.pallas import tpu as pltpu
from jax.sharding import PartitionSpec as P

HEAD = 32
CLIP = 32
LANES = 128
GROUP = 4
PAIR = 2
SWAP_LIMIT = 512
F32 = jnp.float32
BF16 = jnp.bfloat16


VMEM = pl.BlockSpec(memory_space=pltpu.VMEM)
HBM = pl.BlockSpec(memory_space=pltpu.MemorySpace.HBM)


def near(value):
    return pltpu.with_memory_space_constraint(value, pltpu.MemorySpace.VMEM)


def far(value):
    return pltpu.with_memory_space_constraint(value, pltpu.MemorySpace.HBM)


def local_call(kernel, *, scratch_shapes, **options):
    held = 0
    for ref in jax.tree.leaves(scratch_shapes):
        if ref.memory_space != pltpu.MemorySpace.VMEM:
            continue
        held += math.prod(ref.shape) * jnp.dtype(ref.dtype).itemsize
    limit = min(2 * held + (8 << 20), 48 << 20)
    return pl.pallas_call(
        kernel,
        scratch_shapes=scratch_shapes,
        compiler_params=pltpu.CompilerParams(vmem_limit_bytes=limit),
        **options,
    )


def dot(a, b):
    return jnp.dot(a, b, preferred_element_type=F32)


def standardize(values):
    middle = jnp.mean(values, -1, keepdims=True)
    centred = values - middle
    spread = jnp.mean(centred * centred, -1, keepdims=True)
    return centred * lax.rsqrt(spread + 1e-05)


def for_chunks(count, body):
    if count == 1:
        body(0)
    else:
        lax.fori_loop(0, count, lambda i, carry: (body(i), carry)[1], 0)


def rows_at(start, size):
    if not isinstance(start, int):
        start = pl.multiple_of(start, math.gcd(size, 128))
    return pl.ds(start, size)


def chunk_kernel(n_res, parts, x_far, o_far, x_in, o_out, came, left):
    n_seq, amino, feature = x_far.shape
    width = amino // parts
    rows = n_seq * width
    pair = 2 * n_res
    ins, outs = [], []
    for p in range(parts):
        ins.append(
            pltpu.make_async_copy(x_far.at[:, pl.ds(p * width, width), :], x_in.at[p], came.at[p])
        )
        ins[p].start()
    for p in range(parts):
        ins[p].wait()
        values = [
            x_in[p, seq].astype(F32).reshape(width // pair, pair, feature) for seq in range(n_seq)
        ]
        upper = lax.broadcasted_iota(jnp.int32, values[0].shape, 1) < n_res
        even, odd = [], []
        for seq in range(0, n_seq, 2):
            one, two = values[seq], values[seq + 1]
            even.append(jnp.where(upper, one, pltpu.roll(two, n_res, 1)))
            odd.append(jnp.where(upper, pltpu.roll(one, n_res, 1), two))
        made = jnp.stack(even + odd, axis=1).reshape(rows, feature)
        o_out[p * rows : (p + 1) * rows, :] = made.astype(BF16)
        part = pl.ds(p * rows, rows)
        outs.append(pltpu.make_async_copy(o_out.at[part], o_far.at[part], left.at[p]))
        outs[p].start()
    for copy in outs:
        copy.wait()


def chunks(x, n_res):
    n_seq, amino, feature = x.shape
    parts = 4
    width = amino // parts
    assert n_seq % 2 == 0 and 2 * n_res == 8
    return local_call(
        functools.partial(chunk_kernel, n_res, parts),
        out_shape=pltpu.HBM((n_seq * amino, feature), BF16),
        in_specs=[HBM],
        out_specs=HBM,
        scratch_shapes=[
            pltpu.VMEM((parts, n_seq, width, feature), BF16),
            pltpu.VMEM((n_seq * amino, feature), BF16),
            pltpu.SemaphoreType.DMA((parts,)),
            pltpu.SemaphoreType.DMA((parts,)),
        ],
        name="chunks",
    )(far(x))


def turn_kernel(w_ref, o_ref, w_scr):
    factor = math.isqrt(w_ref.shape[0])
    w_scr[...] = w_ref[...].astype(F32)
    for e in range(factor):
        o_ref[e * factor : (e + 1) * factor, :] = w_scr[pl.ds(e, factor, stride=factor), :].astype(
            BF16
        )


def turn_projection(w):
    return local_call(
        turn_kernel,
        out_shape=pltpu.HBM(w.shape, BF16),
        in_specs=[VMEM],
        out_specs=VMEM,
        scratch_shapes=[pltpu.VMEM(w.shape, F32)],
        name="turn",
    )(w)


def attention_kernel(
    n_res,
    x_ref,
    amino_ref,
    wq_ref,
    wk_ref,
    wv_ref,
    wg_ref,
    wo_ref,
    fg_ref,
    re_ref,
    ce_ref,
    w1_ref,
    w2_ref,
    _,
    _2,
    align_ref,
    send_ref,
    nat_scr,
    res_scr,
    q_scr,
    k_scr,
    v_scr,
    g_scr,
    mix_scr,
    ln_scr,
):
    rows, feature = x_ref.shape
    seqs = rows // n_res
    chunk = min(rows, 512)
    tiles = feature // LANES
    tile_lanes = [slice(t * LANES, (t + 1) * LANES) for t in range(tiles)]
    for t, lanes in enumerate(tile_lanes):
        nat_scr[t] = x_ref[:, lanes].astype(F32)
        for i in range(n_res):
            res_scr[i * seqs : (i + 1) * seqs, lanes] = nat_scr[t, pl.ds(i, seqs, stride=n_res), :]

    def project(step):
        at = rows_at(step * chunk, chunk)
        normed = standardize(res_scr[at, :]).astype(BF16)
        q_scr[at, :] = dot(normed, wq_ref[...]).astype(BF16)
        k_scr[at, :] = dot(normed, wk_ref[...]).astype(BF16)
        v_scr[at, :] = dot(normed, wv_ref[...]).astype(BF16)
        g_scr[at, :] = jax.nn.sigmoid(dot(normed, wg_ref[...]))

    for_chunks(rows // chunk, project)

    group = LANES // HEAD
    head_of_row = lax.broadcasted_iota(jnp.int32, (LANES, seqs), 0) // HEAD
    head_of_lane = lax.broadcasted_iota(jnp.int32, (seqs, LANES), 1) // HEAD
    scale = math.log2(math.e) / math.sqrt(HEAD)

    def attend(index, tile):
        at = rows_at(index * seqs, seqs)
        lanes = tile_lanes[tile]
        q_t = q_scr[at, lanes].astype(F32).T.astype(BF16)
        v_t = v_scr[at, lanes].astype(F32).T
        keys = k_scr[at, lanes].astype(F32)
        stacked = jnp.concatenate(
            [jnp.where(head_of_lane == h, keys, 0.0).astype(BF16) for h in range(group)], axis=0
        )
        scores = dot(stacked, q_t)
        powers, inverse = [], []
        for h in range(group):
            mine = scores[h * seqs : (h + 1) * seqs, :]
            power = jnp.exp2((mine - jnp.max(mine, axis=0, keepdims=True)) * scale)
            total = 1.0 / jnp.sum(power, axis=0, keepdims=True)
            powers.append(power.astype(BF16))
            inverse.append(jnp.broadcast_to(total, (HEAD, seqs)))
        values = jnp.concatenate(
            [jnp.where(head_of_row == h, v_t, 0.0).astype(BF16) for h in range(group)], axis=1
        )
        summed = dot(values, jnp.concatenate(powers, axis=0)) * jnp.concatenate(inverse, axis=0)
        mix_scr[at, lanes] = (summed.T * g_scr[at, lanes]).astype(BF16)

    block = 2 * seqs if seqs <= LANES else chunk

    def transition(step):
        at = rows_at(step * block, block)
        first = res_scr[at, :] + dot(mix_scr[at, :], wo_ref[...])
        hidden = jnp.maximum(dot(standardize(first).astype(BF16), w1_ref[...]), 0.0).astype(BF16)
        second = first + dot(hidden, w2_ref[...])
        align_ref[at, :] = second.astype(BF16)
        ln_scr[at, :] = standardize(second).astype(BF16)

    if seqs <= LANES:
        for i in range(n_res):
            for tile in range(tiles):
                attend(i, tile)
        for step in range(n_res // 2):
            transition(step)
    else:
        def attend_all(i):
            for tile in range(tiles):
                attend(i, tile)

        for_chunks(n_res, attend_all)
        for_chunks(rows // block, transition)

    side = jnp.concatenate([ln_scr[i * seqs : (i + 1) * seqs, :] for i in range(n_res)], axis=1)
    factors = dot(side, fg_ref[...])
    send_ref[0:seqs, :] = factors[:, :LANES].astype(BF16)
    for t in range(seqs // LANES):
        turned = factors[t * LANES : (t + 1) * LANES, LANES:].T.astype(BF16)
        if seqs & (seqs - 1) == 0:
            turned = (turned.astype(F32) * (1.0 / seqs)).astype(BF16)
        send_ref[seqs + t * LANES : seqs + (t + 1) * LANES, :] = turned
    by_row = lax.broadcasted_iota(jnp.int32, (16, LANES), 0)
    pairs = jnp.where(
        by_row < n_res, dot(amino_ref[...], re_ref[...]), dot(amino_ref[...], ce_ref[...])
    )
    send_ref[2 * seqs :, :] = pairs.astype(BF16)


def attention(x, amino, weights, ready, n_res):
    rows, feature = x.shape
    seqs = rows // n_res
    return local_call(
        functools.partial(attention_kernel, n_res),
        out_shape=(
            pltpu.VMEM((rows, feature), BF16),
            pltpu.VMEM((2 * seqs + 16, LANES), BF16),
        ),
        in_specs=[VMEM] * (2 + len(weights)) + [HBM] * len(ready),
        out_specs=(VMEM, VMEM),
        scratch_shapes=[
            pltpu.VMEM((feature // LANES, rows, LANES), F32),
            pltpu.VMEM((rows, feature), F32),
            pltpu.VMEM((rows, feature), BF16),
            pltpu.VMEM((rows, feature), BF16),
            pltpu.VMEM((rows, feature), BF16),
            pltpu.VMEM((rows, feature), F32),
            pltpu.VMEM((rows, feature), BF16),
            pltpu.VMEM((rows, feature), BF16),
        ],
        name="attention",
    )(near(x), near(amino), *[near(w) for w in weights], *[far(w) for w in ready])


def placement(n_row, n_col, places):
    my_row = lax.axis_index("row")
    my_col = lax.axis_index("col")
    half = n_row // 2
    row_place = [my_col ^ (2 * (slot % half) + slot // half) for slot in range(n_row)]
    line = []
    for offset in range(n_col):
        entry = jnp.int32(places[offset])
        for column in range(1, n_row):
            entry = jnp.where(my_col == column, places[column * n_col + offset], entry)
        line.append(entry)
    source_row = my_col // (n_row // n_col)
    col_place = []
    for slot in range(n_col):
        key = my_row ^ slot ^ source_row
        where = line[0]
        for offset in range(1, n_col):
            where = jnp.where(key == offset, line[offset], where)
        col_place.append(where)
    return my_row, my_col, row_place, col_place


def relative_kernel(n_row, n_col, n_res, places, off_ref, o_ref, swap_ref, off_scr):
    my_row, my_col, row_place, col_place = placement(n_row, n_col, places)
    count_i, count_j = n_row * n_res, n_col * n_res
    row_start = my_row * count_i
    col_start = my_col * count_j
    bins = lax.broadcasted_iota(jnp.int32, (count_j, LANES), 1)
    j_here = col_start + lax.broadcasted_iota(jnp.int32, (count_j, LANES), 0)
    bins_m = lax.broadcasted_iota(jnp.int32, (count_i, LANES), 1)
    i_slot = lax.broadcasted_iota(jnp.int32, (count_i, LANES), 0)
    i_here = i_slot % n_res + row_start
    for slot in range(n_row):
        i_here = jnp.where(i_slot // n_res == slot, i_here + row_place[slot] * n_res, i_here)

    def relative(offset, lanes):
        index = jnp.clip(offset, -CLIP, CLIP) + CLIP
        return jnp.where(index == lanes, 1.0, 0.0).astype(BF16)

    marks = []
    for slot in range(n_row):
        for r in range(n_res):
            i = row_start + row_place[slot] * n_res + r
            marks.append(relative(j_here - i, bins))
    for slot in range(n_col):
        for r in range(n_res):
            j = col_start + col_place[slot] * n_res + r
            marks.append(relative(i_here - j, bins_m))
    off_scr[...] = jnp.zeros_like(off_scr)
    off_scr[0 : off_ref.shape[0], :] = off_ref[...].astype(F32)
    o_ref[...] = dot(jnp.concatenate(marks, axis=0), off_scr[...].astype(BF16)).astype(BF16)

    width = swap_ref.shape[1]
    chunk = min(swap_ref.shape[0], 128)
    source = lax.broadcasted_iota(jnp.int32, (chunk, width), 1)
    slot_of = source // (n_res * count_i)
    place = jnp.zeros_like(source)
    for slot in range(n_col):
        place = jnp.where(slot_of == slot, col_place[slot], place)
    goal = (source % count_i) * count_j + place * n_res + source // count_i % n_res
    line = lax.broadcasted_iota(jnp.int32, (chunk, width), 0)
    for start in range(0, swap_ref.shape[0], chunk):
        swap_ref[start : start + chunk, :] = jnp.where(goal == line + start, 1.0, 0.0).astype(BF16)


def relative_rows(places, table, n_row, n_col, n_res):
    cells = n_row * n_col * n_res * n_res
    swapped = cells if cells <= SWAP_LIMIT else LANES
    return local_call(
        functools.partial(relative_kernel, n_row, n_col, n_res, places),
        out_shape=(pltpu.HBM((2 * cells, LANES), BF16), pltpu.HBM((swapped, swapped), BF16)),
        in_specs=[VMEM],
        out_specs=(VMEM, VMEM),
        scratch_shapes=[pltpu.VMEM((LANES, LANES), F32)],
        name="relative",
    )(near(table))


def pair_kernel(n_row, n_col, n_res, seqs, places, *refs):
    row_refs = refs[0:n_row]
    col_refs = refs[n_row : n_row + n_col]
    refs = refs[n_row + n_col :]
    rel_ref, swap_ref, bins_ref, wp_ref, w1_ref, w2_ref, pair_far, dist_far = refs[:8]
    (a_r, a_c, lhs, grid, logit_scr) = refs[8:13]
    bd_ref, pair_ref, dist_ref, left_sem = refs[13:]
    factor = LANES // n_res
    count_i = n_row * n_res
    count_j = n_col * n_res
    _, _, row_place, col_place = placement(n_row, n_col, places)

    halves = n_res // PAIR

    def fill(e):
        block = wp_ref[e * factor : (e + 1) * factor, :]
        for r in range(PAIR):
            row = (e * PAIR + r) * factor
            for other in range(PAIR):
                bd_ref[row : row + factor, other * LANES : (other + 1) * LANES] = (
                    block if other == r else jnp.zeros_like(block)
                )

    def gather_rows(count, places):
        width = GROUP * count
        line = lax.broadcasted_iota(jnp.int32, (width, width), 0)
        column = lax.broadcasted_iota(jnp.int32, (width, width), 1)
        piece = column // (GROUP * n_res)
        place = piece
        if places is not None:
            for slot, where in enumerate(places):
                place = jnp.where(piece == slot, where, place)
        goal = column % GROUP * count + place * n_res + column // GROUP % n_res
        return jnp.where(line == goal, 1.0, 0.0).astype(BF16)

    def stack(pieces, g):
        lanes = []
        for t in range(seqs // LANES):
            first = seqs + t * LANES + g * GROUP * n_res
            lanes.append(
                jnp.concatenate([p[first : first + GROUP * n_res, :] for p in pieces], axis=0)
            )
        return jnp.concatenate(lanes, axis=1)

    gather_c = gather_rows(count_j, col_place)
    gather_r = gather_rows(count_i, None)
    groups = factor // GROUP
    for g in range(groups):
        for a_ref, gather, pieces, count in (
            (a_c, gather_c, col_refs, count_j),
            (a_r, gather_r, row_refs, count_i),
        ):
            made = dot(gather, stack(pieces, g)).astype(BF16)
            for k in range(GROUP):
                row = (g * GROUP + k) // PAIR * count
                lane = k % PAIR * seqs
                a_ref[row : row + count, lane : lane + seqs] = made[k * count : (k + 1) * count, :]
    todo = list(range(factor))

    exact = seqs & (seqs - 1) == 0
    width = LANES // PAIR
    lane_half = lax.broadcasted_iota(jnp.int32, (seqs, LANES), 1) // width

    def aside(value):
        value = value.astype(F32)
        rows = []
        for e in range(PAIR):
            tiles = []
            for half in range(halves):
                shifted = value if half == e else pltpu.roll(value, width, 1)
                tiles.append(jnp.where(lane_half == e, shifted, 0.0))
            rows.append(jnp.concatenate(tiles, axis=1))
        return jnp.concatenate(rows, axis=0).astype(BF16)

    def outer(a_ref, count, pieces, base):
        rows = factor // PAIR * count
        chunk = min(rows, 1024)
        per = chunk // count
        for s, piece in enumerate(pieces):
            left = aside(piece[0:seqs, :])

            def one(step):
                made = dot(a_ref[rows_at(step * chunk, chunk), :], left)
                if not exact:
                    made = made * (1.0 / seqs)
                made = made.astype(BF16)
                for e in range(per):
                    lane = (step * per + e) * LANES
                    if not isinstance(lane, int):
                        lane = pl.multiple_of(lane, LANES)
                    for half in range(halves):
                        row = base + (half * len(pieces) + s) * count
                        lhs[row : row + count, pl.ds(lane, LANES)] = made[
                            e * count : (e + 1) * count, half * LANES : (half + 1) * LANES
                        ]

            for_chunks(rows // chunk, one)
            for _ in range(min(share, len(todo))):
                fill(todo.pop())

    share = -(-factor // (n_row + n_col))
    direct = halves * n_row * count_j
    mirrored = halves * n_col * count_i
    outer(a_c, count_j, row_refs, 0)
    outer(a_r, count_i, col_refs, direct)
    while todo:
        fill(todo.pop())

    row_side = jnp.concatenate([r[2 * seqs : 2 * seqs + 16, :] for r in row_refs], axis=0)
    col_side = jnp.concatenate([r[2 * seqs : 2 * seqs + 16, :] for r in col_refs], axis=0)

    def pick(side, places, count):
        width = side.shape[0]
        line = lax.broadcasted_iota(jnp.int32, (count, width), 0)
        column = lax.broadcasted_iota(jnp.int32, (count, width), 1)
        goal = column % 16 - n_res
        place = jnp.zeros_like(column)
        for slot, where in enumerate(places):
            place = jnp.where(column // 16 == slot, where, place)
        hit = (goal >= 0) & (goal < n_res) & (line == place * n_res + goal)
        return dot(jnp.where(hit, 1.0, 0.0).astype(BF16), side)

    right_r = pick(row_side, list(range(n_row)), count_i)
    right_c = pick(col_side, col_place, count_j)
    total = direct + mirrored
    chunk = min(total, 256)

    def project(step):
        at = rows_at(step * chunk, chunk)
        made = dot(lhs[at, :], bd_ref[...])
        lhs_out[at, :] = made

    lhs_out = grid[1]
    start = grid[0]
    if total == 2 * chunk:
        project(0)
        project(1)
    else:
        for_chunks(total // chunk, project)
    side_r = row_side.astype(F32)
    side_c = col_side.astype(F32)
    place = 0
    for slot in range(n_row):
        for r in range(n_res):
            row = (r // PAIR * n_row + slot) * count_j
            lane = r % PAIR * LANES
            made = lhs_out[row : row + count_j, lane : lane + LANES]
            left = side_r[slot * 16 + r : slot * 16 + r + 1, :]
            start[place : place + count_j, :] = (
                (left + right_c) + rel_ref[place : place + count_j, :] + made
            )
            place += count_j
    for slot in range(n_col):
        for r in range(n_res):
            row = direct + (r // PAIR * n_col + slot) * count_i
            lane = r % PAIR * LANES
            made = lhs_out[row : row + count_i, lane : lane + LANES]
            left = side_c[slot * 16 + r : slot * 16 + r + 1, :]
            start[place : place + count_i, :] = (
                (left + right_r) + rel_ref[place : place + count_i, :] + made
            )
            place += count_i

    cells = count_i * count_j
    n_bins = dist_ref.shape[2]
    chunk2 = min(cells, 512)
    rounded_scr, all_logits = grid[2], grid[3]

    def transition(step):
        at = rows_at(step * chunk2, chunk2)
        begin = start[at, :]
        hidden = jnp.maximum(dot(standardize(begin).astype(BF16), w1_ref[...]), 0.0).astype(BF16)
        final = (begin + dot(hidden, w2_ref[...])).astype(BF16)
        rounded_scr[at, :] = final
        if swap_ref.shape[0] == cells:
            return
        all_logits[at, :] = lax.dot_general(
            final, bins_ref[...], (((1,), (1,)), ((), ())), preferred_element_type=F32
        )

    steps = cells // chunk2
    for_chunks(steps, transition)
    for slot in range(n_row):
        for r in range(n_res):
            at = (slot * n_res + r) * count_j
            goal = row_place[slot] * n_res + r
            pair_ref[goal] = rounded_scr[at : at + count_j, :]
    leave_pair = pltpu.make_async_copy(pair_ref, pair_far, left_sem.at[0])
    leave_pair.start()
    if steps == 1:
        transition(1)
    else:
        for_chunks(steps, lambda step: transition(step + steps))
    if swap_ref.shape[0] == cells:
        swapped = dot(swap_ref[...], rounded_scr[cells:, :]).astype(BF16)
        both = jnp.concatenate([rounded_scr[:cells, :], swapped], axis=1)
        twice = jnp.concatenate([bins_ref[...], bins_ref[...]], axis=1)
        made = lax.dot_general(
            both, twice, (((1,), (1,)), ((), ())), preferred_element_type=F32
        ).astype(BF16)
        leaves = [leave_pair]
        for slot in range(n_row):
            for r in range(n_res):
                at = (slot * n_res + r) * count_j
                dist_ref[row_place[slot] * n_res + r] = made[at : at + count_j, :]
        leave = pltpu.make_async_copy(dist_ref, dist_far, left_sem.at[1])
        leave.start()
        leave_pair.wait()
        leave.wait()
        return
    for slot in range(n_col):
        for r in range(n_res):
            source = cells + (slot * n_res + r) * count_i
            goal = (col_place[slot] * n_res + r) * count_i
            logit_scr[rows_at(goal, count_i), :n_bins] = all_logits[source : source + count_i, :]
    leaves = [leave_pair]
    for slot in range(n_row):
        for r in range(n_res):
            at = (slot * n_res + r) * count_j
            goal = row_place[slot] * n_res + r
            mirror = logit_scr[pl.ds(slot * n_res + r, count_j, stride=count_i), :]
            summed = all_logits[at : at + count_j, :] + mirror[:, :n_bins]
            dist_ref[goal] = summed.astype(BF16)
        rows = pl.ds(row_place[slot] * n_res, n_res)
        leave = pltpu.make_async_copy(dist_ref.at[rows], dist_far.at[rows], left_sem.at[1 + slot])
        leave.start()
        leaves.append(leave)
    for leave in leaves:
        leave.wait()


def pair_grid(places, row_pieces, col_pieces, weights, n_res, seqs):
    n_row, n_col = len(row_pieces), len(col_pieces)
    count_i, count_j = n_row * n_res, n_col * n_res
    factor = LANES // n_res
    total = (n_row * count_j + n_col * count_i) * n_res // PAIR
    cells = count_i * count_j
    n_bins = weights[2].shape[0]
    return local_call(
        functools.partial(pair_kernel, n_row, n_col, n_res, seqs, places),
        out_shape=(
            jax.ShapeDtypeStruct((count_i, count_j, LANES), BF16),
            jax.ShapeDtypeStruct((count_i, count_j, n_bins), BF16),
        ),
        in_specs=[VMEM] * (n_row + n_col + len(weights)),
        out_specs=(HBM, HBM),
        scratch_shapes=[
            pltpu.VMEM((factor // PAIR * count_i, PAIR * seqs), BF16),
            pltpu.VMEM((factor // PAIR * count_j, PAIR * seqs), BF16),
            pltpu.VMEM((total, factor // PAIR * LANES), BF16),
            (
                pltpu.VMEM((2 * cells, LANES), F32),
                pltpu.VMEM((total, PAIR * LANES), F32),
                pltpu.VMEM((2 * cells, LANES), BF16),
                pltpu.VMEM((2 * cells, n_bins), F32),
            ),
            pltpu.VMEM((cells, LANES), F32),
            pltpu.VMEM((factor // PAIR * LANES, PAIR * LANES), BF16),
            pltpu.VMEM((count_i, count_j, LANES), BF16),
            pltpu.VMEM((count_i, count_j, n_bins), BF16),
            pltpu.SemaphoreType.DMA((1 + n_row,)),
        ],
        name="pairs",
    )(*[near(v) for v in (*row_pieces, *col_pieces, *weights)])


def plane_offsets(n_row, n_col):
    offsets = []
    by_hops = sorted(range(n_row), key=lambda v: (bin(v).count("1"), v))
    for column in range(n_col):
        home = column // 2
        far = sorted(
            range(n_row),
            key=lambda m: (-abs((column * n_row + m) % n_col // 2 - home), m),
        )
        line = [0] * n_row
        for position, m in enumerate(far):
            line[m] = by_hops[position]
        offsets.append(line)
    return offsets


def shards(
    n_rows,
    n_cols,
    homolog_stack,
    per_amino_features,
    asking_matrix,
    lookup_matrix,
    content_matrix,
    sigmoid_scaling_matrix,
    attention_result_matrix,
    stack_transition_expand_matrix,
    stack_transition_shrink_matrix,
    former_factor_matrix,
    latter_factor_matrix,
    factor_mean_projection,
    row_amino_embedding,
    column_amino_embedding,
    offset_embedding_matrix,
    grid_transition_expand,
    grid_transition_shrink,
    distance_bins_matrix,
):
    devices = n_rows * n_cols
    n_seq, amino, feature = homolog_stack.shape
    n_res = amino // devices
    seqs = n_seq * devices
    axes = ("row", "col")

    sent = chunks(homolog_stack, n_res).reshape(devices, n_seq * n_res, feature)
    moved = lax.all_to_all(sent, axes, split_axis=0, concat_axis=0, tiled=True)
    moved = moved.reshape(seqs * n_res, feature)

    unit = jnp.eye(n_res, dtype=BF16)
    grouped = latter_factor_matrix.reshape(feature, -1, GROUP)
    latter = jnp.einsum("pr,fge->pfgre", unit, grouped).reshape(n_res * feature, -1)
    factors = jnp.concatenate([jnp.kron(unit, former_factor_matrix), latter], axis=1)
    amino_rows = jnp.concatenate(
        [per_amino_features, per_amino_features, jnp.zeros((16 - 2 * n_res, feature), BF16)], axis=0
    )
    projection = turn_projection(factor_mean_projection)
    table = plane_offsets(n_rows, n_cols)
    inverse = []
    for line in table:
        back = [0] * n_rows
        for m, offset in enumerate(line):
            back[offset] = m
        inverse.extend(back)
    relative, swap = relative_rows(inverse, offset_embedding_matrix, n_cols, n_rows, n_res)

    aligned, piece = attention(
        moved,
        amino_rows,
        (
            asking_matrix,
            lookup_matrix,
            content_matrix,
            sigmoid_scaling_matrix,
            attention_result_matrix,
            factors,
            row_amino_embedding,
            column_amino_embedding,
            stack_transition_expand_matrix,
            stack_transition_shrink_matrix,
        ),
        (projection, relative),
        n_res,
    )
    alignment_output = aligned.reshape(n_res, seqs, feature).transpose(1, 0, 2)

    turn = []
    for p in range(devices):
        column, m = p // n_rows, p % n_rows
        turn.append((p, ((p // n_cols) ^ table[column][m]) * n_cols + column))
    turned = lax.ppermute(piece, axes, turn)

    def along_col(value, m):
        return lax.ppermute(value, "col", [(c, c ^ m) for c in range(n_cols)])

    def along_row(value, m):
        return lax.ppermute(value, "row", [(r, r ^ m) for r in range(n_rows)])


    own = [piece] + [along_col(piece, 2 * m) for m in range(1, n_cols // 2)]
    other = [along_col(value, 1) for value in own[1:]]
    other = [along_col(piece, 1)] + other
    col_pieces = [turned] + [along_row(turned, m) for m in range(1, n_rows)]

    pair_output, distogram = pair_grid(
        inverse,
        own + other,
        col_pieces,
        (
            relative,
            swap,
            distance_bins_matrix.T,
            projection,
            grid_transition_expand,
            grid_transition_shrink,
        ),
        n_res,
        seqs,
    )
    return (alignment_output, pair_output, distogram)


def solution(mesh):
    n_rows, n_cols = mesh.shape["row"], mesh.shape["col"]
    assert n_cols == 2 * n_rows and n_rows & (n_rows - 1) == 0
    placed = (P(("row", "col"), None, None), P(("row", "col"), None)) + (P(),) * 16
    return jax.shard_map(
        functools.partial(shards, n_rows, n_cols),
        mesh=mesh,
        in_specs=placed,
        out_specs=(P(None, ("row", "col"), None), P("row", "col", None), P("row", "col", None)),
        check_vma=False,
    )
```

```python
import functools
import math

import jax
import jax.numpy as jnp
from jax import lax
from jax.experimental import pallas as pl
from jax.experimental.pallas import tpu as pltpu
from jax.sharding import PartitionSpec as P

HEAD = 32
CLIP = 32
LANES = 128
GROUP = 4
PAIR = 2
SWAP_LIMIT = 512
F32 = jnp.float32
BF16 = jnp.bfloat16


VMEM = pl.BlockSpec(memory_space=pltpu.VMEM)
HBM = pl.BlockSpec(memory_space=pltpu.MemorySpace.HBM)


def near(value):
    return pltpu.with_memory_space_constraint(value, pltpu.MemorySpace.VMEM)


def far(value):
    return pltpu.with_memory_space_constraint(value, pltpu.MemorySpace.HBM)


def local_call(kernel, *, scratch_shapes, **options):
    held = 0
    for ref in jax.tree.leaves(scratch_shapes):
        if ref.memory_space != pltpu.MemorySpace.VMEM:
            continue
        held += math.prod(ref.shape) * jnp.dtype(ref.dtype).itemsize
    limit = min(2 * held + (8 << 20), 48 << 20)
    return pl.pallas_call(
        kernel,
        scratch_shapes=scratch_shapes,
        compiler_params=pltpu.CompilerParams(vmem_limit_bytes=limit),
        **options,
    )


def dot(a, b):
    return jnp.dot(a, b, preferred_element_type=F32)


def standardize(values):
    middle = jnp.mean(values, -1, keepdims=True)
    centred = values - middle
    spread = jnp.mean(centred * centred, -1, keepdims=True)
    return centred * lax.rsqrt(spread + 1e-05)


def for_chunks(count, body):
    if count == 1:
        body(0)
    else:
        lax.fori_loop(0, count, lambda i, carry: (body(i), carry)[1], 0)


def rows_at(start, size):
    if not isinstance(start, int):
        start = pl.multiple_of(start, math.gcd(size, 128))
    return pl.ds(start, size)


def chunk_kernel(n_res, parts, x_far, o_far, x_in, o_out, came, left):
    n_seq, amino, feature = x_far.shape
    width = amino // parts
    rows = n_seq * width
    pair = 2 * n_res
    ins, outs = [], []
    for p in range(parts):
        ins.append(
            pltpu.make_async_copy(x_far.at[:, pl.ds(p * width, width), :], x_in.at[p], came.at[p])
        )
        ins[p].start()
    for p in range(parts):
        ins[p].wait()
        values = [
            x_in[p, seq].astype(F32).reshape(width // pair, pair, feature) for seq in range(n_seq)
        ]
        upper = lax.broadcasted_iota(jnp.int32, values[0].shape, 1) < n_res
        even, odd = [], []
        for seq in range(0, n_seq, 2):
            one, two = values[seq], values[seq + 1]
            even.append(jnp.where(upper, one, pltpu.roll(two, n_res, 1)))
            odd.append(jnp.where(upper, pltpu.roll(one, n_res, 1), two))
        made = jnp.stack(even + odd, axis=1).reshape(rows, feature)
        o_out[p * rows : (p + 1) * rows, :] = made.astype(BF16)
        part = pl.ds(p * rows, rows)
        outs.append(pltpu.make_async_copy(o_out.at[part], o_far.at[part], left.at[p]))
        outs[p].start()
    for copy in outs:
        copy.wait()


def chunks(x, n_res):
    n_seq, amino, feature = x.shape
    parts = 4
    width = amino // parts
    assert n_seq % 2 == 0 and 2 * n_res == 8
    return local_call(
        functools.partial(chunk_kernel, n_res, parts),
        out_shape=pltpu.HBM((n_seq * amino, feature), BF16),
        in_specs=[HBM],
        out_specs=HBM,
        scratch_shapes=[
            pltpu.VMEM((parts, n_seq, width, feature), BF16),
            pltpu.VMEM((n_seq * amino, feature), BF16),
            pltpu.SemaphoreType.DMA((parts,)),
            pltpu.SemaphoreType.DMA((parts,)),
        ],
        name="chunks",
    )(far(x))


def turn_kernel(w_ref, o_ref, w_scr):
    factor = math.isqrt(w_ref.shape[0])
    w_scr[...] = w_ref[...].astype(F32)
    for e in range(factor):
        o_ref[e * factor : (e + 1) * factor, :] = w_scr[pl.ds(e, factor, stride=factor), :].astype(
            BF16
        )


def turn_projection(w):
    return local_call(
        turn_kernel,
        out_shape=pltpu.HBM(w.shape, BF16),
        in_specs=[VMEM],
        out_specs=VMEM,
        scratch_shapes=[pltpu.VMEM(w.shape, F32)],
        name="turn",
    )(w)


def attention_kernel(
    n_res,
    x_ref,
    amino_ref,
    wq_ref,
    wk_ref,
    wv_ref,
    wg_ref,
    wo_ref,
    fg_ref,
    re_ref,
    ce_ref,
    w1_ref,
    w2_ref,
    _,
    _2,
    align_ref,
    send_ref,
    nat_scr,
    res_scr,
    q_scr,
    k_scr,
    v_scr,
    g_scr,
    mix_scr,
    ln_scr,
):
    rows, feature = x_ref.shape
    seqs = rows // n_res
    chunk = min(rows, 512)
    tiles = feature // LANES
    tile_lanes = [slice(t * LANES, (t + 1) * LANES) for t in range(tiles)]
    for t, lanes in enumerate(tile_lanes):
        nat_scr[t] = x_ref[:, lanes].astype(F32)
        for i in range(n_res):
            res_scr[i * seqs : (i + 1) * seqs, lanes] = nat_scr[t, pl.ds(i, seqs, stride=n_res), :]

    def project(step):
        at = rows_at(step * chunk, chunk)
        normed = standardize(res_scr[at, :]).astype(BF16)
        q_scr[at, :] = dot(normed, wq_ref[...]).astype(BF16)
        k_scr[at, :] = dot(normed, wk_ref[...]).astype(BF16)
        v_scr[at, :] = dot(normed, wv_ref[...]).astype(BF16)
        g_scr[at, :] = jax.nn.sigmoid(dot(normed, wg_ref[...]))

    for_chunks(rows // chunk, project)

    group = LANES // HEAD
    head_of_row = lax.broadcasted_iota(jnp.int32, (LANES, seqs), 0) // HEAD
    head_of_lane = lax.broadcasted_iota(jnp.int32, (seqs, LANES), 1) // HEAD
    scale = math.log2(math.e) / math.sqrt(HEAD)

    def attend(index, tile):
        at = rows_at(index * seqs, seqs)
        lanes = tile_lanes[tile]
        q_t = q_scr[at, lanes].astype(F32).T.astype(BF16)
        v_t = v_scr[at, lanes].astype(F32).T
        keys = k_scr[at, lanes].astype(F32)
        stacked = jnp.concatenate(
            [jnp.where(head_of_lane == h, keys, 0.0).astype(BF16) for h in range(group)], axis=0
        )
        scores = dot(stacked, q_t)
        powers, inverse = [], []
        for h in range(group):
            mine = scores[h * seqs : (h + 1) * seqs, :]
            power = jnp.exp2((mine - jnp.max(mine, axis=0, keepdims=True)) * scale)
            total = 1.0 / jnp.sum(power, axis=0, keepdims=True)
            powers.append(power.astype(BF16))
            inverse.append(jnp.broadcast_to(total, (HEAD, seqs)))
        values = jnp.concatenate(
            [jnp.where(head_of_row == h, v_t, 0.0).astype(BF16) for h in range(group)], axis=1
        )
        summed = dot(values, jnp.concatenate(powers, axis=0)) * jnp.concatenate(inverse, axis=0)
        mix_scr[at, lanes] = (summed.T * g_scr[at, lanes]).astype(BF16)

    block = 2 * seqs if seqs <= LANES else chunk

    def transition(step):
        at = rows_at(step * block, block)
        first = res_scr[at, :] + dot(mix_scr[at, :], wo_ref[...])
        hidden = jnp.maximum(dot(standardize(first).astype(BF16), w1_ref[...]), 0.0).astype(BF16)
        second = first + dot(hidden, w2_ref[...])
        align_ref[at, :] = second.astype(BF16)
        ln_scr[at, :] = standardize(second).astype(BF16)

    if seqs <= LANES:
        for i in range(n_res):
            for tile in range(tiles):
                attend(i, tile)
        for step in range(n_res // 2):
            transition(step)
    else:
        def attend_all(i):
            for tile in range(tiles):
                attend(i, tile)

        for_chunks(n_res, attend_all)
        for_chunks(rows // block, transition)

    side = jnp.concatenate([ln_scr[i * seqs : (i + 1) * seqs, :] for i in range(n_res)], axis=1)
    factors = dot(side, fg_ref[...])
    send_ref[0:seqs, :] = factors[:, :LANES].astype(BF16)
    for t in range(seqs // LANES):
        turned = factors[t * LANES : (t + 1) * LANES, LANES:].T.astype(BF16)
        if seqs & (seqs - 1) == 0:
            turned = (turned.astype(F32) * (1.0 / seqs)).astype(BF16)
        send_ref[seqs + t * LANES : seqs + (t + 1) * LANES, :] = turned
    by_row = lax.broadcasted_iota(jnp.int32, (2 * n_res, LANES), 0)
    pairs = jnp.where(
        by_row < n_res, dot(amino_ref[...], re_ref[...]), dot(amino_ref[...], ce_ref[...])
    )
    send_ref[2 * seqs :, :] = pairs.astype(BF16)


def attention(x, amino, weights, ready, n_res):
    rows, feature = x.shape
    seqs = rows // n_res
    return local_call(
        functools.partial(attention_kernel, n_res),
        out_shape=(
            pltpu.VMEM((rows, feature), BF16),
            pltpu.VMEM((2 * (seqs + n_res), LANES), BF16),
        ),
        in_specs=[VMEM] * (2 + len(weights)) + [HBM] * len(ready),
        out_specs=(VMEM, VMEM),
        scratch_shapes=[
            pltpu.VMEM((feature // LANES, rows, LANES), F32),
            pltpu.VMEM((rows, feature), F32),
            pltpu.VMEM((rows, feature), BF16),
            pltpu.VMEM((rows, feature), BF16),
            pltpu.VMEM((rows, feature), BF16),
            pltpu.VMEM((rows, feature), F32),
            pltpu.VMEM((rows, feature), BF16),
            pltpu.VMEM((rows, feature), BF16),
        ],
        name="attention",
    )(near(x), near(amino), *[near(w) for w in weights], *[far(w) for w in ready])


def placement(n_row, n_col, places):
    my_row = lax.axis_index("row")
    my_col = lax.axis_index("col")
    half = n_row // 2
    row_place = [my_col ^ (2 * (slot % half) + slot // half) for slot in range(n_row)]
    line = []
    for offset in range(n_col):
        entry = jnp.int32(places[offset])
        for column in range(1, n_row):
            entry = jnp.where(my_col == column, places[column * n_col + offset], entry)
        line.append(entry)
    source_row = my_col // (n_row // n_col)
    col_place = []
    for slot in range(n_col):
        key = my_row ^ slot ^ source_row
        where = line[0]
        for offset in range(1, n_col):
            where = jnp.where(key == offset, line[offset], where)
        col_place.append(where)
    return my_row, my_col, row_place, col_place


def relative_kernel(n_row, n_col, n_res, places, off_ref, o_ref, swap_ref, off_scr):
    my_row, my_col, row_place, col_place = placement(n_row, n_col, places)
    count_i, count_j = n_row * n_res, n_col * n_res
    row_start = my_row * count_i
    col_start = my_col * count_j
    bins = lax.broadcasted_iota(jnp.int32, (count_j, LANES), 1)
    j_here = col_start + lax.broadcasted_iota(jnp.int32, (count_j, LANES), 0)
    bins_m = lax.broadcasted_iota(jnp.int32, (count_i, LANES), 1)
    i_slot = lax.broadcasted_iota(jnp.int32, (count_i, LANES), 0)
    i_here = i_slot % n_res + row_start
    for slot in range(n_row):
        i_here = jnp.where(i_slot // n_res == slot, i_here + row_place[slot] * n_res, i_here)

    def relative(offset, lanes):
        index = jnp.clip(offset, -CLIP, CLIP) + CLIP
        return jnp.where(index == lanes, 1.0, 0.0).astype(BF16)

    marks = []
    for slot in range(n_row):
        for r in range(n_res):
            i = row_start + row_place[slot] * n_res + r
            marks.append(relative(j_here - i, bins))
    for slot in range(n_col):
        for r in range(n_res):
            j = col_start + col_place[slot] * n_res + r
            marks.append(relative(i_here - j, bins_m))
    off_scr[...] = jnp.zeros_like(off_scr)
    off_scr[0 : off_ref.shape[0], :] = off_ref[...].astype(F32)
    o_ref[...] = dot(jnp.concatenate(marks, axis=0), off_scr[...].astype(BF16)).astype(BF16)

    width = swap_ref.shape[1]
    chunk = min(swap_ref.shape[0], 128)
    source = lax.broadcasted_iota(jnp.int32, (chunk, width), 1)
    slot_of = source // (n_res * count_i)
    place = jnp.zeros_like(source)
    for slot in range(n_col):
        place = jnp.where(slot_of == slot, col_place[slot], place)
    goal = (source % count_i) * count_j + place * n_res + source // count_i % n_res
    line = lax.broadcasted_iota(jnp.int32, (chunk, width), 0)
    for start in range(0, swap_ref.shape[0], chunk):
        swap_ref[start : start + chunk, :] = jnp.where(goal == line + start, 1.0, 0.0).astype(BF16)


def relative_rows(places, table, n_row, n_col, n_res):
    cells = n_row * n_col * n_res * n_res
    swapped = cells if cells <= SWAP_LIMIT else LANES
    return local_call(
        functools.partial(relative_kernel, n_row, n_col, n_res, places),
        out_shape=(pltpu.HBM((2 * cells, LANES), BF16), pltpu.HBM((swapped, swapped), BF16)),
        in_specs=[VMEM],
        out_specs=(VMEM, VMEM),
        scratch_shapes=[pltpu.VMEM((LANES, LANES), F32)],
        name="relative",
    )(near(table))


def pair_kernel(n_row, n_col, n_res, seqs, places, *refs):
    row_refs = refs[0:n_row]
    col_refs = refs[n_row : n_row + n_col]
    refs = refs[n_row + n_col :]
    rel_ref, swap_ref, bins_ref, wp_ref, w1_ref, w2_ref, pair_far, dist_far = refs[:8]
    (a_r, a_c, lhs, grid, logit_scr) = refs[8:13]
    bd_ref, pair_ref, dist_ref, left_sem = refs[13:]
    factor = LANES // n_res
    count_i = n_row * n_res
    count_j = n_col * n_res
    _, _, row_place, col_place = placement(n_row, n_col, places)

    halves = n_res // PAIR

    def fill(e):
        block = wp_ref[e * factor : (e + 1) * factor, :]
        for r in range(PAIR):
            row = (e * PAIR + r) * factor
            for other in range(PAIR):
                bd_ref[row : row + factor, other * LANES : (other + 1) * LANES] = (
                    block if other == r else jnp.zeros_like(block)
                )

    def gather_rows(count, places):
        width = GROUP * count
        line = lax.broadcasted_iota(jnp.int32, (width, width), 0)
        column = lax.broadcasted_iota(jnp.int32, (width, width), 1)
        piece = column // (GROUP * n_res)
        place = piece
        if places is not None:
            for slot, where in enumerate(places):
                place = jnp.where(piece == slot, where, place)
        goal = column % GROUP * count + place * n_res + column // GROUP % n_res
        return jnp.where(line == goal, 1.0, 0.0).astype(BF16)

    def stack(pieces, g):
        lanes = []
        for t in range(seqs // LANES):
            first = seqs + t * LANES + g * GROUP * n_res
            lanes.append(
                jnp.concatenate([p[first : first + GROUP * n_res, :] for p in pieces], axis=0)
            )
        return jnp.concatenate(lanes, axis=1)

    gather_c = gather_rows(count_j, col_place)
    gather_r = gather_rows(count_i, None)
    groups = factor // GROUP
    for g in range(groups):
        for a_ref, gather, pieces, count in (
            (a_c, gather_c, col_refs, count_j),
            (a_r, gather_r, row_refs, count_i),
        ):
            made = dot(gather, stack(pieces, g)).astype(BF16)
            for k in range(GROUP):
                row = (g * GROUP + k) // PAIR * count
                lane = k % PAIR * seqs
                a_ref[row : row + count, lane : lane + seqs] = made[k * count : (k + 1) * count, :]
    todo = list(range(factor))

    exact = seqs & (seqs - 1) == 0
    width = LANES // PAIR
    lane_half = lax.broadcasted_iota(jnp.int32, (seqs, LANES), 1) // width

    def aside(value):
        value = value.astype(F32)
        rows = []
        for e in range(PAIR):
            tiles = []
            for half in range(halves):
                shifted = value if half == e else pltpu.roll(value, width, 1)
                tiles.append(jnp.where(lane_half == e, shifted, 0.0))
            rows.append(jnp.concatenate(tiles, axis=1))
        return jnp.concatenate(rows, axis=0).astype(BF16)

    def outer(a_ref, count, pieces, base):
        rows = factor // PAIR * count
        chunk = min(rows, 1024)
        per = chunk // count
        for s, piece in enumerate(pieces):
            left = aside(piece[0:seqs, :])

            def one(step):
                made = dot(a_ref[rows_at(step * chunk, chunk), :], left)
                if not exact:
                    made = made * (1.0 / seqs)
                made = made.astype(BF16)
                for e in range(per):
                    lane = (step * per + e) * LANES
                    if not isinstance(lane, int):
                        lane = pl.multiple_of(lane, LANES)
                    for half in range(halves):
                        row = base + (half * len(pieces) + s) * count
                        lhs[row : row + count, pl.ds(lane, LANES)] = made[
                            e * count : (e + 1) * count, half * LANES : (half + 1) * LANES
                        ]

            for_chunks(rows // chunk, one)
            for _ in range(min(share, len(todo))):
                fill(todo.pop())

    share = -(-factor // (n_row + n_col))
    direct = halves * n_row * count_j
    mirrored = halves * n_col * count_i
    outer(a_c, count_j, row_refs, 0)
    outer(a_r, count_i, col_refs, direct)
    while todo:
        fill(todo.pop())

    aux = 2 * n_res
    side_r = jnp.concatenate([r[2 * seqs :, :].astype(F32) for r in row_refs], axis=0)
    side_c = jnp.concatenate([r[2 * seqs :, :].astype(F32) for r in col_refs], axis=0)
    row_side = side_r.astype(BF16)
    col_side = side_c.astype(BF16)

    def pick(side, places, count):
        width = side.shape[0]
        line = lax.broadcasted_iota(jnp.int32, (count, width), 0)
        column = lax.broadcasted_iota(jnp.int32, (count, width), 1)
        goal = column % aux - n_res
        place = jnp.zeros_like(column)
        for slot, where in enumerate(places):
            place = jnp.where(column // aux == slot, where, place)
        hit = (goal >= 0) & (goal < n_res) & (line == place * n_res + goal)
        return dot(jnp.where(hit, 1.0, 0.0).astype(BF16), side)

    right_r = pick(row_side, list(range(n_row)), count_i)
    right_c = pick(col_side, col_place, count_j)
    total = direct + mirrored
    chunk = min(total, 256)

    def project(step):
        at = rows_at(step * chunk, chunk)
        made = dot(lhs[at, :], bd_ref[...])
        lhs_out[at, :] = made

    lhs_out = grid[1]
    start = grid[0]
    if total == 2 * chunk:
        project(0)
        project(1)
    else:
        for_chunks(total // chunk, project)
    place = 0
    for slot in range(n_row):
        for r in range(n_res):
            row = (r // PAIR * n_row + slot) * count_j
            lane = r % PAIR * LANES
            made = lhs_out[row : row + count_j, lane : lane + LANES]
            left = side_r[slot * aux + r : slot * aux + r + 1, :]
            start[place : place + count_j, :] = (
                (left + right_c) + rel_ref[place : place + count_j, :] + made
            )
            place += count_j
    for slot in range(n_col):
        for r in range(n_res):
            row = direct + (r // PAIR * n_col + slot) * count_i
            lane = r % PAIR * LANES
            made = lhs_out[row : row + count_i, lane : lane + LANES]
            left = side_c[slot * aux + r : slot * aux + r + 1, :]
            start[place : place + count_i, :] = (
                (left + right_r) + rel_ref[place : place + count_i, :] + made
            )
            place += count_i

    cells = count_i * count_j
    n_bins = dist_ref.shape[2]
    chunk2 = min(cells, 512)
    rounded_scr, all_logits = grid[2], grid[3]

    def transition(step):
        at = rows_at(step * chunk2, chunk2)
        begin = start[at, :]
        hidden = jnp.maximum(dot(standardize(begin).astype(BF16), w1_ref[...]), 0.0).astype(BF16)
        final = (begin + dot(hidden, w2_ref[...])).astype(BF16)
        rounded_scr[at, :] = final
        if swap_ref.shape[0] == cells:
            return
        all_logits[at, :] = lax.dot_general(
            final, bins_ref[...], (((1,), (1,)), ((), ())), preferred_element_type=F32
        )

    steps = cells // chunk2
    for_chunks(steps, transition)
    for slot in range(n_row):
        for r in range(n_res):
            at = (slot * n_res + r) * count_j
            goal = row_place[slot] * n_res + r
            pair_ref[goal] = rounded_scr[at : at + count_j, :]
    leave_pair = pltpu.make_async_copy(pair_ref, pair_far, left_sem.at[0])
    leave_pair.start()
    if steps == 1:
        transition(1)
    else:
        for_chunks(steps, lambda step: transition(step + steps))
    if swap_ref.shape[0] == cells:
        swapped = dot(swap_ref[...], rounded_scr[cells:, :]).astype(BF16)
        both = jnp.concatenate([rounded_scr[:cells, :], swapped], axis=1)
        twice = jnp.concatenate([bins_ref[...], bins_ref[...]], axis=1)
        made = lax.dot_general(
            both, twice, (((1,), (1,)), ((), ())), preferred_element_type=F32
        ).astype(BF16)
        leaves = [leave_pair]
        for slot in range(n_row):
            for r in range(n_res):
                at = (slot * n_res + r) * count_j
                dist_ref[row_place[slot] * n_res + r] = made[at : at + count_j, :]
        leave = pltpu.make_async_copy(dist_ref, dist_far, left_sem.at[1])
        leave.start()
        leave_pair.wait()
        leave.wait()
        return
    for slot in range(n_col):
        for r in range(n_res):
            source = cells + (slot * n_res + r) * count_i
            goal = (col_place[slot] * n_res + r) * count_i
            logit_scr[rows_at(goal, count_i), :n_bins] = all_logits[source : source + count_i, :]
    leaves = [leave_pair]
    for slot in range(n_row):
        for r in range(n_res):
            at = (slot * n_res + r) * count_j
            goal = row_place[slot] * n_res + r
            mirror = logit_scr[pl.ds(slot * n_res + r, count_j, stride=count_i), :]
            summed = all_logits[at : at + count_j, :] + mirror[:, :n_bins]
            dist_ref[goal] = summed.astype(BF16)
        rows = pl.ds(row_place[slot] * n_res, n_res)
        leave = pltpu.make_async_copy(dist_ref.at[rows], dist_far.at[rows], left_sem.at[1 + slot])
        leave.start()
        leaves.append(leave)
    for leave in leaves:
        leave.wait()


def pair_grid(places, row_pieces, col_pieces, weights, n_res, seqs):
    n_row, n_col = len(row_pieces), len(col_pieces)
    count_i, count_j = n_row * n_res, n_col * n_res
    factor = LANES // n_res
    total = (n_row * count_j + n_col * count_i) * n_res // PAIR
    cells = count_i * count_j
    n_bins = weights[2].shape[0]
    return local_call(
        functools.partial(pair_kernel, n_row, n_col, n_res, seqs, places),
        out_shape=(
            jax.ShapeDtypeStruct((count_i, count_j, LANES), BF16),
            jax.ShapeDtypeStruct((count_i, count_j, n_bins), BF16),
        ),
        in_specs=[VMEM] * (n_row + n_col + len(weights)),
        out_specs=(HBM, HBM),
        scratch_shapes=[
            pltpu.VMEM((factor // PAIR * count_i, PAIR * seqs), BF16),
            pltpu.VMEM((factor // PAIR * count_j, PAIR * seqs), BF16),
            pltpu.VMEM((total, factor // PAIR * LANES), BF16),
            (
                pltpu.VMEM((2 * cells, LANES), F32),
                pltpu.VMEM((total, PAIR * LANES), F32),
                pltpu.VMEM((2 * cells, LANES), BF16),
                pltpu.VMEM((2 * cells, n_bins), F32),
            ),
            pltpu.VMEM((cells, LANES), F32),
            pltpu.VMEM((factor // PAIR * LANES, PAIR * LANES), BF16),
            pltpu.VMEM((count_i, count_j, LANES), BF16),
            pltpu.VMEM((count_i, count_j, n_bins), BF16),
            pltpu.SemaphoreType.DMA((1 + n_row,)),
        ],
        name="pairs",
    )(*[near(v) for v in (*row_pieces, *col_pieces, *weights)])


def plane_offsets(n_row, n_col):
    offsets = []
    by_hops = sorted(range(n_row), key=lambda v: (bin(v).count("1"), v))
    for column in range(n_col):
        home = column // 2
        far = sorted(
            range(n_row),
            key=lambda m: (-abs((column * n_row + m) % n_col // 2 - home), m),
        )
        line = [0] * n_row
        for position, m in enumerate(far):
            line[m] = by_hops[position]
        offsets.append(line)
    return offsets


def shards(
    n_rows,
    n_cols,
    homolog_stack,
    per_amino_features,
    asking_matrix,
    lookup_matrix,
    content_matrix,
    sigmoid_scaling_matrix,
    attention_result_matrix,
    stack_transition_expand_matrix,
    stack_transition_shrink_matrix,
    former_factor_matrix,
    latter_factor_matrix,
    factor_mean_projection,
    row_amino_embedding,
    column_amino_embedding,
    offset_embedding_matrix,
    grid_transition_expand,
    grid_transition_shrink,
    distance_bins_matrix,
):
    devices = n_rows * n_cols
    n_seq, amino, feature = homolog_stack.shape
    n_res = amino // devices
    seqs = n_seq * devices
    axes = ("row", "col")

    sent = chunks(homolog_stack, n_res).reshape(devices, n_seq * n_res, feature)
    moved = lax.all_to_all(sent, axes, split_axis=0, concat_axis=0, tiled=True)
    moved = moved.reshape(seqs * n_res, feature)

    unit = jnp.eye(n_res, dtype=BF16)
    grouped = latter_factor_matrix.reshape(feature, -1, GROUP)
    latter = jnp.einsum("pr,fge->pfgre", unit, grouped).reshape(n_res * feature, -1)
    factors = jnp.concatenate([jnp.kron(unit, former_factor_matrix), latter], axis=1)
    amino_rows = jnp.concatenate([per_amino_features, per_amino_features], axis=0)
    projection = turn_projection(factor_mean_projection)
    table = plane_offsets(n_rows, n_cols)
    inverse = []
    for line in table:
        back = [0] * n_rows
        for m, offset in enumerate(line):
            back[offset] = m
        inverse.extend(back)
    relative, swap = relative_rows(inverse, offset_embedding_matrix, n_cols, n_rows, n_res)

    aligned, piece = attention(
        moved,
        amino_rows,
        (
            asking_matrix,
            lookup_matrix,
            content_matrix,
            sigmoid_scaling_matrix,
            attention_result_matrix,
            factors,
            row_amino_embedding,
            column_amino_embedding,
            stack_transition_expand_matrix,
            stack_transition_shrink_matrix,
        ),
        (projection, relative),
        n_res,
    )
    alignment_output = aligned.reshape(n_res, seqs, feature).transpose(1, 0, 2)

    turn = []
    for p in range(devices):
        column, m = p // n_rows, p % n_rows
        turn.append((p, ((p // n_cols) ^ table[column][m]) * n_cols + column))
    turned = lax.ppermute(piece, axes, turn)

    def along_col(value, m):
        return lax.ppermute(value, "col", [(c, c ^ m) for c in range(n_cols)])

    def along_row(value, m):
        return lax.ppermute(value, "row", [(r, r ^ m) for r in range(n_rows)])


    own = [piece] + [along_col(piece, 2 * m) for m in range(1, n_cols // 2)]
    other = [along_col(value, 1) for value in own[1:]]
    other = [along_col(piece, 1)] + other
    col_pieces = [turned] + [along_row(turned, m) for m in range(1, n_rows)]

    pair_output, distogram = pair_grid(
        inverse,
        own + other,
        col_pieces,
        (
            relative,
            swap,
            distance_bins_matrix.T,
            projection,
            grid_transition_expand,
            grid_transition_shrink,
        ),
        n_res,
        seqs,
    )
    return (alignment_output, pair_output, distogram)


def solution(mesh):
    n_rows, n_cols = mesh.shape["row"], mesh.shape["col"]
    assert n_cols == 2 * n_rows and n_rows & (n_rows - 1) == 0
    placed = (P(("row", "col"), None, None), P(("row", "col"), None)) + (P(),) * 16
    return jax.shard_map(
        functools.partial(shards, n_rows, n_cols),
        mesh=mesh,
        in_specs=placed,
        out_specs=(P(None, ("row", "col"), None), P("row", "col", None), P("row", "col", None)),
        check_vma=False,
    )
```

```python
import functools
import math

import jax
import jax.numpy as jnp
from jax import lax
from jax.experimental import pallas as pl
from jax.experimental.pallas import tpu as pltpu
from jax.sharding import PartitionSpec as P

HEAD = 32
CLIP = 32
LANES = 128
GROUP = 4
PAIR = 2
SWAP_LIMIT = 512
F32 = jnp.float32
BF16 = jnp.bfloat16


VMEM = pl.BlockSpec(memory_space=pltpu.VMEM)
HBM = pl.BlockSpec(memory_space=pltpu.MemorySpace.HBM)


def near(value):
    return pltpu.with_memory_space_constraint(value, pltpu.MemorySpace.VMEM)


def far(value):
    return pltpu.with_memory_space_constraint(value, pltpu.MemorySpace.HBM)


def local_call(kernel, *, scratch_shapes, **options):
    held = 0
    for ref in jax.tree.leaves(scratch_shapes):
        if ref.memory_space != pltpu.MemorySpace.VMEM:
            continue
        held += math.prod(ref.shape) * jnp.dtype(ref.dtype).itemsize
    limit = min(2 * held + (8 << 20), 48 << 20)
    return pl.pallas_call(
        kernel,
        scratch_shapes=scratch_shapes,
        compiler_params=pltpu.CompilerParams(vmem_limit_bytes=limit),
        **options,
    )


def dot(a, b):
    return jnp.dot(a, b, preferred_element_type=F32)


def standardize(values):
    middle = jnp.mean(values, -1, keepdims=True)
    centred = values - middle
    spread = jnp.mean(centred * centred, -1, keepdims=True)
    return centred * lax.rsqrt(spread + 1e-05)


def for_chunks(count, body):
    if count == 1:
        body(0)
    else:
        lax.fori_loop(0, count, lambda i, carry: (body(i), carry)[1], 0)


def rows_at(start, size):
    if not isinstance(start, int):
        start = pl.multiple_of(start, math.gcd(size, 128))
    return pl.ds(start, size)


def chunk_kernel(n_res, parts, x_far, o_far, x_in, o_out, came, left):
    n_seq, amino, feature = x_far.shape
    width = amino // parts
    rows = n_seq * width
    pair = 2 * n_res
    ins, outs = [], []
    for p in range(parts):
        ins.append(
            pltpu.make_async_copy(x_far.at[:, pl.ds(p * width, width), :], x_in.at[p], came.at[p])
        )
        ins[p].start()
    for p in range(parts):
        ins[p].wait()
        values = [
            x_in[p, seq].astype(F32).reshape(width // pair, pair, feature) for seq in range(n_seq)
        ]
        upper = lax.broadcasted_iota(jnp.int32, values[0].shape, 1) < n_res
        even, odd = [], []
        for seq in range(0, n_seq, 2):
            one, two = values[seq], values[seq + 1]
            even.append(jnp.where(upper, one, pltpu.roll(two, n_res, 1)))
            odd.append(jnp.where(upper, pltpu.roll(one, n_res, 1), two))
        made = jnp.stack(even + odd, axis=1).reshape(rows, feature)
        o_out[p * rows : (p + 1) * rows, :] = made.astype(BF16)
        part = pl.ds(p * rows, rows)
        outs.append(pltpu.make_async_copy(o_out.at[part], o_far.at[part], left.at[p]))
        outs[p].start()
    for copy in outs:
        copy.wait()


def chunks(x, n_res):
    n_seq, amino, feature = x.shape
    parts = 4
    width = amino // parts
    assert n_seq % 2 == 0 and 2 * n_res == 8
    return local_call(
        functools.partial(chunk_kernel, n_res, parts),
        out_shape=pltpu.HBM((n_seq * amino, feature), BF16),
        in_specs=[HBM],
        out_specs=HBM,
        scratch_shapes=[
            pltpu.VMEM((parts, n_seq, width, feature), BF16),
            pltpu.VMEM((n_seq * amino, feature), BF16),
            pltpu.SemaphoreType.DMA((parts,)),
            pltpu.SemaphoreType.DMA((parts,)),
        ],
        name="chunks",
    )(far(x))


def turn_kernel(w_ref, o_ref, w_scr):
    factor = math.isqrt(w_ref.shape[0])
    w_scr[...] = w_ref[...].astype(F32)
    for e in range(factor):
        o_ref[e * factor : (e + 1) * factor, :] = w_scr[pl.ds(e, factor, stride=factor), :].astype(
            BF16
        )


def turn_projection(w):
    return local_call(
        turn_kernel,
        out_shape=pltpu.HBM(w.shape, BF16),
        in_specs=[VMEM],
        out_specs=VMEM,
        scratch_shapes=[pltpu.VMEM(w.shape, F32)],
        name="turn",
    )(w)


def attention_kernel(
    n_res,
    x_ref,
    amino_ref,
    wq_ref,
    wk_ref,
    wv_ref,
    wg_ref,
    wo_ref,
    fg_ref,
    re_ref,
    ce_ref,
    w1_ref,
    w2_ref,
    _,
    _2,
    align_ref,
    send_ref,
    nat_scr,
    res_scr,
    q_scr,
    k_scr,
    v_scr,
    g_scr,
    mix_scr,
    ln_scr,
):
    rows, feature = x_ref.shape
    seqs = rows // n_res
    chunk = min(rows, 512)
    tiles = feature // LANES
    tile_lanes = [slice(t * LANES, (t + 1) * LANES) for t in range(tiles)]
    for t, lanes in enumerate(tile_lanes):
        nat_scr[t] = x_ref[:, lanes].astype(F32)
        for i in range(n_res):
            res_scr[i * seqs : (i + 1) * seqs, lanes] = nat_scr[t, pl.ds(i, seqs, stride=n_res), :]

    def project(step):
        at = rows_at(step * chunk, chunk)
        normed = standardize(res_scr[at, :]).astype(BF16)
        q_scr[at, :] = dot(normed, wq_ref[...]).astype(BF16)
        k_scr[at, :] = dot(normed, wk_ref[...]).astype(BF16)
        v_scr[at, :] = dot(normed, wv_ref[...]).astype(BF16)
        g_scr[at, :] = jax.nn.sigmoid(dot(normed, wg_ref[...]))

    for_chunks(rows // chunk, project)

    group = LANES // HEAD
    head_of_row = lax.broadcasted_iota(jnp.int32, (LANES, seqs), 0) // HEAD
    head_of_lane = lax.broadcasted_iota(jnp.int32, (seqs, LANES), 1) // HEAD
    scale = math.log2(math.e) / math.sqrt(HEAD)

    def attend(index, tile):
        at = rows_at(index * seqs, seqs)
        lanes = tile_lanes[tile]
        q_t = q_scr[at, lanes].astype(F32).T.astype(BF16)
        v_t = v_scr[at, lanes].astype(F32).T
        keys = k_scr[at, lanes].astype(F32)
        stacked = jnp.concatenate(
            [jnp.where(head_of_lane == h, keys, 0.0).astype(BF16) for h in range(group)], axis=0
        )
        scores = dot(stacked, q_t)
        powers, inverse = [], []
        for h in range(group):
            mine = scores[h * seqs : (h + 1) * seqs, :]
            power = jnp.exp2((mine - jnp.max(mine, axis=0, keepdims=True)) * scale)
            total = 1.0 / jnp.sum(power, axis=0, keepdims=True)
            powers.append(power.astype(BF16))
            inverse.append(jnp.broadcast_to(total, (HEAD, seqs)))
        values = jnp.concatenate(
            [jnp.where(head_of_row == h, v_t, 0.0).astype(BF16) for h in range(group)], axis=1
        )
        summed = dot(values, jnp.concatenate(powers, axis=0)) * jnp.concatenate(inverse, axis=0)
        mix_scr[at, lanes] = (summed.T * g_scr[at, lanes]).astype(BF16)

    block = 2 * seqs if seqs <= LANES else chunk

    def transition(step):
        at = rows_at(step * block, block)
        first = res_scr[at, :] + dot(mix_scr[at, :], wo_ref[...])
        hidden = jnp.maximum(dot(standardize(first).astype(BF16), w1_ref[...]), 0.0).astype(BF16)
        second = first + dot(hidden, w2_ref[...])
        align_ref[at, :] = second.astype(BF16)
        ln_scr[at, :] = standardize(second).astype(BF16)

    if seqs <= LANES:
        for i in range(n_res):
            for tile in range(tiles):
                attend(i, tile)
        for step in range(n_res // 2):
            transition(step)
    else:
        def attend_all(i):
            for tile in range(tiles):
                attend(i, tile)

        for_chunks(n_res, attend_all)
        for_chunks(rows // block, transition)

    side = jnp.concatenate([ln_scr[i * seqs : (i + 1) * seqs, :] for i in range(n_res)], axis=1)
    factors = dot(side, fg_ref[...])
    send_ref[0:seqs, :] = factors[:, :LANES].astype(BF16)
    for t in range(seqs // LANES):
        turned = factors[t * LANES : (t + 1) * LANES, LANES:].T.astype(BF16)
        if seqs & (seqs - 1) == 0:
            turned = (turned.astype(F32) * (1.0 / seqs)).astype(BF16)
        send_ref[seqs + t * LANES : seqs + (t + 1) * LANES, :] = turned
    by_row = lax.broadcasted_iota(jnp.int32, (2 * n_res, LANES), 0)
    pairs = jnp.where(
        by_row < n_res, dot(amino_ref[...], re_ref[...]), dot(amino_ref[...], ce_ref[...])
    )
    send_ref[2 * seqs :, :] = pairs.astype(BF16)


def attention(x, amino, weights, ready, n_res):
    rows, feature = x.shape
    seqs = rows // n_res
    return local_call(
        functools.partial(attention_kernel, n_res),
        out_shape=(
            pltpu.VMEM((rows, feature), BF16),
            pltpu.VMEM((2 * (seqs + n_res), LANES), BF16),
        ),
        in_specs=[VMEM] * (2 + len(weights)) + [HBM] * len(ready),
        out_specs=(VMEM, VMEM),
        scratch_shapes=[
            pltpu.VMEM((feature // LANES, rows, LANES), F32),
            pltpu.VMEM((rows, feature), F32),
            pltpu.VMEM((rows, feature), BF16),
            pltpu.VMEM((rows, feature), BF16),
            pltpu.VMEM((rows, feature), BF16),
            pltpu.VMEM((rows, feature), F32),
            pltpu.VMEM((rows, feature), BF16),
            pltpu.VMEM((rows, feature), BF16),
        ],
        name="attention",
    )(near(x), near(amino), *[near(w) for w in weights], *[far(w) for w in ready])


def placement(n_row, n_col, places):
    my_row = lax.axis_index("row")
    my_col = lax.axis_index("col")
    half = n_row // 2
    row_place = [my_col ^ (2 * (slot % half) + slot // half) for slot in range(n_row)]
    line = []
    for offset in range(n_col):
        entry = jnp.int32(places[offset])
        for column in range(1, n_row):
            entry = jnp.where(my_col == column, places[column * n_col + offset], entry)
        line.append(entry)
    source_row = my_col // (n_row // n_col)
    col_place = []
    for slot in range(n_col):
        key = my_row ^ slot ^ source_row
        where = line[0]
        for offset in range(1, n_col):
            where = jnp.where(key == offset, line[offset], where)
        col_place.append(where)
    return my_row, my_col, row_place, col_place


def relative_kernel(n_row, n_col, n_res, places, off_ref, o_ref, swap_ref, off_scr):
    my_row, my_col, row_place, col_place = placement(n_row, n_col, places)
    count_i, count_j = n_row * n_res, n_col * n_res
    row_start = my_row * count_i
    col_start = my_col * count_j
    bins = lax.broadcasted_iota(jnp.int32, (count_j, LANES), 1)
    j_here = col_start + lax.broadcasted_iota(jnp.int32, (count_j, LANES), 0)
    bins_m = lax.broadcasted_iota(jnp.int32, (count_i, LANES), 1)
    i_slot = lax.broadcasted_iota(jnp.int32, (count_i, LANES), 0)
    i_here = i_slot % n_res + row_start
    for slot in range(n_row):
        i_here = jnp.where(i_slot // n_res == slot, i_here + row_place[slot] * n_res, i_here)

    def relative(offset, lanes):
        index = jnp.clip(offset, -CLIP, CLIP) + CLIP
        return jnp.where(index == lanes, 1.0, 0.0).astype(BF16)

    marks = []
    for slot in range(n_row):
        for r in range(n_res):
            i = row_start + row_place[slot] * n_res + r
            marks.append(relative(j_here - i, bins))
    for slot in range(n_col):
        for r in range(n_res):
            j = col_start + col_place[slot] * n_res + r
            marks.append(relative(i_here - j, bins_m))
    off_scr[...] = jnp.zeros_like(off_scr)
    off_scr[0 : off_ref.shape[0], :] = off_ref[...].astype(F32)
    o_ref[...] = dot(jnp.concatenate(marks, axis=0), off_scr[...].astype(BF16)).astype(BF16)

    width = swap_ref.shape[1]
    chunk = min(swap_ref.shape[0], 128)
    source = lax.broadcasted_iota(jnp.int32, (chunk, width), 1)
    slot_of = source // (n_res * count_i)
    place = jnp.zeros_like(source)
    for slot in range(n_col):
        place = jnp.where(slot_of == slot, col_place[slot], place)
    goal = (source % count_i) * count_j + place * n_res + source // count_i % n_res
    line = lax.broadcasted_iota(jnp.int32, (chunk, width), 0)
    for start in range(0, swap_ref.shape[0], chunk):
        swap_ref[start : start + chunk, :] = jnp.where(goal == line + start, 1.0, 0.0).astype(BF16)


def relative_rows(places, table, n_row, n_col, n_res):
    cells = n_row * n_col * n_res * n_res
    swapped = cells if cells <= SWAP_LIMIT else LANES
    return local_call(
        functools.partial(relative_kernel, n_row, n_col, n_res, places),
        out_shape=(pltpu.HBM((2 * cells, LANES), BF16), pltpu.HBM((swapped, swapped), BF16)),
        in_specs=[VMEM],
        out_specs=(VMEM, VMEM),
        scratch_shapes=[pltpu.VMEM((LANES, LANES), F32)],
        name="relative",
    )(near(table))


def pair_kernel(n_row, n_col, n_res, seqs, places, *refs):
    row_refs = refs[0:n_row]
    col_refs = refs[n_row : n_row + n_col]
    refs = refs[n_row + n_col :]
    rel_ref, swap_ref, bins_ref, wp_ref, w1_ref, w2_ref, pair_far, dist_far = refs[:8]
    (a_r, a_c, lhs, grid, logit_scr) = refs[8:13]
    bd_ref, pair_ref, dist_ref, left_sem = refs[13:]
    factor = LANES // n_res
    count_i = n_row * n_res
    count_j = n_col * n_res
    _, _, row_place, col_place = placement(n_row, n_col, places)

    halves = n_res // PAIR

    def fill(e):
        block = wp_ref[e * factor : (e + 1) * factor, :]
        for r in range(PAIR):
            row = (e * PAIR + r) * factor
            for other in range(PAIR):
                bd_ref[row : row + factor, other * LANES : (other + 1) * LANES] = (
                    block if other == r else jnp.zeros_like(block)
                )

    def gather_rows(count, places):
        width = GROUP * count
        line = lax.broadcasted_iota(jnp.int32, (width, width), 0)
        column = lax.broadcasted_iota(jnp.int32, (width, width), 1)
        piece = column // (GROUP * n_res)
        place = piece
        if places is not None:
            for slot, where in enumerate(places):
                place = jnp.where(piece == slot, where, place)
        goal = column % GROUP * count + place * n_res + column // GROUP % n_res
        return jnp.where(line == goal, 1.0, 0.0).astype(BF16)

    def stack(pieces, g):
        lanes = []
        for t in range(seqs // LANES):
            first = seqs + t * LANES + g * GROUP * n_res
            lanes.append(
                jnp.concatenate([p[first : first + GROUP * n_res, :] for p in pieces], axis=0)
            )
        return jnp.concatenate(lanes, axis=1)

    gather_c = gather_rows(count_j, col_place)
    gather_r = gather_rows(count_i, None)
    groups = factor // GROUP
    for g in range(groups):
        for a_ref, gather, pieces, count in (
            (a_c, gather_c, col_refs, count_j),
            (a_r, gather_r, row_refs, count_i),
        ):
            made = dot(gather, stack(pieces, g)).astype(BF16)
            for k in range(GROUP):
                row = (g * GROUP + k) // PAIR * count
                lane = k % PAIR * seqs
                a_ref[row : row + count, lane : lane + seqs] = made[k * count : (k + 1) * count, :]
    todo = list(range(factor))

    exact = seqs & (seqs - 1) == 0
    width = LANES // PAIR
    lane_half = lax.broadcasted_iota(jnp.int32, (seqs, LANES), 1) // width

    def aside(value):
        value = value.astype(F32)
        rows = []
        for e in range(PAIR):
            tiles = []
            for half in range(halves):
                shifted = value if half == e else pltpu.roll(value, width, 1)
                tiles.append(jnp.where(lane_half == e, shifted, 0.0))
            rows.append(jnp.concatenate(tiles, axis=1))
        return jnp.concatenate(rows, axis=0).astype(BF16)

    def outer(a_ref, count, pieces, base):
        rows = factor // PAIR * count
        chunk = min(rows, 1024)
        per = chunk // count
        for s, piece in enumerate(pieces):
            left = aside(piece[0:seqs, :])

            def one(step):
                made = dot(a_ref[rows_at(step * chunk, chunk), :], left)
                if not exact:
                    made = made * (1.0 / seqs)
                made = made.astype(BF16)
                for e in range(per):
                    lane = (step * per + e) * LANES
                    if not isinstance(lane, int):
                        lane = pl.multiple_of(lane, LANES)
                    for half in range(halves):
                        row = base + (half * len(pieces) + s) * count
                        lhs[row : row + count, pl.ds(lane, LANES)] = made[
                            e * count : (e + 1) * count, half * LANES : (half + 1) * LANES
                        ]

            for_chunks(rows // chunk, one)
            for _ in range(min(share, len(todo))):
                fill(todo.pop())

    share = -(-factor // (n_row + n_col))
    direct = halves * n_row * count_j
    mirrored = halves * n_col * count_i
    outer(a_c, count_j, row_refs, 0)
    outer(a_r, count_i, col_refs, direct)
    while todo:
        fill(todo.pop())

    aux = 2 * n_res
    side_r = jnp.concatenate([r[2 * seqs :, :].astype(F32) for r in row_refs], axis=0)
    side_c = jnp.concatenate([r[2 * seqs :, :].astype(F32) for r in col_refs], axis=0)
    row_side = side_r.astype(BF16)
    col_side = side_c.astype(BF16)

    def pick(side, places, count):
        width = side.shape[0]
        line = lax.broadcasted_iota(jnp.int32, (count, width), 0)
        column = lax.broadcasted_iota(jnp.int32, (count, width), 1)
        goal = column % aux - n_res
        place = jnp.zeros_like(column)
        for slot, where in enumerate(places):
            place = jnp.where(column // aux == slot, where, place)
        hit = (goal >= 0) & (goal < n_res) & (line == place * n_res + goal)
        return dot(jnp.where(hit, 1.0, 0.0).astype(BF16), side)

    right_r = pick(row_side, list(range(n_row)), count_i)
    right_c = pick(col_side, col_place, count_j)
    total = direct + mirrored
    chunk = min(total, 256)

    def project(step):
        at = rows_at(step * chunk, chunk)
        made = dot(lhs[at, :], bd_ref[...])
        lhs_out[at, :] = made

    lhs_out = grid[1]
    start = grid[0]
    if total == 2 * chunk:
        project(0)
        project(1)
    else:
        for_chunks(total // chunk, project)
    place = 0
    for slot in range(n_row):
        for r in range(n_res):
            row = (r // PAIR * n_row + slot) * count_j
            lane = r % PAIR * LANES
            made = lhs_out[row : row + count_j, lane : lane + LANES]
            left = side_r[slot * aux + r : slot * aux + r + 1, :]
            start[place : place + count_j, :] = (
                (left + right_c) + rel_ref[place : place + count_j, :] + made
            )
            place += count_j
    for slot in range(n_col):
        for r in range(n_res):
            row = direct + (r // PAIR * n_col + slot) * count_i
            lane = r % PAIR * LANES
            made = lhs_out[row : row + count_i, lane : lane + LANES]
            left = side_c[slot * aux + r : slot * aux + r + 1, :]
            start[place : place + count_i, :] = (
                (left + right_r) + rel_ref[place : place + count_i, :] + made
            )
            place += count_i

    cells = count_i * count_j
    n_bins = dist_ref.shape[2]
    chunk2 = min(cells, 512)
    rounded_scr, all_logits = grid[2], grid[3]

    def transition(step):
        at = rows_at(step * chunk2, chunk2)
        begin = start[at, :]
        hidden = jnp.maximum(dot(standardize(begin).astype(BF16), w1_ref[...]), 0.0).astype(BF16)
        final = (begin + dot(hidden, w2_ref[...])).astype(BF16)
        rounded_scr[at, :] = final
        if swap_ref.shape[0] == cells:
            return
        all_logits[at, :] = lax.dot_general(
            final, bins_ref[...], (((1,), (1,)), ((), ())), preferred_element_type=F32
        )

    steps = cells // chunk2
    for_chunks(steps, transition)
    for slot in range(n_row):
        for r in range(n_res):
            at = (slot * n_res + r) * count_j
            goal = row_place[slot] * n_res + r
            pair_ref[goal] = rounded_scr[at : at + count_j, :]
    leave_pair = pltpu.make_async_copy(pair_ref, pair_far, left_sem.at[0])
    leave_pair.start()
    if steps == 1:
        transition(1)
    else:
        for_chunks(steps, lambda step: transition(step + steps))
    if swap_ref.shape[0] == cells:
        swapped = dot(swap_ref[...], rounded_scr[cells:, :]).astype(BF16)
        both = jnp.concatenate([rounded_scr[:cells, :], swapped], axis=1)
        twice = jnp.concatenate([bins_ref[...], bins_ref[...]], axis=1)
        made = lax.dot_general(
            both, twice, (((1,), (1,)), ((), ())), preferred_element_type=F32
        ).astype(BF16)
        leaves = [leave_pair]
        for slot in range(n_row):
            for r in range(n_res):
                at = (slot * n_res + r) * count_j
                dist_ref[row_place[slot] * n_res + r] = made[at : at + count_j, :]
        leave = pltpu.make_async_copy(dist_ref, dist_far, left_sem.at[1])
        leave.start()
        leave_pair.wait()
        leave.wait()
        return
    for slot in range(n_col):
        for r in range(n_res):
            source = cells + (slot * n_res + r) * count_i
            goal = (col_place[slot] * n_res + r) * count_i
            logit_scr[rows_at(goal, count_i), :n_bins] = all_logits[source : source + count_i, :]
    leaves = [leave_pair]
    for slot in range(n_row):
        for r in range(n_res):
            at = (slot * n_res + r) * count_j
            goal = row_place[slot] * n_res + r
            mirror = logit_scr[pl.ds(slot * n_res + r, count_j, stride=count_i), :]
            summed = all_logits[at : at + count_j, :] + mirror[:, :n_bins]
            dist_ref[goal] = summed.astype(BF16)
        rows = pl.ds(row_place[slot] * n_res, n_res)
        leave = pltpu.make_async_copy(dist_ref.at[rows], dist_far.at[rows], left_sem.at[1 + slot])
        leave.start()
        leaves.append(leave)
    for leave in leaves:
        leave.wait()


def pair_grid(places, row_pieces, col_pieces, weights, n_res, seqs):
    n_row, n_col = len(row_pieces), len(col_pieces)
    count_i, count_j = n_row * n_res, n_col * n_res
    factor = LANES // n_res
    total = (n_row * count_j + n_col * count_i) * n_res // PAIR
    cells = count_i * count_j
    n_bins = weights[2].shape[0]
    return local_call(
        functools.partial(pair_kernel, n_row, n_col, n_res, seqs, places),
        out_shape=(
            jax.ShapeDtypeStruct((count_i, count_j, LANES), BF16),
            jax.ShapeDtypeStruct((count_i, count_j, n_bins), BF16),
        ),
        in_specs=[VMEM] * (n_row + n_col + len(weights)),
        out_specs=(HBM, HBM),
        scratch_shapes=[
            pltpu.VMEM((factor // PAIR * count_i, PAIR * seqs), BF16),
            pltpu.VMEM((factor // PAIR * count_j, PAIR * seqs), BF16),
            pltpu.VMEM((total, factor // PAIR * LANES), BF16),
            (
                pltpu.VMEM((2 * cells, LANES), F32),
                pltpu.VMEM((total, PAIR * LANES), F32),
                pltpu.VMEM((2 * cells, LANES), BF16),
                pltpu.VMEM((2 * cells, n_bins), F32),
            ),
            pltpu.VMEM((cells, LANES), F32),
            pltpu.VMEM((factor // PAIR * LANES, PAIR * LANES), BF16),
            pltpu.VMEM((count_i, count_j, LANES), BF16),
            pltpu.VMEM((count_i, count_j, n_bins), BF16),
            pltpu.SemaphoreType.DMA((1 + n_row,)),
        ],
        name="pairs",
    )(*[near(v) for v in (*row_pieces, *col_pieces, *weights)])


def plane_offsets(n_row, n_col):
    offsets = []
    by_hops = sorted(range(n_row), key=lambda v: (bin(v).count("1"), v))
    for column in range(n_col):
        home = column // 2
        far = sorted(
            range(n_row),
            key=lambda m: (-abs((column * n_row + m) % n_col // 2 - home), -m),
        )
        line = [0] * n_row
        for position, m in enumerate(far):
            line[m] = by_hops[position]
        offsets.append(line)
    return offsets


def shards(
    n_rows,
    n_cols,
    homolog_stack,
    per_amino_features,
    asking_matrix,
    lookup_matrix,
    content_matrix,
    sigmoid_scaling_matrix,
    attention_result_matrix,
    stack_transition_expand_matrix,
    stack_transition_shrink_matrix,
    former_factor_matrix,
    latter_factor_matrix,
    factor_mean_projection,
    row_amino_embedding,
    column_amino_embedding,
    offset_embedding_matrix,
    grid_transition_expand,
    grid_transition_shrink,
    distance_bins_matrix,
):
    devices = n_rows * n_cols
    n_seq, amino, feature = homolog_stack.shape
    n_res = amino // devices
    seqs = n_seq * devices
    axes = ("row", "col")

    sent = chunks(homolog_stack, n_res).reshape(devices, n_seq * n_res, feature)
    moved = lax.all_to_all(sent, axes, split_axis=0, concat_axis=0, tiled=True)
    moved = moved.reshape(seqs * n_res, feature)

    unit = jnp.eye(n_res, dtype=BF16)
    grouped = latter_factor_matrix.reshape(feature, -1, GROUP)
    latter = jnp.einsum("pr,fge->pfgre", unit, grouped).reshape(n_res * feature, -1)
    factors = jnp.concatenate([jnp.kron(unit, former_factor_matrix), latter], axis=1)
    amino_rows = jnp.concatenate([per_amino_features, per_amino_features], axis=0)
    projection = turn_projection(factor_mean_projection)
    table = plane_offsets(n_rows, n_cols)
    inverse = []
    for line in table:
        back = [0] * n_rows
        for m, offset in enumerate(line):
            back[offset] = m
        inverse.extend(back)
    relative, swap = relative_rows(inverse, offset_embedding_matrix, n_cols, n_rows, n_res)

    aligned, piece = attention(
        moved,
        amino_rows,
        (
            asking_matrix,
            lookup_matrix,
            content_matrix,
            sigmoid_scaling_matrix,
            attention_result_matrix,
            factors,
            row_amino_embedding,
            column_amino_embedding,
            stack_transition_expand_matrix,
            stack_transition_shrink_matrix,
        ),
        (projection, relative),
        n_res,
    )
    alignment_output = aligned.reshape(n_res, seqs, feature).transpose(1, 0, 2)

    turn = []
    for p in range(devices):
        column, m = p // n_rows, p % n_rows
        turn.append((p, ((p // n_cols) ^ table[column][m]) * n_cols + column))
    turned = lax.ppermute(piece, axes, turn)

    def along_col(value, m):
        return lax.ppermute(value, "col", [(c, c ^ m) for c in range(n_cols)])

    def along_row(value, m):
        return lax.ppermute(value, "row", [(r, r ^ m) for r in range(n_rows)])


    own = [piece]
    for m in range(1, n_cols // 2):
        own.append(along_col(piece, 2 * m))
    other = [along_col(value, 1) for value in own[1:]]
    other = [along_col(piece, 1)] + other
    col_pieces = [turned] + [along_row(turned, m) for m in range(1, n_rows)]

    pair_output, distogram = pair_grid(
        inverse,
        own + other,
        col_pieces,
        (
            relative,
            swap,
            distance_bins_matrix.T,
            projection,
            grid_transition_expand,
            grid_transition_shrink,
        ),
        n_res,
        seqs,
    )
    return (alignment_output, pair_output, distogram)


def solution(mesh):
    n_rows, n_cols = mesh.shape["row"], mesh.shape["col"]
    assert n_cols == 2 * n_rows and n_rows & (n_rows - 1) == 0
    placed = (P(("row", "col"), None, None), P(("row", "col"), None)) + (P(),) * 16
    return jax.shard_map(
        functools.partial(shards, n_rows, n_cols),
        mesh=mesh,
        in_specs=placed,
        out_specs=(P(None, ("row", "col"), None), P("row", "col", None), P("row", "col", None)),
        check_vma=False,
    )
```
